32 devices in a mesh: grp: 4 (over x, core), ep: 4 (over z), sq: 2 (over y).
Axes of the slice: x: 2, y: 2, z: 4, core: 2. Of those that a mesh axis runs over, the one named last changes fastest.
Arguments:
- queries: bfloat16 [8192, 2048], P(('grp', 'ep', 'sq')), may hold values from -32 to 32
- keys: bfloat16 [8192, 512], P(('grp', 'ep', 'sq')), may hold values from -32 to 32
- values: bfloat16 [8192, 512], P(('grp', 'ep', 'sq')), may hold values from -6 to 6
- norm_gain: float32 [2048], replicated, may hold values from 0.1 to 1.9
- expert_ids: int32 [8192, 2], P(('grp', 'ep', 'sq')), may hold values from 0 to 3, all different within a row; in each aligned block of 256 rows (0 to 255, 256 to 511, ...) at most 192 rows name the same one
- gate_values: float32 [8192, 2], P(('grp', 'ep', 'sq')), may hold values from 0.1 to 1
- hidden_grad: bfloat16 [8192, 1024], P(('grp', 'ep', 'sq')), may hold values from -0.59765625 to 0.59765625
- gate_weight: bfloat16 [4, 2048, 1024], P('ep', None, 'sq'), may hold values from -0.125 to 0.125
- up_weight: bfloat16 [4, 2048, 1024], P('ep', None, 'sq'), may hold values from -0.125 to 0.125
Outputs:
- gate_grad: float32 [4, 2048, 1024], P('ep', 'grp', 'sq')
The draws below stay inside these ranges and needn't reach their ends.
Inputs may be any that keep to these rules, and one draw needn't show every extreme that they name: `expert_ids`: each token names 2 different experts; within the 256 tokens of one device no expert is named more than 192 times.
All inputs are finite; a program needn't handle non-finite values.
Results may differ from the reference program's by a relative error of at most 0.0085.
Values may be sent and summed in bfloat16 or wider, within the bound.
A program may use at most 64 MiB of HBM per device.

```python
import math
import jax
import jax.numpy as jnp
import numpy as np
from jax import lax

D = 2048
HEADS = 16
HEAD_DIM = 128
KV_HEADS = 4
FF = 1024
TOP = 2
LENGTH = 512
TOK_DEV = 256
EXPERTS = 4
CAP = 192
REPLICAS = 4
REPLICA_TOKENS = 2048
TOKENS = 8192
N_EP = 4
N_SQ = 2


def draw_queries(key, part):
    drawn = jnp.clip(jax.random.normal(jax.random.fold_in(key, 11), (TOKENS, HEADS * HEAD_DIM), jnp.float32), -3.5, 3.5)
    return drawn.astype(jnp.bfloat16)


def draw_keys(key, part):
    drawn = jnp.clip(jax.random.normal(jax.random.fold_in(key, 12), (TOKENS, KV_HEADS * HEAD_DIM), jnp.float32), -3.5, 3.5)
    return drawn.astype(jnp.bfloat16)


def block_scale(key, shape, shards, least, high):
    factor_of = 1.0
    for position, blocks in shards:
        draws = jax.random.uniform(jax.random.fold_in(jax.random.fold_in(key, 6), position), (blocks,), jnp.float32, least / len(shards), high / len(shards))
        factor_of = factor_of * jnp.repeat(jnp.exp(draws), shape[position] // blocks).reshape((-1,) + (1,) * (len(shape) - 1 - position))
    return factor_of


def routed_block(key, own, number, rows, amount, top, bound, skew):
    order = jax.random.permutation(key, amount)
    packed, common = portions_of(amount, rows * top, bound, skew, True), portions_of(amount, rows * top, bound, skew, False)
    places = jnp.arange(amount)

    def named(lengths, rotation):
        used = int((lengths > 0).sum())
        fixed = max(1, used // 4)
        moved = fixed + (places - fixed + rotation * (used - fixed)) % max(1, amount - fixed)
        return jnp.zeros((amount,), jnp.int32).at[order[jnp.where(places < fixed, places, moved)]].set(jnp.asarray(lengths, jnp.int32))

    lengths = jnp.where(number % 4 == 0, named(packed, number // 4), named(common, number - number // 4 - 1))
    mixed = jax.random.permutation(jax.random.fold_in(own, 3), amount)
    donor, receiver = mixed[0:amount // 2 * 2:2], mixed[1:amount // 2 * 2:2]
    slack = jnp.minimum(lengths[donor] - 1, bound - lengths[receiver]) // 2
    slack = jnp.where((donor == order[0]) | (receiver == order[0]) | (lengths[receiver] == 0), 0, jnp.maximum(slack, 0))
    moved = jax.random.randint(jax.random.fold_in(own, 4), (amount // 2,), 0, 1 << 20) % (slack + 1)
    lengths = lengths.at[donor].add(-moved).at[receiver].add(moved)
    items = jnp.searchsorted(jnp.cumsum(lengths), jnp.arange(rows * top), side="right").astype(jnp.int32)
    table = items.reshape(top, rows).T
    table = table[jax.random.permutation(jax.random.fold_in(own, 1), rows)]
    rotation = jax.random.randint(jax.random.fold_in(own, 2), (rows, 1), 0, top)
    return jnp.take_along_axis(table, (jnp.arange(top)[None, :] + rotation) % top, axis=1)


def portions_of(number_of, total, most, skew, full):
    portions = [(1 << 20) // math.isqrt(standing ** skew) + 1 for standing in range(1, number_of + 1)]
    largest = most if full else min(most, max(-(-total // number_of), total * portions[0] // sum(portions)))
    least = 1 if total - largest >= number_of - 1 else 0
    holding, spare = [largest] + [least] * (number_of - 1), total - largest - least * (number_of - 1)
    while spare > 0:
        movable = [i for i in range(1, number_of) if holding[i] < largest] or [i for i in range(1, number_of) if holding[i] < most]
        pool, left = sum([portions[i] for i in movable]), spare
        for i in movable:
            extra = min(most - holding[i], max(1, left * portions[i] // pool), spare)
            holding[i] = holding[i] + extra
            spare = spare - extra
    return np.array(holding)


def centred(stream_key, dims, scale, reach, pieces=(), kind=jnp.bfloat16):
    array = scale * jax.random.normal(stream_key, dims, jnp.float32)
    if pieces:
        array = array * block_scale(stream_key, dims, pieces, -0.22, 0.18)
    return jnp.clip(array, -reach, reach).astype(kind)


def setup_inputs(seed: int = 0) -> dict:
    arg_keys = jax.random.split(jax.random.key(seed), 10)
    queries = draw_queries(jax.random.fold_in(arg_keys[9], 71), 0)
    keys = draw_keys(jax.random.fold_in(arg_keys[9], 71), 0)
    values = centred(arg_keys[2], (TOKENS, KV_HEADS * HEAD_DIM), 1.0, 6.0, ((0, 32),))
    norm_gain = jnp.clip(1.0 + 0.18 * jax.random.normal(arg_keys[3], (D,), jnp.float32), 0.1, 1.9)
    expert_ids_keys = jax.random.split(jax.random.fold_in(arg_keys[4], 1), TOKENS // TOK_DEV)
    expert_ids_turns = jax.random.permutation(jax.random.fold_in(arg_keys[4], 3), TOKENS // TOK_DEV)
    expert_ids = jax.vmap(lambda own, number: routed_block(jax.random.fold_in(arg_keys[4], 2), own, number, TOK_DEV, EXPERTS, TOP, CAP, 1))(expert_ids_keys, expert_ids_turns).reshape((TOKENS, TOP))
    gate_values = jnp.clip(jnp.exp(math.log(1.0) - 2.3025851 * jax.random.uniform(arg_keys[5], (TOKENS, TOP), jnp.float32) ** block_scale(arg_keys[5], (TOKENS, TOP), ((0, 32),), -0.2, 0.2)), 0.1, 1.0)
    hidden_grad = centred(arg_keys[6], (TOKENS, FF), 0.1, 0.59765625, ((0, 32),))
    gate_weight = centred(arg_keys[7], (EXPERTS, D, FF), D ** -0.5, 0.125, ((0, 4), (2, 2)))
    up_weight = centred(arg_keys[8], (EXPERTS, D, FF), D ** -0.5, 0.125, ((0, 4), (2, 2)))
    return {"queries": queries, "keys": keys, "values": values, "norm_gain": norm_gain, "expert_ids": expert_ids, "gate_values": gate_values, "hidden_grad": hidden_grad, "gate_weight": gate_weight, "up_weight": up_weight}


epsilon = 1e-05
masked_score = -1e+30

def attend_sequence(operands, norm_gain):
    query_rows, key_rows, value_rows = operands
    length_here = query_rows.shape[0]
    group_size = HEADS // KV_HEADS
    query_heads = query_rows.reshape(length_here, KV_HEADS, group_size, HEAD_DIM).astype(jnp.float32)
    key_heads = key_rows.reshape(length_here, KV_HEADS, HEAD_DIM).astype(jnp.float32)
    value_heads = value_rows.reshape(length_here, KV_HEADS, HEAD_DIM).astype(jnp.float32)
    scores = jnp.einsum('tkgd,rkd->tkgr', query_heads, key_heads) * (1.0 / math.sqrt(HEAD_DIM))
    positions = jnp.arange(length_here, dtype=jnp.int32)
    allowed = (positions[None, :] <= positions[:, None])[:, None, None, :]
    scores = jnp.where(allowed, scores, masked_score)
    row_max = lax.optimization_barrier(jnp.max(scores, axis=-1, keepdims=True))
    exponent_terms = jnp.where(allowed, jnp.exp(scores - row_max), 0.0)
    denominator = lax.optimization_barrier(jnp.sum(exponent_terms, axis=-1))
    rounded = lax.optimization_barrier(exponent_terms.astype(jnp.bfloat16)).astype(jnp.float32)
    attended = jnp.einsum('tkgr,rkd->tkgd', rounded, value_heads) / denominator[..., None]
    attended = attended.reshape(length_here, HEADS * HEAD_DIM)
    mean_square = lax.optimization_barrier(jnp.mean(attended * attended, axis=-1, keepdims=True))
    return (attended * lax.rsqrt(mean_square + epsilon) * norm_gain).astype(jnp.bfloat16)

def replica_gradient(operands, gate_weight, up_weight):
    normed_rows, id_rows, gate_rows, grad_rows = operands
    flat_ids = id_rows.reshape(-1)
    flat_gates = gate_rows.reshape(-1)
    most_rows = N_EP * N_SQ * CAP

    def one_expert(expert_operands):
        expert_index, weight_gate, weight_up = expert_operands
        hit = flat_ids == expert_index
        order = jnp.argsort(jnp.where(hit, 0, 1).astype(jnp.int32), stable=True)[:most_rows].astype(jnp.int32)
        valid = hit[order]
        token_index = order // TOP
        inputs = jnp.where(valid[:, None], normed_rows[token_index], jnp.zeros((), jnp.bfloat16))
        scaled = flat_gates[order][:, None] * grad_rows[token_index].astype(jnp.float32)
        cotangent = jnp.where(valid[:, None], scaled, 0.0).astype(jnp.bfloat16)
        pre_gate = jnp.dot(inputs, weight_gate, preferred_element_type=jnp.float32)
        pre_up = jnp.dot(inputs, weight_up, preferred_element_type=jnp.float32)
        sigmoid_gate = jax.nn.sigmoid(pre_gate)
        slope = sigmoid_gate * (1.0 + pre_gate * (1.0 - sigmoid_gate))
        delta_gate = (cotangent.astype(jnp.float32) * pre_up * slope).astype(jnp.bfloat16)
        return jnp.dot(inputs.T, delta_gate, preferred_element_type=jnp.float32)
    expert_range = jnp.arange(EXPERTS, dtype=jnp.int32)
    return lax.map(one_expert, (expert_range, gate_weight, up_weight))

def reference(queries, keys, values, norm_gain, expert_ids, gate_values, hidden_grad, gate_weight, up_weight):
    sequences = TOKENS // LENGTH

    def attend_one(operands):
        return attend_sequence(operands, norm_gain)
    normed = lax.map(attend_one, (queries.reshape(sequences, LENGTH, D), keys.reshape(sequences, LENGTH, KV_HEADS * HEAD_DIM), values.reshape(sequences, LENGTH, KV_HEADS * HEAD_DIM)))
    normed = normed.reshape(REPLICAS, REPLICA_TOKENS, D)
    id_blocks = expert_ids.reshape(REPLICAS, REPLICA_TOKENS, TOP)
    gate_blocks = gate_values.reshape(REPLICAS, REPLICA_TOKENS, TOP)
    grad_blocks = hidden_grad.reshape(REPLICAS, REPLICA_TOKENS, FF)

    def add_replica(accumulated, operands):
        replica_part = replica_gradient(operands, gate_weight, up_weight)
        rounded = lax.optimization_barrier(replica_part.astype(jnp.bfloat16))
        return (accumulated + rounded.astype(jnp.float32), None)
    initial = jnp.zeros((EXPERTS, D, FF), jnp.float32)
    result, unused = lax.scan(add_replica, initial, (normed, id_blocks, gate_blocks, grad_blocks))
    return result
```

```python
import functools
import math

import jax
import jax.numpy as jnp
from jax import lax
from jax.experimental import pallas as pl
from jax.experimental.pallas import tpu as pltpu
from jax.sharding import PartitionSpec as P

HEAD_DIM = 128

epsilon = 1e-05
masked_score = -1e30
MESH = pl.DeviceIdType.MESH


def attention_kernel(group_size, shard_ref, q_ref, ko_ref, vo_ref, kp_ref, vp_ref, gain_ref, out_ref, acc_ref):
    rows, model_width = q_ref.shape
    past = kp_ref.shape[0]
    scale = 1.0 / math.sqrt(HEAD_DIM)
    shard = shard_ref[0]
    contract = (((1,), (1,)), ((), ()))
    causal = lax.broadcasted_iota(jnp.int32, (rows, rows), 1) <= lax.broadcasted_iota(
        jnp.int32, (rows, rows), 0
    )
    seen = lax.broadcasted_iota(jnp.int32, (rows, past), 1) < shard * rows
    squares = jnp.zeros((rows, 1), jnp.float32)
    for head in range(model_width // HEAD_DIM):
        cols = slice(head * HEAD_DIM, (head + 1) * HEAD_DIM)
        kv = head // group_size
        kv_cols = slice(kv * HEAD_DIM, (kv + 1) * HEAD_DIM)
        q = q_ref[:, cols]
        own = lax.dot_general(q, ko_ref[:, kv_cols], contract, preferred_element_type=jnp.float32)
        old = lax.dot_general(q, kp_ref[:, kv_cols], contract, preferred_element_type=jnp.float32)
        own = jnp.where(causal, own * scale, masked_score)
        old = jnp.where(seen, old * scale, masked_score)
        top = jnp.maximum(
            jnp.max(own, axis=1, keepdims=True), jnp.max(old, axis=1, keepdims=True)
        )
        own = jnp.exp(own - top)
        old = jnp.exp(old - top)
        total = jnp.sum(own, axis=1, keepdims=True) + jnp.sum(old, axis=1, keepdims=True)
        out = jnp.dot(
            own.astype(jnp.bfloat16), vo_ref[:, kv_cols], preferred_element_type=jnp.float32
        ) + jnp.dot(
            old.astype(jnp.bfloat16), vp_ref[:, kv_cols], preferred_element_type=jnp.float32
        )
        out = out / total
        acc_ref[:, cols] = out
        squares = squares + jnp.sum(out * out, axis=1, keepdims=True)
    inverse = lax.rsqrt(squares / model_width + epsilon)
    out_ref[...] = (acc_ref[...] * inverse * gain_ref[...]).astype(jnp.bfloat16)


def attend(shard, queries, keys, values, past_keys, past_values, norm_gain):
    rows, model_width = queries.shape
    group_size = model_width // keys.shape[1]
    vmem = pl.BlockSpec(memory_space=pltpu.VMEM)
    return pl.pallas_call(
        functools.partial(attention_kernel, group_size),
        out_shape=jax.ShapeDtypeStruct((rows, model_width), jnp.bfloat16),
        in_specs=[pl.BlockSpec(memory_space=pltpu.SMEM)] + [vmem] * 6,
        out_specs=vmem,
        scratch_shapes=[pltpu.VMEM((rows, model_width), jnp.float32)],
        compiler_params=pltpu.CompilerParams(vmem_limit_bytes=32 << 20),
        cost_estimate=pl.CostEstimate(
            flops=4 * rows * model_width * (rows + past_keys.shape[0]),
            bytes_accessed=4 * rows * model_width,
            transcendentals=rows * (model_width // HEAD_DIM) * (rows + past_keys.shape[0]),
        ),
    )(shard.reshape(1), queries, keys, values, past_keys, past_values, norm_gain.reshape(1, -1))


def ring(size, shift):
    return [(i, (i + shift) % size) for i in range(size)]


def body(
    queries, keys, values, norm_gain, expert_ids, gate_values, hidden_grad, gate_weight, up_weight
):
    rows, model_width = queries.shape
    n_ep = lax.axis_size("ep")
    n_sq = lax.axis_size("sq")
    shard = lax.axis_index("sq")
    expert = lax.axis_index("ep")
    weight_gate = gate_weight[0]
    weight_up = up_weight[0]
    width = weight_gate.shape[1]
    kv_width = keys.shape[1]

    both = jnp.concatenate([keys, values], axis=1)
    past = []
    for j in range(1, n_sq):
        past.append(lax.ppermute(both, "sq", [(i, i + j) for i in range(n_sq - j)]))
    past = jnp.concatenate(past, axis=0)

    def columns_of(owner):
        return lax.dynamic_slice_in_dim(hidden_grad, owner * width, width, 1)

    grads = [columns_of(shard)]
    for j in range(1, n_sq):
        grads.append(lax.ppermute(columns_of((shard + j) % n_sq), "sq", ring(n_sq, j)))
    grad = jnp.concatenate(grads, axis=0)

    chosen = expert_ids[:, :, None] == jnp.arange(n_ep, dtype=jnp.int32)
    share = jnp.sum(jnp.where(chosen, gate_values[:, :, None], 0.0), axis=1).T
    shares = lax.all_gather(share, ("ep", "sq"), axis=0, tiled=False)
    shares = lax.dynamic_index_in_dim(shares, expert, 1, keepdims=False).reshape(n_ep, n_sq, rows)
    shares = jnp.concatenate(
        [
            lax.dynamic_index_in_dim(shares, (shard - j) % n_sq, 1, keepdims=False)
            for j in range(n_sq)
        ],
        axis=1,
    )

    normed = attend(
        shard, queries, keys, values, past[:, :kv_width], past[:, kv_width:], norm_gain
    )

    def add_chunk(step, tokens, grad, summed):
        source = (expert - step) % n_ep
        share_here = lax.dynamic_index_in_dim(shares, source, 0, keepdims=False)
        pieces = [tokens]
        for j in range(1, n_sq):
            pieces.append(lax.ppermute(tokens, "sq", ring(n_sq, j)))
        for j, inputs in enumerate(pieces):
            part = slice(j * rows, (j + 1) * rows)
            cotangent = (share_here[part, None] * grad[part].astype(jnp.float32)).astype(
                jnp.bfloat16
            )
            pre_gate = jnp.dot(inputs, weight_gate, preferred_element_type=jnp.float32)
            pre_up = jnp.dot(inputs, weight_up, preferred_element_type=jnp.float32)
            sigmoid_gate = jax.nn.sigmoid(pre_gate)
            slope = sigmoid_gate * (1.0 + pre_gate * (1.0 - sigmoid_gate))
            delta = (cotangent.astype(jnp.float32) * pre_up * slope).astype(jnp.bfloat16)
            term = lax.dot_general(
                inputs, delta, (((0,), (0,)), ((), ())), preferred_element_type=jnp.float32
            )
            summed = term if summed is None else summed + term
        return summed

    def turn(tokens, grad):
        return lax.ppermute(tokens, "ep", ring(n_ep, 1)), lax.ppermute(grad, "ep", ring(n_ep, 1))

    if n_ep <= 8:
        summed = None
        tokens = normed
        for step in range(n_ep):
            if step < n_ep - 1:
                turned = turn(tokens, grad)
            summed = add_chunk(step, tokens, grad, summed)
            if step < n_ep - 1:
                tokens, grad = turned
    else:

        def one_step(step, carried):
            tokens, grad, summed = carried
            turned = turn(tokens, grad)
            return (*turned, add_chunk(step, tokens, grad, summed))

        start = jnp.zeros((model_width, width), jnp.float32)
        summed = lax.fori_loop(0, n_ep, one_step, (normed, grad, start))[2]
    return lax.psum_scatter(
        summed[None].astype(jnp.bfloat16), "grp", scatter_dimension=1, tiled=True
    ).astype(jnp.float32)


def whole_kernel(
    q_hbm, k_hbm, v_hbm, gain_ref, share_ref, hidden_hbm, gate_hbm, up_hbm, out_ref,
    q_ref, k_ref, v_ref, x_full, x_comp, x_out, g_full, g_comp, g_out, c_buf, kv_buf,
    weight_gate, weight_up, delta_ref, attended, acc, stage, from_core, carry, from_chip,
    load_sem, y_send, y_recv, c_send, c_recv, g_send, g_recv, x_send, x_recv, yx_send, yx_recv,
    core_send, core_recv, chip_send, chip_recv,
):
    n_ep = x_full.shape[0]
    rows, model_width = q_ref.shape
    cap = x_comp.shape[3]
    parts = x_full.shape[1]
    half = model_width // parts
    width = weight_gate.shape[1]
    kv_heads = k_ref.shape[1] // HEAD_DIM
    group_size = model_width // k_ref.shape[1]
    block = model_width // 4
    scale = 1.0 / math.sqrt(HEAD_DIM)
    grp, expert, shard = lax.axis_index("grp"), lax.axis_index("ep"), lax.axis_index("sq")
    peer = 1 - shard
    last = n_ep - 1
    right, left = lax.rem(expert + 1, n_ep), lax.rem(expert + last, n_ep)
    inner = jnp.logical_and(expert > 0, expert < last)
    core = lax.rem(grp, 2)
    chip = grp // 2
    sibling = chip * 2 + 1 - core
    across = (1 - chip) * 2 + core
    diagonal = (1 - chip) * 2 + 1 - core
    peer_columns = pl.ds(pl.multiple_of(peer * width, width), width)
    own_columns = pl.ds(pl.multiple_of(shard * width, width), width)

    def load(i, src, dst):
        return pltpu.make_async_copy(src, dst, load_sem.at[i])

    loads = [
        load(0, q_hbm, q_ref),
        load(1, k_hbm, k_ref),
        load(2, v_hbm, v_ref),
        load(3, hidden_hbm.at[:, own_columns], g_full.at[expert, 0]),
        load(4, gate_hbm, weight_gate),
        load(5, up_hbm, weight_up),
    ]
    for copy in loads:
        copy.start()

    barrier = pltpu.get_barrier_semaphore()
    for target in ({"sq": peer}, {"ep": right}, {"ep": left}, {"grp": sibling}, {"grp": across}):
        pl.semaphore_signal(barrier, inc=1, device_id=target, device_id_type=MESH)
    pl.semaphore_wait(barrier, 5)

    def send(src, dst, send_sem, recv_sem, target):
        return pltpu.make_async_remote_copy(
            src_ref=src, dst_ref=dst, send_sem=send_sem, recv_sem=recv_sem,
            device_id=target, device_id_type=MESH,
        )

    def neighbour(d):
        return {"ep": right if d else left}

    def c_copy(z, j, d):
        return send(c_buf.at[z, j], c_buf.at[z, j], c_send.at[d, z, j], c_recv.at[z, j],
                    neighbour(d))

    def g_whole(z, j, d):
        return send(g_full.at[z, j], g_full.at[z, j], g_send.at[d, z, j], g_recv.at[z, j],
                    neighbour(d))

    def g_picked(z, j, d):
        return send(g_out.at[z, j], g_comp.at[z, j], g_send.at[d, z, j], g_recv.at[z, j],
                    neighbour(d))

    def x_whole(z, h, d):
        return send(x_full.at[z, h], x_full.at[z, h], x_send.at[d, z, h], x_recv.at[z, h],
                    neighbour(d))

    def x_picked(z, h, d):
        return send(x_out.at[z, h], x_comp.at[z, 0, h], x_send.at[d, z, h], x_recv.at[z, h],
                    neighbour(d))

    def yx(z, h):
        return send(x_comp.at[z, 0, h], x_comp.at[z, 1, h], yx_send.at[z, h], yx_recv.at[z, h],
                    {"sq": peer})

    def goes(d):
        return expert < last if d else expert > 0

    def to_inner(d):
        return expert < last - 1 if d else expert > 1

    def to_end(d):
        return expert == last - 1 if d else expert == 1

    def end_of(d):
        return last if d else 0

    y_keys = send(k_hbm, kv_buf.at[0], y_send.at[0], y_recv.at[0], {"sq": peer})
    y_values = send(v_hbm, kv_buf.at[1], y_send.at[1], y_recv.at[1], {"sq": peer})
    y_share = send(share_ref, c_buf.at[expert, 1], y_send.at[2], y_recv.at[2], {"sq": peer})
    y_grad = send(hidden_hbm.at[:, peer_columns], g_full.at[expert, 1],
                  y_send.at[3], y_recv.at[3], {"sq": peer})
    y_share.start()
    y_keys.start()
    y_values.start()
    y_grad.start()
    c_buf[expert, 0] = share_ref[...]
    acc[...] = jnp.zeros_like(acc)
    upper = (
        lax.broadcasted_iota(jnp.int32, (rows, rows), 0)
        <= lax.broadcasted_iota(jnp.int32, (rows, rows), 1)
    ).astype(jnp.float32).astype(jnp.bfloat16)
    places = lax.broadcasted_iota(jnp.int32, (cap, rows), 0).astype(jnp.float32)

    def pick(z, j, who):
        share = c_buf[z, j]
        here = lax.broadcasted_iota(jnp.int32, share.shape, 0) == who
        share = jnp.sum(jnp.where(here, share, 0.0), axis=0, keepdims=True)
        routed = jnp.where(share > 0.0, 1.0, 0.0)
        count = jnp.dot(
            jnp.broadcast_to(routed, (16, rows)).astype(jnp.bfloat16), upper,
            preferred_element_type=jnp.float32,
        )[:1]
        key = jnp.where(share > 0.0, count - 1.0, -1.0)
        return places == key, share

    def chooser(z, j, who):
        return jnp.where(pick(z, j, who)[0], 1.0, 0.0).astype(jnp.bfloat16)

    def picked(choice, array):
        return jnp.dot(choice, array, preferred_element_type=jnp.float32).astype(jnp.bfloat16)

    def pass_grad(z, j, d):
        @pl.when(goes(d))
        def _():
            c_copy(z, j, d).start()

        @pl.when(to_inner(d))
        def _():
            g_whole(z, j, d).start()

        @pl.when(to_end(d))
        def _():
            g_out[z, j] = picked(chooser(z, j, end_of(d)), g_full[z, j])
            g_picked(z, j, d).start()

    def pass_tokens(z, h, d):
        @pl.when(to_inner(d))
        def _():
            x_whole(z, h, d).start()

        @pl.when(to_end(d))
        def _():
            x_out[z, h] = picked(chooser(z, 0, end_of(d)), x_full[z, h])
            x_picked(z, h, d).start()

    def keep_tokens(z, h):
        x_comp[z, 0, h] = picked(chooser(z, 0, expert), x_full[z, h])
        yx(z, h).start()

    loads[3].wait()
    for d in range(2):
        pass_grad(expert, 0, d)
    for copy in loads[:3]:
        copy.wait()
    y_keys.wait_recv()
    y_values.wait_recv()

    contract = (((1,), (1,)), ((), ()))
    part_rows = rows // 2

    @pl.loop(0, 2)
    def _(p):
        part = pl.ds(pl.multiple_of(p * part_rows, part_rows), part_rows)
        causal = lax.broadcasted_iota(jnp.int32, (part_rows, rows), 1) <= (
            lax.broadcasted_iota(jnp.int32, (part_rows, rows), 0) + p * part_rows
        )
        seen = lax.broadcasted_iota(jnp.int32, (part_rows, rows), 1) < shard * rows
        squares = jnp.zeros((part_rows, 1), jnp.float32)
        for head in range(kv_heads * group_size):
            cols = slice(head * HEAD_DIM, (head + 1) * HEAD_DIM)
            kv = head // group_size
            kv_cols = slice(kv * HEAD_DIM, (kv + 1) * HEAD_DIM)
            q = q_ref[part, cols]
            own = lax.dot_general(
                q, k_ref[:, kv_cols], contract, preferred_element_type=jnp.float32
            )
            old = lax.dot_general(
                q, kv_buf[0, :, kv_cols], contract, preferred_element_type=jnp.float32
            )
            own = jnp.where(causal, own * scale, masked_score)
            old = jnp.where(seen, old * scale, masked_score)
            top = jnp.maximum(
                jnp.max(own, axis=1, keepdims=True), jnp.max(old, axis=1, keepdims=True)
            )
            own = jnp.exp(own - top)
            old = jnp.exp(old - top)
            total = jnp.sum(own, axis=1, keepdims=True) + jnp.sum(old, axis=1, keepdims=True)
            out = jnp.dot(
                own.astype(jnp.bfloat16), v_ref[:, kv_cols], preferred_element_type=jnp.float32
            ) + jnp.dot(
                old.astype(jnp.bfloat16), kv_buf[1, :, kv_cols],
                preferred_element_type=jnp.float32,
            )
            out = out / total
            attended[:, cols] = out
            squares = squares + jnp.sum(out * out, axis=1, keepdims=True)
        inverse = lax.rsqrt(squares / model_width + epsilon)
        normed = (attended[...] * inverse * gain_ref[...]).astype(jnp.bfloat16)
        for h in range(parts):
            x_full[expert, h, part] = normed[:, h * half : (h + 1) * half]

        @pl.when(p == 0)
        def _():
            y_share.wait_recv()
            y_grad.wait_recv()
            for d in range(2):
                pass_grad(expert, 1, d)

    for h in range(parts):
        for d in range(2):
            pass_tokens(expert, h, d)
        keep_tokens(expert, h)
    for j in range(2):
        g_comp[expert, j] = picked(chooser(expert, j, expert), g_full[expert, j])
    for copy in loads[4:]:
        copy.wait()

    tile = min(256, width)

    def columns(b):
        return pl.ds(pl.multiple_of(b * block, block), block)

    def add_piece(z, j):
        where, share = pick(z, j, expert)
        share = jnp.sum(jnp.where(where, share, 0.0), axis=1, keepdims=True)

        @pl.loop(0, width // tile)
        def _(t):
            cols = pl.ds(pl.multiple_of(t * tile, tile), tile)

            def product(weight):
                return sum(
                    jnp.dot(
                        x_comp[z, j, h], weight[h * half : (h + 1) * half, cols],
                        preferred_element_type=jnp.float32,
                    )
                    for h in range(parts)
                )

            pre_gate = product(weight_gate)
            pre_up = product(weight_up)
            cotangent = (share * g_comp[z, j, :, cols].astype(jnp.float32)).astype(jnp.bfloat16)
            sigmoid_gate = 1.0 / (1.0 + jnp.exp(-pre_gate))
            slope = sigmoid_gate * (1.0 + pre_gate * (1.0 - sigmoid_gate))
            delta_ref[:, cols] = (cotangent.astype(jnp.float32) * pre_up * slope).astype(
                jnp.bfloat16
            )

        @pl.loop(0, 4)
        def _(b):
            acc[:, columns(b)] += lax.dot_general(
                delta_ref[...], x_comp[z, j, b], (((0,), (0,)), ((), ())),
                preferred_element_type=jnp.float32,
            )

    def add_chunk(z):
        @pl.loop(0, 2)
        def _(j):
            @pl.when(j == 1)
            def _():
                for h in range(parts):
                    yx(z, h).wait_recv()

            add_piece(z, j)

    def present(z):
        return jnp.logical_and(z >= 0, z <= last)

    @pl.loop(1, n_ep + 1)
    def _(dist):
        for d in range(2):
            z = expert - dist if d else expert + dist

            @pl.when(present(z))
            def _():
                for j in range(2):
                    c_copy(z, j, d).wait_recv()

            @pl.when(jnp.logical_and(present(z), inner))
            def _():
                for j in range(2):
                    g_whole(z, j, d).wait_recv()
                    pass_grad(z, j, d)
                for h in range(parts):
                    x_whole(z, h, d).wait_recv()
                    pass_tokens(z, h, d)
                    keep_tokens(z, h)
                for j in range(2):
                    g_comp[z, j] = picked(chooser(z, j, expert), g_full[z, j])

            @pl.when(jnp.logical_and(present(z), jnp.logical_not(inner)))
            def _():
                for j in range(2):
                    g_picked(z, j, d).wait_recv()
                for h in range(parts):
                    x_picked(z, h, d).wait_recv()
                    yx(z, h).start()

        @pl.when(dist == 1)
        def _():
            add_chunk(expert)

        @pl.loop(0, 2)
        def _(d):
            z = expert + (dist - 1) * (1 - 2 * d)

            @pl.when(jnp.logical_and(dist > 1, present(z)))
            def _():
                add_chunk(z)

    slab = width // 2

    def to_core(i, t):
        rows_of = pl.ds(t * slab, slab)
        return send(stage.at[i, rows_of], from_core.at[i, rows_of], core_send.at[i, t],
                    core_recv.at[i, t], {"grp": sibling})

    def to_chip(t):
        rows_of = pl.ds(t * slab, slab)
        return send(carry.at[rows_of], from_chip.at[rows_of], chip_send.at[t], chip_recv.at[t],
                    {"grp": across})

    slabs = [slice(0, slab), slice(slab, width)]
    for t in range(2):
        stage[0, slabs[t]] = acc[slabs[t], columns(diagonal)].astype(jnp.bfloat16)
        to_core(0, t).start()
    for t in range(2):
        to_core(0, t).wait_recv()
        carry[slabs[t]] = (
            acc[slabs[t], columns(across)] + from_core[0, slabs[t]].astype(jnp.float32)
        ).astype(jnp.bfloat16)
        to_chip(t).start()
    for t in range(2):
        stage[1, slabs[t]] = acc[slabs[t], columns(sibling)].astype(jnp.bfloat16)
        to_core(1, t).start()
    for t in range(2):
        to_core(1, t).wait_recv()
        acc[slabs[t], columns(grp)] += from_core[1, slabs[t]].astype(jnp.float32)
    for t in range(2):
        to_chip(t).wait_recv()
        out_ref[:, slabs[t]] = (
            acc[slabs[t], columns(grp)] + from_chip[slabs[t]].astype(jnp.float32)
        ).T

    for copy in (y_keys, y_values, y_share, y_grad):
        copy.wait_send()
    for t in range(2):
        to_core(0, t).wait_send()
        to_core(1, t).wait_send()
        to_chip(t).wait_send()

    @pl.loop(0, n_ep)
    def _(z):
        for h in range(parts):
            yx(z, h).wait_send()
            for d in range(2):
                passed = z <= expert if d else z >= expert

                @pl.when(jnp.logical_and(passed, to_inner(d)))
                def _():
                    x_whole(z, h, d).wait_send()

                @pl.when(jnp.logical_and(passed, to_end(d)))
                def _():
                    x_picked(z, h, d).wait_send()

        for j in range(2):
            for d in range(2):
                passed = z <= expert if d else z >= expert

                @pl.when(jnp.logical_and(passed, goes(d)))
                def _():
                    c_copy(z, j, d).wait_send()

                @pl.when(jnp.logical_and(passed, to_inner(d)))
                def _():
                    g_whole(z, j, d).wait_send()

                @pl.when(jnp.logical_and(passed, to_end(d)))
                def _():
                    g_picked(z, j, d).wait_send()


def fused(
    queries, keys, values, norm_gain, expert_ids, gate_values, hidden_grad, gate_weight, up_weight
):
    rows, model_width = queries.shape
    n_ep = lax.axis_size("ep")
    width = gate_weight.shape[2]
    kv_width = keys.shape[1]
    block = model_width // 4
    parts = 4
    half = model_width // parts
    cap = rows * expert_ids.shape[1] // n_ep * 3 // 2
    chosen = expert_ids.T[:, None, :] == jnp.arange(8, dtype=jnp.int32)[:, None]
    share = jnp.sum(jnp.where(chosen, gate_values.T[:, None, :], 0.0), axis=0)
    vmem = pl.BlockSpec(memory_space=pltpu.VMEM)
    hbm = pl.BlockSpec(memory_space=pltpu.HBM)
    dma = pltpu.SemaphoreType.DMA
    bf16, f32 = jnp.bfloat16, jnp.float32
    out = pl.pallas_call(
        whole_kernel,
        out_shape=jax.ShapeDtypeStruct((block, width), f32),
        in_specs=[hbm] * 3 + [vmem] * 2 + [hbm] * 3,
        out_specs=vmem,
        scratch_shapes=[
            pltpu.VMEM((rows, model_width), bf16),
            pltpu.VMEM((rows, kv_width), bf16),
            pltpu.VMEM((rows, kv_width), bf16),
            pltpu.VMEM((n_ep, parts, rows, half), bf16),
            pltpu.VMEM((n_ep, 2, parts, cap, half), bf16),
            pltpu.VMEM((n_ep, parts, cap, half), bf16),
            pltpu.VMEM((n_ep, 2, rows, width), bf16),
            pltpu.VMEM((n_ep, 2, cap, width), bf16),
            pltpu.VMEM((n_ep, 2, cap, width), bf16),
            pltpu.VMEM((n_ep, 2, 8, rows), f32),
            pltpu.VMEM((2, rows, kv_width), bf16),
            pltpu.VMEM((model_width, width), bf16),
            pltpu.VMEM((model_width, width), bf16),
            pltpu.VMEM((cap, width), bf16),
            pltpu.VMEM((rows // 2, model_width), f32),
            pltpu.VMEM((width, model_width), f32),
            pltpu.VMEM((2, width, block), bf16),
            pltpu.VMEM((2, width, block), bf16),
            pltpu.VMEM((width, block), bf16),
            pltpu.VMEM((width, block), bf16),
            dma((6,)), dma((4,)), dma((4,)),
            dma((2, n_ep, 2)), dma((n_ep, 2)), dma((2, n_ep, 2)), dma((n_ep, 2)),
            dma((2, n_ep, parts)), dma((n_ep, parts)), dma((n_ep, parts)), dma((n_ep, parts)),
            dma((2, 2)), dma((2, 2)), dma((2,)), dma((2,)),
        ],
        compiler_params=pltpu.CompilerParams(
            collective_id=0, has_side_effects=True, vmem_limit_bytes=56 << 20
        ),
    )(
        queries, keys, values, norm_gain.reshape(1, -1), share, hidden_grad,
        gate_weight[0], up_weight[0],
    )
    return out[None]


def solution(mesh):
    small = mesh.shape["grp"] == 4 and mesh.shape["sq"] == 2 and mesh.shape["ep"] == 4
    return jax.shard_map(
        fused if small else body,
        mesh=mesh,
        in_specs=(
            P(("grp", "ep", "sq"), None),
            P(("grp", "ep", "sq"), None),
            P(("grp", "ep", "sq"), None),
            P(),
            P(("grp", "ep", "sq"), None),
            P(("grp", "ep", "sq"), None),
            P(("grp", "ep", "sq"), None),
            P("ep", None, "sq"),
            P("ep", None, "sq"),
        ),
        out_specs=P("ep", "grp", "sq"),
        check_vma=False,
    )
```

```python
import functools
import math

import jax
import jax.numpy as jnp
from jax import lax
from jax.experimental import pallas as pl
from jax.experimental.pallas import tpu as pltpu
from jax.sharding import PartitionSpec as P

HEAD_DIM = 128

epsilon = 1e-05
masked_score = -1e30
LOG2E = 1.4426950408889634
MESH = pl.DeviceIdType.MESH


def attention_kernel(group_size, shard_ref, q_ref, ko_ref, vo_ref, kp_ref, vp_ref, gain_ref, out_ref, acc_ref):
    rows, model_width = q_ref.shape
    past = kp_ref.shape[0]
    scale = 1.0 / math.sqrt(HEAD_DIM)
    shard = shard_ref[0]
    contract = (((1,), (1,)), ((), ()))
    causal = lax.broadcasted_iota(jnp.int32, (rows, rows), 1) <= lax.broadcasted_iota(
        jnp.int32, (rows, rows), 0
    )
    seen = lax.broadcasted_iota(jnp.int32, (rows, past), 1) < shard * rows
    squares = jnp.zeros((rows, 1), jnp.float32)
    for head in range(model_width // HEAD_DIM):
        cols = slice(head * HEAD_DIM, (head + 1) * HEAD_DIM)
        kv = head // group_size
        kv_cols = slice(kv * HEAD_DIM, (kv + 1) * HEAD_DIM)
        q = q_ref[:, cols]
        own = lax.dot_general(q, ko_ref[:, kv_cols], contract, preferred_element_type=jnp.float32)
        old = lax.dot_general(q, kp_ref[:, kv_cols], contract, preferred_element_type=jnp.float32)
        own = jnp.where(causal, own * scale, masked_score)
        old = jnp.where(seen, old * scale, masked_score)
        top = jnp.maximum(
            jnp.max(own, axis=1, keepdims=True), jnp.max(old, axis=1, keepdims=True)
        )
        own = jnp.exp(own - top)
        old = jnp.exp(old - top)
        total = jnp.sum(own, axis=1, keepdims=True) + jnp.sum(old, axis=1, keepdims=True)
        out = jnp.dot(
            own.astype(jnp.bfloat16), vo_ref[:, kv_cols], preferred_element_type=jnp.float32
        ) + jnp.dot(
            old.astype(jnp.bfloat16), vp_ref[:, kv_cols], preferred_element_type=jnp.float32
        )
        out = out / total
        acc_ref[:, cols] = out
        squares = squares + jnp.sum(out * out, axis=1, keepdims=True)
    inverse = lax.rsqrt(squares / model_width + epsilon)
    out_ref[...] = (acc_ref[...] * inverse * gain_ref[...]).astype(jnp.bfloat16)


def attend(shard, queries, keys, values, past_keys, past_values, norm_gain):
    rows, model_width = queries.shape
    group_size = model_width // keys.shape[1]
    vmem = pl.BlockSpec(memory_space=pltpu.VMEM)
    return pl.pallas_call(
        functools.partial(attention_kernel, group_size),
        out_shape=jax.ShapeDtypeStruct((rows, model_width), jnp.bfloat16),
        in_specs=[pl.BlockSpec(memory_space=pltpu.SMEM)] + [vmem] * 6,
        out_specs=vmem,
        scratch_shapes=[pltpu.VMEM((rows, model_width), jnp.float32)],
        compiler_params=pltpu.CompilerParams(vmem_limit_bytes=32 << 20),
        cost_estimate=pl.CostEstimate(
            flops=4 * rows * model_width * (rows + past_keys.shape[0]),
            bytes_accessed=4 * rows * model_width,
            transcendentals=rows * (model_width // HEAD_DIM) * (rows + past_keys.shape[0]),
        ),
    )(shard.reshape(1), queries, keys, values, past_keys, past_values, norm_gain.reshape(1, -1))


def ring(size, shift):
    return [(i, (i + shift) % size) for i in range(size)]


def body(
    queries, keys, values, norm_gain, expert_ids, gate_values, hidden_grad, gate_weight, up_weight
):
    rows, model_width = queries.shape
    n_ep = lax.axis_size("ep")
    n_sq = lax.axis_size("sq")
    shard = lax.axis_index("sq")
    expert = lax.axis_index("ep")
    weight_gate = gate_weight[0]
    weight_up = up_weight[0]
    width = weight_gate.shape[1]
    kv_width = keys.shape[1]

    both = jnp.concatenate([keys, values], axis=1)
    past = []
    for j in range(1, n_sq):
        past.append(lax.ppermute(both, "sq", [(i, i + j) for i in range(n_sq - j)]))
    past = jnp.concatenate(past, axis=0)

    def columns_of(owner):
        return lax.dynamic_slice_in_dim(hidden_grad, owner * width, width, 1)

    grads = [columns_of(shard)]
    for j in range(1, n_sq):
        grads.append(lax.ppermute(columns_of((shard + j) % n_sq), "sq", ring(n_sq, j)))
    grad = jnp.concatenate(grads, axis=0)

    chosen = expert_ids[:, :, None] == jnp.arange(n_ep, dtype=jnp.int32)
    share = jnp.sum(jnp.where(chosen, gate_values[:, :, None], 0.0), axis=1).T
    shares = lax.all_gather(share, ("ep", "sq"), axis=0, tiled=False)
    shares = lax.dynamic_index_in_dim(shares, expert, 1, keepdims=False).reshape(n_ep, n_sq, rows)
    shares = jnp.concatenate(
        [
            lax.dynamic_index_in_dim(shares, (shard - j) % n_sq, 1, keepdims=False)
            for j in range(n_sq)
        ],
        axis=1,
    )

    normed = attend(
        shard, queries, keys, values, past[:, :kv_width], past[:, kv_width:], norm_gain
    )

    def add_chunk(step, tokens, grad, summed):
        source = (expert - step) % n_ep
        share_here = lax.dynamic_index_in_dim(shares, source, 0, keepdims=False)
        pieces = [tokens]
        for j in range(1, n_sq):
            pieces.append(lax.ppermute(tokens, "sq", ring(n_sq, j)))
        for j, inputs in enumerate(pieces):
            part = slice(j * rows, (j + 1) * rows)
            cotangent = (share_here[part, None] * grad[part].astype(jnp.float32)).astype(
                jnp.bfloat16
            )
            pre_gate = jnp.dot(inputs, weight_gate, preferred_element_type=jnp.float32)
            pre_up = jnp.dot(inputs, weight_up, preferred_element_type=jnp.float32)
            sigmoid_gate = jax.nn.sigmoid(pre_gate)
            slope = sigmoid_gate * (1.0 + pre_gate * (1.0 - sigmoid_gate))
            delta = (cotangent.astype(jnp.float32) * pre_up * slope).astype(jnp.bfloat16)
            term = lax.dot_general(
                inputs, delta, (((0,), (0,)), ((), ())), preferred_element_type=jnp.float32
            )
            summed = term if summed is None else summed + term
        return summed

    def turn(tokens, grad):
        return lax.ppermute(tokens, "ep", ring(n_ep, 1)), lax.ppermute(grad, "ep", ring(n_ep, 1))

    if n_ep <= 8:
        summed = None
        tokens = normed
        for step in range(n_ep):
            if step < n_ep - 1:
                turned = turn(tokens, grad)
            summed = add_chunk(step, tokens, grad, summed)
            if step < n_ep - 1:
                tokens, grad = turned
    else:

        def one_step(step, carried):
            tokens, grad, summed = carried
            turned = turn(tokens, grad)
            return (*turned, add_chunk(step, tokens, grad, summed))

        start = jnp.zeros((model_width, width), jnp.float32)
        summed = lax.fori_loop(0, n_ep, one_step, (normed, grad, start))[2]
    return lax.psum_scatter(
        summed[None].astype(jnp.bfloat16), "grp", scatter_dimension=1, tiled=True
    ).astype(jnp.float32)


def whole_kernel(
    q_hbm, k_hbm, v_hbm, gain_ref, share_ref, hidden_hbm, gate_hbm, up_hbm, out_ref,
    q_ref, k_ref, v_ref, kv_buf, attended, x_full, x_out, g_full, g_out, c_buf, choice_ref,
    w_gate, w_up, h_ref, delta_ref, acc, stage, from_core, x_stage, y_stage, own_block,
    x_first, y_first, x_second, y_second,
    load_sem, kv_send, kv_recv, wy_send, wy_recv, ws_send, ws_recv, wa_send, wa_recv,
    wd_send, wd_recv, c_send, c_recv, gf_send, gn_send, g_recv, xf_send, xn_send, x_recv,
    core_send, core_recv, first_send, first_recv, second_send, second_recv,
):
    n_ep = x_full.shape[0]
    rows, model_width = q_ref.shape
    cap = x_out.shape[2]
    parts = x_full.shape[1]
    part_width = model_width // parts
    width = gate_hbm.shape[1]
    quarter = width // 2
    half = quarter // 2
    kv_heads = k_ref.shape[1] // HEAD_DIM
    group_size = model_width // k_ref.shape[1]
    block = model_width // 4
    bf16, f32 = jnp.bfloat16, jnp.float32
    grp, expert, shard = lax.axis_index("grp"), lax.axis_index("ep"), lax.axis_index("sq")
    peer = 1 - shard
    core = lax.rem(grp, 2)
    chip = grp // 2
    sibling = chip * 2 + 1 - core
    across = (1 - chip) * 2 + core
    diagonal = (1 - chip) * 2 + 1 - core
    last = n_ep - 1
    right, left = lax.rem(expert + 1, n_ep), lax.rem(expert + last, n_ep)
    upper_side = expert // 2
    inner = jnp.logical_and(expert > 0, expert < last)
    outer = jnp.logical_not(inner)
    end = 3 * upper_side
    middle = 1 + upper_side
    far_middle = 2 - upper_side
    far_end = 3 - 3 * upper_side
    far = {"ep": jnp.where(inner, far_middle, middle)}
    near = {"ep": end}
    first = jnp.where(inner, end, middle)

    def load(i, src, dst):
        return pltpu.make_async_copy(src, dst, load_sem.at[i])

    loads = [
        load(0, q_hbm, q_ref),
        load(1, k_hbm, k_ref),
        load(2, v_hbm, v_ref),
        load(3, gate_hbm, w_gate.at[shard]),
        load(4, up_hbm, w_up.at[shard]),
    ]
    grad_loads = [
        load(
            5 + 2 * ab + h,
            hidden_hbm.at[:, h * width + ab * quarter : h * width + (ab + 1) * quarter],
            g_full.at[expert, ab, :, h * quarter : (h + 1) * quarter],
        )
        for ab in range(2)
        for h in range(2)
    ]
    for copy in grad_loads + loads:
        copy.start()

    c_buf[...] = jnp.ones_like(c_buf)
    c_buf[expert] = share_ref[...]

    @pl.when(outer)
    def _():
        for z in range(n_ep):

            @pl.when(z != expert)
            def _():
                for p in range(parts):
                    x_full[z, p, cap:rows] = jnp.zeros((rows - cap, part_width), bf16)
                for ab in range(2):
                    g_full[z, ab, cap:rows] = jnp.zeros((rows - cap, width), bf16)

    @pl.when(shard == 0)
    def _():
        kv_buf[...] = jnp.zeros_like(kv_buf)

    barrier = pltpu.get_barrier_semaphore()
    for target in ({"sq": peer}, {"ep": right}, {"ep": left}, {"grp": sibling}, {"grp": across}):
        pl.semaphore_signal(barrier, inc=1, device_id=target, device_id_type=MESH)
    pl.semaphore_wait(barrier, 5)

    def send(src, dst, send_sem, recv_sem, target):
        return pltpu.make_async_remote_copy(
            src_ref=src, dst_ref=dst, send_sem=send_sem, recv_sem=recv_sem,
            device_id=target, device_id_type=MESH,
        )

    def kv_copy(i, kv):
        cols = slice(kv * HEAD_DIM, (kv + 1) * HEAD_DIM)
        return send((k_hbm, v_hbm)[i].at[:, cols], kv_buf.at[i, :, cols],
                    kv_send.at[i, kv], kv_recv.at[i, kv], {"sq": peer})

    weights = (w_gate, w_up)

    def rows_of(owner):
        return pl.ds(pl.multiple_of(owner * block, block), block)

    def w_across_y(i):
        mine = rows_of(grp)
        return send((gate_hbm, up_hbm)[i].at[mine], weights[i].at[shard, mine],
                    wy_send.at[i], wy_recv.at[i], {"sq": peer})

    def w_arrived_y(i):
        mine = rows_of(grp)
        return send((gate_hbm, up_hbm)[i].at[mine], weights[i].at[peer, mine],
                    wy_send.at[i], wy_recv.at[i], {"sq": peer})

    def w_on(i, owner, target, send_sem, recv_sem):
        there = weights[i].at[peer, rows_of(owner)]
        return send(there, there, send_sem.at[i], recv_sem.at[i], {"grp": target})

    def w_sibling(i, owner):
        return w_on(i, owner, sibling, ws_send, ws_recv)

    def w_across(i, owner):
        return w_on(i, owner, across, wa_send, wa_recv)

    def w_diagonal(i, owner):
        return w_on(i, owner, sibling, wd_send, wd_recv)

    def c_copy(z, slot):
        return send(c_buf.at[z], c_buf.at[z], c_send.at[slot], c_recv.at[z], far)

    def g_far(z, ab, slot):
        return send(g_full.at[z, ab], g_full.at[z, ab], gf_send.at[slot, ab], g_recv.at[z, ab], far)

    def g_near(z, ab, slot):
        return send(g_out.at[slot, ab], g_full.at[z, ab, 0:cap], gn_send.at[slot, ab],
                    g_recv.at[z, ab], near)

    def x_far(z, p, slot):
        return send(x_full.at[z, p], x_full.at[z, p], xf_send.at[slot, p], x_recv.at[z, p], far)

    def x_near(z, p, slot):
        return send(x_out.at[slot, p], x_full.at[z, p, 0:cap], xn_send.at[slot, p],
                    x_recv.at[z, p], near)

    @pl.when(shard == 0)
    def _():
        for kv in range(kv_heads):
            for i in range(2):
                kv_copy(i, kv).start()

    for i in range(2):
        w_across_y(i).start()

    def share_row(z, who):
        share = c_buf[z]
        here = lax.broadcasted_iota(jnp.int32, share.shape, 0) == who
        return jnp.sum(jnp.where(here, share, 0.0), axis=0, keepdims=True)

    def choose(z, slot):
        upper = (
            lax.broadcasted_iota(jnp.int32, (rows, rows), 0)
            <= lax.broadcasted_iota(jnp.int32, (rows, rows), 1)
        ).astype(f32).astype(bf16)
        places = lax.broadcasted_iota(jnp.int32, (cap, rows), 0).astype(f32)
        share = share_row(z, end)
        routed = jnp.where(share > 0.0, 1.0, 0.0)
        count = jnp.dot(
            jnp.broadcast_to(routed, (16, rows)).astype(bf16), upper, preferred_element_type=f32
        )[:1]
        key = jnp.where(share > 0.0, count - 1.0, -1.0)
        choice_ref[slot] = jnp.where(places == key, 1.0, 0.0).astype(bf16)

    def grad_near(z, ab, slot):
        choice = choice_ref[slot]
        share = jnp.sum(choice.astype(f32) * share_row(z, end), axis=1, keepdims=True)
        grad = jnp.dot(choice, g_full[z, ab], preferred_element_type=f32)
        g_out[slot, ab] = (share * grad).astype(bf16)
        g_near(z, ab, slot).start()

    def tokens_near(z, p, slot):
        x_out[slot, p] = jnp.dot(
            choice_ref[slot], x_full[z, p], preferred_element_type=f32
        ).astype(bf16)
        x_near(z, p, slot).start()

    for copy in grad_loads[:2]:
        copy.wait()
    c_copy(expert, 0).start()
    g_far(expert, 0, 0).start()

    @pl.when(inner)
    def _():
        choose(expert, 0)
        grad_near(expert, 0, 0)

    for copy in loads[:3] + grad_loads[2:]:
        copy.wait()

    def early_grads():
        @pl.when(inner)
        def _():
            c_copy(end, 1).wait_recv()
            g_far(end, 0, 1).wait_recv()
            c_copy(end, 1).start()
            g_far(end, 0, 1).start()
            c_copy(far_middle, 0).wait_recv()
            g_far(far_middle, 0, 0).wait_recv()
            choose(far_middle, 1)
            grad_near(far_middle, 0, 1)

    contract = (((1,), (1,)), ((), ()))
    part_rows = rows // 2
    factor = LOG2E / math.sqrt(HEAD_DIM)
    hide = jnp.where(shard == 0, masked_score, 0.0)
    causal = lax.broadcasted_iota(jnp.int32, (part_rows, part_rows), 1) <= (
        lax.broadcasted_iota(jnp.int32, (part_rows, part_rows), 0)
    )
    squares = [jnp.zeros((part_rows, 1), f32)] * 2
    for kv in range(kv_heads):
        kv_cols = slice(kv * HEAD_DIM, (kv + 1) * HEAD_DIM)

        @pl.when(shard == 1)
        def _():
            for i in range(2):
                kv_copy(i, kv).wait_recv()

        if kv == 2:
            early_grads()
        for head in range(kv * group_size, (kv + 1) * group_size):
            cols = slice(head * HEAD_DIM, (head + 1) * HEAD_DIM)
            for p in range(2):
                part = slice(p * part_rows, (p + 1) * part_rows)
                q = q_ref[part, cols]

                def scored(keys):
                    return lax.dot_general(q, keys, contract, preferred_element_type=f32)

                near_scores = jnp.where(causal, scored(k_ref[part, kv_cols]), masked_score)
                pieces = [(near_scores, v_ref[part, kv_cols], 0.0)]
                if p:
                    pieces.append(
                        (scored(k_ref[:part_rows, kv_cols]), v_ref[:part_rows, kv_cols], 0.0)
                    )
                pieces.append((scored(kv_buf[0, :, kv_cols]), kv_buf[1, :, kv_cols], hide))
                top = functools.reduce(
                    jnp.maximum,
                    [jnp.max(s, axis=1, keepdims=True) * factor + away for s, _, away in pieces],
                )
                terms = [jnp.exp2(s * factor - (top - away)) for s, _, away in pieces]
                total = functools.reduce(
                    jnp.add, [jnp.sum(e, axis=1, keepdims=True) for e in terms]
                )
                out = functools.reduce(
                    jnp.add,
                    [
                        jnp.dot(e.astype(bf16), v, preferred_element_type=f32)
                        for e, (_, v, _) in zip(terms, pieces)
                    ],
                )
                out = out * (1.0 / total)
                attended[part, cols] = out
                squares[p] = squares[p] + jnp.sum(out * out, axis=1, keepdims=True)
    inverse = [lax.rsqrt(s / model_width + epsilon) for s in squares]
    for h in range(parts):
        cols = slice(h * part_width, (h + 1) * part_width)
        for p in range(2):
            part = slice(p * part_rows, (p + 1) * part_rows)
            x_full[expert, h, part] = (
                attended[part, cols] * inverse[p] * gain_ref[:, cols]
            ).astype(bf16)
        x_far(expert, h, 0).start()

    @pl.when(inner)
    def _():
        c_copy(far_end, 1).wait_recv()
        g_far(far_end, 0, 1).wait_recv()
        choose(far_end, 2)
        grad_near(far_end, 0, 2)
        for h in range(parts):
            tokens_near(expert, h, 0)

    @pl.when(outer)
    def _():
        g_far(expert, 1, 0).start()

    for i in range(2):
        loads[3 + i].wait()

    def weights_from_y(i):
        w_arrived_y(i).wait_recv()
        w_across(i, grp).start()
        w_sibling(i, grp).start()

    def weights_from_x(i):
        w_across(i, across).wait_recv()
        w_diagonal(i, across).start()

    def first_tokens(h):
        @pl.when(inner)
        def _():
            x_far(end, h, 1).wait_recv()
            x_far(end, h, 1).start()
            x_far(far_middle, h, 0).wait_recv()
            tokens_near(far_middle, h, 1)

    def second_tokens(h):
        @pl.when(inner)
        def _():
            x_far(far_end, h, 1).wait_recv()
            tokens_near(far_end, h, 2)

    first_tokens(0)
    weights_from_y(0)
    first_tokens(1)
    weights_from_y(1)
    first_tokens(2)
    weights_from_x(0)
    first_tokens(3)

    @pl.when(inner)
    def _():
        g_far(expert, 1, 0).start()
        g_far(end, 1, 1).wait_recv()
        g_far(end, 1, 1).start()

    weights_from_x(1)
    for i in range(2):
        w_sibling(i, sibling).wait_recv()
        w_diagonal(i, diagonal).wait_recv()

    def forward(z):
        @pl.loop(0, 4)
        def _(t):
            ab, side = t // 2, lax.rem(t, 2)
            cols = pl.ds(pl.multiple_of(ab * quarter, quarter), quarter)

            def product(weight):
                return sum(
                    jnp.dot(
                        x_full[z, h], weight[side, h * part_width : (h + 1) * part_width, cols],
                        preferred_element_type=f32,
                    )
                    for h in range(parts)
                )

            pre_gate = product(w_gate)
            pre_up = product(w_up)
            sigmoid_gate = 1.0 / (1.0 + jnp.exp(-pre_gate))
            slope = sigmoid_gate * (1.0 + pre_gate * (1.0 - sigmoid_gate))
            h_ref[z, ab, :, pl.ds(pl.multiple_of(side * quarter, quarter), quarter)] = (
                pre_up * slope
            )

    diag = lax.broadcasted_iota(jnp.int32, (rows, rows), 0) == lax.broadcasted_iota(
        jnp.int32, (rows, rows), 1
    )

    def products(z, ab, fresh):
        share = jnp.sum(jnp.where(diag, share_row(z, expert), 0.0), axis=1, keepdims=True)
        cotangent = (share * g_full[z, ab].astype(f32)).astype(bf16).astype(f32)
        delta_ref[...] = (cotangent * h_ref[z, ab]).T.astype(bf16)

        @pl.loop(0, parts)
        def _(h):
            cols = pl.ds(pl.multiple_of(h * part_width, part_width), part_width)
            term = jnp.dot(delta_ref[...], x_full[z, h], preferred_element_type=f32)
            if fresh:
                acc[ab, :, cols] = term
            else:
                acc[ab, :, cols] += term

    def grads_here(z, ab, slot):
        @pl.when(outer)
        def _():
            g_near(z, ab, slot).wait_recv()

    def tokens_here(z, slot):
        @pl.when(outer)
        def _():
            for h in range(parts):
                x_near(z, h, slot).wait_recv()

    forward(expert)
    second_tokens(0)
    products(expert, 0, True)
    tokens_here(first, 0)
    forward(first)
    second_tokens(1)
    grads_here(first, 0, 0)
    products(first, 0, False)
    tokens_here(far_middle, 1)
    second_tokens(2)
    forward(far_middle)
    grads_here(far_middle, 0, 1)
    products(far_middle, 0, False)
    products(expert, 1, True)
    second_tokens(3)

    @pl.when(inner)
    def _():
        grad_near(expert, 1, 0)
        g_far(far_middle, 1, 0).wait_recv()
        grad_near(far_middle, 1, 1)

    tokens_here(far_end, 2)
    forward(far_end)
    grads_here(far_end, 0, 2)
    products(far_end, 0, False)

    def block_of(c):
        return pl.ds(pl.multiple_of(c * block, block), block)

    def to_core(ab, t):
        return send(stage.at[ab, t], from_core.at[ab, t], core_send.at[ab, t],
                    core_recv.at[ab, t], {"grp": sibling})

    def first_copy(ab, t):
        src, dst, target = (
            (x_stage, x_first, {"grp": across}),
            (y_stage, y_first, {"sq": peer}),
        )[t]
        return send(src.at[ab, 0], dst.at[ab], first_send.at[ab, t], first_recv.at[ab, t], target)

    def second_copy(ab, t, i):
        src, dst, target = (
            (x_stage, x_second, {"grp": across}),
            (y_stage, y_second, {"sq": peer}),
        )[t]
        return send(src.at[ab, 1 + i], dst.at[ab, i], second_send.at[ab, t, i],
                    second_recv.at[ab, t, i], target)

    def side_rows(side):
        return pl.ds(pl.multiple_of(side * quarter, quarter), quarter)

    def reduce_start(ab):
        for t, owner in enumerate((diagonal, sibling)):
            stage[ab, t] = acc[ab, :, block_of(owner)].astype(bf16)
            to_core(ab, t).start()

    def chip_sum(ab, t, owner, side):
        return acc[ab, side_rows(side), block_of(owner)] + (
            from_core[ab, t, side_rows(side)].astype(f32)
        )

    def reduce_middle(ab):
        to_core(ab, 0).wait_recv()
        both = chip_sum(ab, 0, across, peer).astype(bf16)
        x_stage[ab, 0] = both[:half]
        y_stage[ab, 0] = both[half:]
        for t in range(2):
            first_copy(ab, t).start()
        x_side = chip_sum(ab, 0, across, shard)
        x_stage[ab, 1] = x_side[:half].astype(bf16)
        second_copy(ab, 0, 0).start()
        to_core(ab, 1).wait_recv()
        y_side = chip_sum(ab, 1, grp, peer)
        y_stage[ab, 1] = y_side[half:].astype(bf16)
        second_copy(ab, 1, 0).start()
        own_block[ab] = chip_sum(ab, 1, grp, shard)
        first_copy(ab, 1).wait_recv()
        x_stage[ab, 2] = (x_side[half:] + y_first[ab].astype(f32)).astype(bf16)
        second_copy(ab, 0, 1).start()
        first_copy(ab, 0).wait_recv()
        y_stage[ab, 2] = (y_side[:half] + x_first[ab].astype(f32)).astype(bf16)
        second_copy(ab, 1, 1).start()

    def reduce_end(ab):
        for t in range(2):
            for i in range(2):
                second_copy(ab, t, i).wait_recv()
        top = (
            own_block[ab, :half] + x_second[ab, 0].astype(f32) + y_second[ab, 1].astype(f32)
        )
        bottom = (
            own_block[ab, half:] + x_second[ab, 1].astype(f32) + y_second[ab, 0].astype(f32)
        )
        out_ref[:, ab * quarter : ab * quarter + half] = top.T
        out_ref[:, ab * quarter + half : (ab + 1) * quarter] = bottom.T

    reduce_start(0)

    @pl.when(inner)
    def _():
        g_far(far_end, 1, 1).wait_recv()
        grad_near(far_end, 1, 2)

    reduce_middle(0)
    grads_here(first, 1, 0)
    products(first, 1, False)
    grads_here(far_middle, 1, 1)
    products(far_middle, 1, False)
    grads_here(far_end, 1, 2)
    products(far_end, 1, False)
    reduce_start(1)
    reduce_middle(1)
    reduce_end(0)
    reduce_end(1)

    @pl.when(shard == 0)
    def _():
        for kv in range(kv_heads):
            for i in range(2):
                kv_copy(i, kv).wait_send()

    for i in range(2):
        w_across_y(i).wait_send()
        w_sibling(i, grp).wait_send()
        w_across(i, grp).wait_send()
        w_diagonal(i, across).wait_send()
    c_copy(expert, 0).wait_send()
    for ab in range(2):
        g_far(expert, ab, 0).wait_send()
    for h in range(parts):
        x_far(expert, h, 0).wait_send()

    @pl.when(inner)
    def _():
        c_copy(end, 1).wait_send()
        for ab in range(2):
            g_far(end, ab, 1).wait_send()
        for h in range(parts):
            x_far(end, h, 1).wait_send()
        for slot, z in enumerate((expert, far_middle, far_end)):
            for ab in range(2):
                g_near(z, ab, slot).wait_send()
            for h in range(parts):
                x_near(z, h, slot).wait_send()

    for ab in range(2):
        for t in range(2):
            to_core(ab, t).wait_send()
            first_copy(ab, t).wait_send()
            for i in range(2):
                second_copy(ab, t, i).wait_send()


def fused(
    queries, keys, values, norm_gain, expert_ids, gate_values, hidden_grad, gate_weight, up_weight
):
    rows, model_width = queries.shape
    n_ep = lax.axis_size("ep")
    width = gate_weight.shape[2]
    kv_width = keys.shape[1]
    kv_heads = kv_width // HEAD_DIM
    block = model_width // 4
    parts = 4
    part_width = model_width // parts
    quarter = width // 2
    cap = rows * expert_ids.shape[1] // n_ep * 3 // 2
    chosen = expert_ids.T[:, None, :] == jnp.arange(8, dtype=jnp.int32)[:, None]
    share = jnp.sum(jnp.where(chosen, gate_values.T[:, None, :], 0.0), axis=0)
    vmem = pl.BlockSpec(memory_space=pltpu.VMEM)
    hbm = pl.BlockSpec(memory_space=pltpu.HBM)
    dma = pltpu.SemaphoreType.DMA
    bf16, f32 = jnp.bfloat16, jnp.float32
    out = pl.pallas_call(
        whole_kernel,
        out_shape=jax.ShapeDtypeStruct((block, width), f32),
        in_specs=[hbm] * 3 + [vmem] * 2 + [hbm] * 3,
        out_specs=vmem,
        scratch_shapes=[
            pltpu.VMEM((rows, model_width), bf16),
            pltpu.VMEM((rows, kv_width), bf16),
            pltpu.VMEM((rows, kv_width), bf16),
            pltpu.VMEM((2, rows, kv_width), bf16),
            pltpu.VMEM((rows, model_width), f32),
            pltpu.VMEM((n_ep, parts, rows, part_width), bf16),
            pltpu.VMEM((3, parts, cap, part_width), bf16),
            pltpu.VMEM((n_ep, 2, rows, width), bf16),
            pltpu.VMEM((3, 2, cap, width), bf16),
            pltpu.VMEM((n_ep, 8, rows), f32),
            pltpu.VMEM((3, cap, rows), bf16),
            pltpu.VMEM((2, model_width, width), bf16),
            pltpu.VMEM((2, model_width, width), bf16),
            pltpu.VMEM((n_ep, 2, rows, width), f32),
            pltpu.VMEM((width, rows), bf16),
            pltpu.VMEM((2, width, model_width), f32),
            pltpu.VMEM((2, 2, width, block), bf16),
            pltpu.VMEM((2, 2, width, block), bf16),
            pltpu.VMEM((2, 3, quarter // 2, block), bf16),
            pltpu.VMEM((2, 3, quarter // 2, block), bf16),
            pltpu.VMEM((2, quarter, block), f32),
            pltpu.VMEM((2, quarter // 2, block), bf16),
            pltpu.VMEM((2, quarter // 2, block), bf16),
            pltpu.VMEM((2, 2, quarter // 2, block), bf16),
            pltpu.VMEM((2, 2, quarter // 2, block), bf16),
            dma((9,)), dma((2, kv_heads)), dma((2, kv_heads)),
            dma((2,)), dma((2,)), dma((2,)), dma((2,)), dma((2,)), dma((2,)), dma((2,)), dma((2,)),
            dma((2,)), dma((n_ep,)), dma((2, 2)), dma((3, 2)), dma((n_ep, 2)),
            dma((2, parts)), dma((3, parts)), dma((n_ep, parts)),
            dma((2, 2)), dma((2, 2)), dma((2, 2)), dma((2, 2)), dma((2, 2, 2)), dma((2, 2, 2)),
        ],
        compiler_params=pltpu.CompilerParams(
            collective_id=0, has_side_effects=True, vmem_limit_bytes=56 << 20
        ),
    )(
        queries, keys, values, norm_gain.reshape(1, -1), share, hidden_grad,
        gate_weight[0], up_weight[0],
    )
    return out[None]


def solution(mesh):
    small = mesh.shape["grp"] == 4 and mesh.shape["sq"] == 2 and mesh.shape["ep"] == 4
    return jax.shard_map(
        fused if small else body,
        mesh=mesh,
        in_specs=(
            P(("grp", "ep", "sq"), None),
            P(("grp", "ep", "sq"), None),
            P(("grp", "ep", "sq"), None),
            P(),
            P(("grp", "ep", "sq"), None),
            P(("grp", "ep", "sq"), None),
            P(("grp", "ep", "sq"), None),
            P("ep", None, "sq"),
            P("ep", None, "sq"),
        ),
        out_specs=P("ep", "grp", "sq"),
        check_vma=False,
    )
```

```python
import functools
import math

import jax
import jax.numpy as jnp
from jax import lax
from jax.experimental import pallas as pl
from jax.experimental.pallas import tpu as pltpu
from jax.sharding import PartitionSpec as P

HEAD_DIM = 128

epsilon = 1e-05
masked_score = -1e30
LOG2E = 1.4426950408889634
MESH = pl.DeviceIdType.MESH


def attention_kernel(group_size, shard_ref, q_ref, ko_ref, vo_ref, kp_ref, vp_ref, gain_ref, out_ref, acc_ref):
    rows, model_width = q_ref.shape
    past = kp_ref.shape[0]
    scale = 1.0 / math.sqrt(HEAD_DIM)
    shard = shard_ref[0]
    contract = (((1,), (1,)), ((), ()))
    causal = lax.broadcasted_iota(jnp.int32, (rows, rows), 1) <= lax.broadcasted_iota(
        jnp.int32, (rows, rows), 0
    )
    seen = lax.broadcasted_iota(jnp.int32, (rows, past), 1) < shard * rows
    squares = jnp.zeros((rows, 1), jnp.float32)
    for head in range(model_width // HEAD_DIM):
        cols = slice(head * HEAD_DIM, (head + 1) * HEAD_DIM)
        kv = head // group_size
        kv_cols = slice(kv * HEAD_DIM, (kv + 1) * HEAD_DIM)
        q = q_ref[:, cols]
        own = lax.dot_general(q, ko_ref[:, kv_cols], contract, preferred_element_type=jnp.float32)
        old = lax.dot_general(q, kp_ref[:, kv_cols], contract, preferred_element_type=jnp.float32)
        own = jnp.where(causal, own * scale, masked_score)
        old = jnp.where(seen, old * scale, masked_score)
        top = jnp.maximum(
            jnp.max(own, axis=1, keepdims=True), jnp.max(old, axis=1, keepdims=True)
        )
        own = jnp.exp(own - top)
        old = jnp.exp(old - top)
        total = jnp.sum(own, axis=1, keepdims=True) + jnp.sum(old, axis=1, keepdims=True)
        out = jnp.dot(
            own.astype(jnp.bfloat16), vo_ref[:, kv_cols], preferred_element_type=jnp.float32
        ) + jnp.dot(
            old.astype(jnp.bfloat16), vp_ref[:, kv_cols], preferred_element_type=jnp.float32
        )
        out = out / total
        acc_ref[:, cols] = out
        squares = squares + jnp.sum(out * out, axis=1, keepdims=True)
    inverse = lax.rsqrt(squares / model_width + epsilon)
    out_ref[...] = (acc_ref[...] * inverse * gain_ref[...]).astype(jnp.bfloat16)


def attend(shard, queries, keys, values, past_keys, past_values, norm_gain):
    rows, model_width = queries.shape
    group_size = model_width // keys.shape[1]
    vmem = pl.BlockSpec(memory_space=pltpu.VMEM)
    return pl.pallas_call(
        functools.partial(attention_kernel, group_size),
        out_shape=jax.ShapeDtypeStruct((rows, model_width), jnp.bfloat16),
        in_specs=[pl.BlockSpec(memory_space=pltpu.SMEM)] + [vmem] * 6,
        out_specs=vmem,
        scratch_shapes=[pltpu.VMEM((rows, model_width), jnp.float32)],
        compiler_params=pltpu.CompilerParams(vmem_limit_bytes=32 << 20),
        cost_estimate=pl.CostEstimate(
            flops=4 * rows * model_width * (rows + past_keys.shape[0]),
            bytes_accessed=4 * rows * model_width,
            transcendentals=rows * (model_width // HEAD_DIM) * (rows + past_keys.shape[0]),
        ),
    )(shard.reshape(1), queries, keys, values, past_keys, past_values, norm_gain.reshape(1, -1))


def ring(size, shift):
    return [(i, (i + shift) % size) for i in range(size)]


def body(
    queries, keys, values, norm_gain, expert_ids, gate_values, hidden_grad, gate_weight, up_weight
):
    rows, model_width = queries.shape
    n_ep = lax.axis_size("ep")
    n_sq = lax.axis_size("sq")
    shard = lax.axis_index("sq")
    expert = lax.axis_index("ep")
    weight_gate = gate_weight[0]
    weight_up = up_weight[0]
    width = weight_gate.shape[1]
    kv_width = keys.shape[1]

    both = jnp.concatenate([keys, values], axis=1)
    past = []
    for j in range(1, n_sq):
        past.append(lax.ppermute(both, "sq", [(i, i + j) for i in range(n_sq - j)]))
    past = jnp.concatenate(past, axis=0)

    def columns_of(owner):
        return lax.dynamic_slice_in_dim(hidden_grad, owner * width, width, 1)

    grads = [columns_of(shard)]
    for j in range(1, n_sq):
        grads.append(lax.ppermute(columns_of((shard + j) % n_sq), "sq", ring(n_sq, j)))
    grad = jnp.concatenate(grads, axis=0)

    chosen = expert_ids[:, :, None] == jnp.arange(n_ep, dtype=jnp.int32)
    share = jnp.sum(jnp.where(chosen, gate_values[:, :, None], 0.0), axis=1).T
    shares = lax.all_gather(share, ("ep", "sq"), axis=0, tiled=False)
    shares = lax.dynamic_index_in_dim(shares, expert, 1, keepdims=False).reshape(n_ep, n_sq, rows)
    shares = jnp.concatenate(
        [
            lax.dynamic_index_in_dim(shares, (shard - j) % n_sq, 1, keepdims=False)
            for j in range(n_sq)
        ],
        axis=1,
    )

    normed = attend(
        shard, queries, keys, values, past[:, :kv_width], past[:, kv_width:], norm_gain
    )

    def add_chunk(step, tokens, grad, summed):
        source = (expert - step) % n_ep
        share_here = lax.dynamic_index_in_dim(shares, source, 0, keepdims=False)
        pieces = [tokens]
        for j in range(1, n_sq):
            pieces.append(lax.ppermute(tokens, "sq", ring(n_sq, j)))
        for j, inputs in enumerate(pieces):
            part = slice(j * rows, (j + 1) * rows)
            cotangent = (share_here[part, None] * grad[part].astype(jnp.float32)).astype(
                jnp.bfloat16
            )
            pre_gate = jnp.dot(inputs, weight_gate, preferred_element_type=jnp.float32)
            pre_up = jnp.dot(inputs, weight_up, preferred_element_type=jnp.float32)
            sigmoid_gate = jax.nn.sigmoid(pre_gate)
            slope = sigmoid_gate * (1.0 + pre_gate * (1.0 - sigmoid_gate))
            delta = (cotangent.astype(jnp.float32) * pre_up * slope).astype(jnp.bfloat16)
            term = lax.dot_general(
                inputs, delta, (((0,), (0,)), ((), ())), preferred_element_type=jnp.float32
            )
            summed = term if summed is None else summed + term
        return summed

    def turn(tokens, grad):
        return lax.ppermute(tokens, "ep", ring(n_ep, 1)), lax.ppermute(grad, "ep", ring(n_ep, 1))

    if n_ep <= 8:
        summed = None
        tokens = normed
        for step in range(n_ep):
            if step < n_ep - 1:
                turned = turn(tokens, grad)
            summed = add_chunk(step, tokens, grad, summed)
            if step < n_ep - 1:
                tokens, grad = turned
    else:

        def one_step(step, carried):
            tokens, grad, summed = carried
            turned = turn(tokens, grad)
            return (*turned, add_chunk(step, tokens, grad, summed))

        start = jnp.zeros((model_width, width), jnp.float32)
        summed = lax.fori_loop(0, n_ep, one_step, (normed, grad, start))[2]
    return lax.psum_scatter(
        summed[None].astype(jnp.bfloat16), "grp", scatter_dimension=1, tiled=True
    ).astype(jnp.float32)


def whole_kernel(
    q_hbm, k_hbm, v_hbm, gain_ref, share_ref, hidden_hbm, gate_hbm, up_hbm, out_ref,
    q_ref, k_ref, v_ref, kv_buf, attended, x_full, x_out, g_full, g_out, c_buf, choice_ref,
    w_gate, w_up, h_ref, pre_ref, delta_ref, acc, stage, from_core, x_stage, y_stage, own_block,
    x_rest, y_rest,
    x_first, y_first, x_second, y_second,
    load_sem, kv_send, kv_recv, wy_send, wy_recv, ws_send, ws_recv, wa_send, wa_recv,
    wd_send, wd_recv, c_send, c_recv, gf_send, gn_send, g_recv, xf_send, xn_send, x_recv,
    core_send, core_recv, first_send, first_recv, second_send, second_recv,
):
    n_ep = x_full.shape[0]
    rows, model_width = q_ref.shape
    cap = x_out.shape[2]
    parts = x_full.shape[1]
    part_width = model_width // parts
    width = gate_hbm.shape[1]
    quarters = g_full.shape[1]
    slab = width // quarters
    half = slab // 2
    kv_heads = k_ref.shape[1] // HEAD_DIM
    group_size = model_width // k_ref.shape[1]
    block = model_width // 4
    bf16, f32 = jnp.bfloat16, jnp.float32
    grp, expert, shard = lax.axis_index("grp"), lax.axis_index("ep"), lax.axis_index("sq")
    peer = 1 - shard
    core = lax.rem(grp, 2)
    chip = grp // 2
    sibling = chip * 2 + 1 - core
    across = (1 - chip) * 2 + core
    diagonal = (1 - chip) * 2 + 1 - core
    last = n_ep - 1
    right, left = lax.rem(expert + 1, n_ep), lax.rem(expert + last, n_ep)
    upper_side = expert // 2
    inner = jnp.logical_and(expert > 0, expert < last)
    outer = jnp.logical_not(inner)
    end = 3 * upper_side
    middle = 1 + upper_side
    far_middle = 2 - upper_side
    far_end = 3 - 3 * upper_side
    far = {"ep": jnp.where(inner, far_middle, middle)}
    near = {"ep": end}
    first = jnp.where(inner, end, middle)

    def load(i, src, dst):
        return pltpu.make_async_copy(src, dst, load_sem.at[i])

    loads = [
        load(0, q_hbm, q_ref),
        load(1, k_hbm, k_ref),
        load(2, v_hbm, v_ref),
        load(3, gate_hbm, w_gate.at[shard]),
        load(4, up_hbm, w_up.at[shard]),
    ]
    grad_loads = [
        load(
            5 + 2 * q + h,
            hidden_hbm.at[:, h * width + q * slab : h * width + (q + 1) * slab],
            g_full.at[expert, q, :, h * slab : (h + 1) * slab],
        )
        for q in range(quarters)
        for h in range(2)
    ]
    for copy in grad_loads + loads:
        copy.start()

    c_buf[...] = jnp.ones_like(c_buf)
    c_buf[expert] = share_ref[...]

    @pl.when(outer)
    def _():
        for z in range(n_ep):

            @pl.when(z != expert)
            def _():
                for p in range(parts):
                    x_full[z, p, cap:rows] = jnp.zeros((rows - cap, part_width), bf16)
                for q in range(quarters):
                    g_full[z, q, cap:rows] = jnp.zeros((rows - cap, 2 * slab), bf16)

    @pl.when(shard == 0)
    def _():
        kv_buf[...] = jnp.zeros_like(kv_buf)

    barrier = pltpu.get_barrier_semaphore()
    for target in ({"sq": peer}, {"ep": right}, {"ep": left}, {"grp": sibling}, {"grp": across}):
        pl.semaphore_signal(barrier, inc=1, device_id=target, device_id_type=MESH)
    pl.semaphore_wait(barrier, 5)

    def send(src, dst, send_sem, recv_sem, target):
        return pltpu.make_async_remote_copy(
            src_ref=src, dst_ref=dst, send_sem=send_sem, recv_sem=recv_sem,
            device_id=target, device_id_type=MESH,
        )

    def kv_copy(i, kv):
        cols = slice(kv * HEAD_DIM, (kv + 1) * HEAD_DIM)
        return send((k_hbm, v_hbm)[i].at[:, cols], kv_buf.at[i, :, cols],
                    kv_send.at[i, kv], kv_recv.at[i, kv], {"sq": peer})

    weights = (w_gate, w_up)

    def rows_of(owner):
        return pl.ds(pl.multiple_of(owner * block, block), block)

    def w_across_y(i):
        mine = rows_of(grp)
        return send((gate_hbm, up_hbm)[i].at[mine], weights[i].at[shard, mine],
                    wy_send.at[i], wy_recv.at[i], {"sq": peer})

    def w_arrived_y(i):
        mine = rows_of(grp)
        return send((gate_hbm, up_hbm)[i].at[mine], weights[i].at[peer, mine],
                    wy_send.at[i], wy_recv.at[i], {"sq": peer})

    def w_on(i, owner, target, send_sem, recv_sem):
        there = weights[i].at[peer, rows_of(owner)]
        return send(there, there, send_sem.at[i], recv_sem.at[i], {"grp": target})

    def w_sibling(i, owner):
        return w_on(i, owner, sibling, ws_send, ws_recv)

    def w_across(i, owner):
        return w_on(i, owner, across, wa_send, wa_recv)

    def w_diagonal(i, owner):
        return w_on(i, owner, sibling, wd_send, wd_recv)

    def c_copy(z, slot):
        return send(c_buf.at[z], c_buf.at[z], c_send.at[slot], c_recv.at[z], far)

    def g_far(z, q, slot):
        return send(g_full.at[z, q], g_full.at[z, q], gf_send.at[slot, q], g_recv.at[z, q], far)

    def g_near(z, q, slot):
        return send(g_out.at[slot, q], g_full.at[z, q, 0:cap], gn_send.at[slot, q],
                    g_recv.at[z, q], near)

    def x_far(z, p, slot):
        return send(x_full.at[z, p], x_full.at[z, p], xf_send.at[slot, p], x_recv.at[z, p], far)

    def x_near(z, p, slot):
        return send(x_out.at[slot, p], x_full.at[z, p, 0:cap], xn_send.at[slot, p],
                    x_recv.at[z, p], near)

    @pl.when(shard == 0)
    def _():
        for kv in range(kv_heads):
            for i in range(2):
                kv_copy(i, kv).start()

    for i in range(2):
        w_across_y(i).start()

    def share_row(z, who):
        share = c_buf[z]
        here = lax.broadcasted_iota(jnp.int32, share.shape, 0) == who
        return jnp.sum(jnp.where(here, share, 0.0), axis=0, keepdims=True)

    def choose(z, slot):
        upper = (
            lax.broadcasted_iota(jnp.int32, (rows, rows), 0)
            <= lax.broadcasted_iota(jnp.int32, (rows, rows), 1)
        ).astype(f32).astype(bf16)
        places = lax.broadcasted_iota(jnp.int32, (cap, rows), 0).astype(f32)
        share = share_row(z, end)
        routed = jnp.where(share > 0.0, 1.0, 0.0)
        count = jnp.dot(
            jnp.broadcast_to(routed, (16, rows)).astype(bf16), upper, preferred_element_type=f32
        )[:1]
        key = jnp.where(share > 0.0, count - 1.0, -1.0)
        choice_ref[slot] = jnp.where(places == key, 1.0, 0.0).astype(bf16)

    def grads_near(z, which, slot):
        choice = choice_ref[slot]
        share = jnp.sum(choice.astype(f32) * share_row(z, end), axis=1, keepdims=True)
        for q in which:
            grad = jnp.dot(choice, g_full[z, q], preferred_element_type=f32)
            g_out[slot, q] = (share * grad).astype(bf16)
            g_near(z, q, slot).start()

    def tokens_near(z, p, slot):
        x_out[slot, p] = jnp.dot(
            choice_ref[slot], x_full[z, p], preferred_element_type=f32
        ).astype(bf16)
        x_near(z, p, slot).start()

    early, late = range(quarters // 2), range(quarters // 2, quarters)
    c_copy(expert, 0).start()
    for copy in grad_loads:
        copy.wait()
    for q in early:
        g_far(expert, q, 0).start()

    @pl.when(outer)
    def _():
        for q in late:
            g_far(expert, q, 0).start()

    @pl.when(inner)
    def _():
        choose(expert, 0)
        grads_near(expert, range(quarters), 0)

    for copy in loads[:3]:
        copy.wait()

    def early_grads():
        @pl.when(inner)
        def _():
            c_copy(end, 1).wait_recv()
            c_copy(end, 1).start()
            for q in early:
                g_far(end, q, 1).wait_recv()
                g_far(end, q, 1).start()
            g_far(expert, late[0], 0).start()
            c_copy(far_middle, 0).wait_recv()
            for q in early:
                g_far(far_middle, q, 0).wait_recv()
            choose(far_middle, 1)
            grads_near(far_middle, early, 1)

    contract = (((1,), (1,)), ((), ()))
    part_rows = rows // 2
    factor = LOG2E / math.sqrt(HEAD_DIM)
    hide = jnp.where(shard == 0, masked_score, 0.0)
    causal = lax.broadcasted_iota(jnp.int32, (part_rows, part_rows), 1) <= (
        lax.broadcasted_iota(jnp.int32, (part_rows, part_rows), 0)
    )
    squares = [jnp.zeros((part_rows, 1), f32)] * 2
    for kv in range(kv_heads):
        kv_cols = slice(kv * HEAD_DIM, (kv + 1) * HEAD_DIM)

        @pl.when(shard == 1)
        def _():
            for i in range(2):
                kv_copy(i, kv).wait_recv()

        if kv == 2:
            early_grads()
        for head in range(kv * group_size, (kv + 1) * group_size):
            cols = slice(head * HEAD_DIM, (head + 1) * HEAD_DIM)
            for p in range(2):
                part = slice(p * part_rows, (p + 1) * part_rows)
                q = q_ref[part, cols]

                def scored(keys):
                    return lax.dot_general(q, keys, contract, preferred_element_type=f32)

                near_scores = jnp.where(causal, scored(k_ref[part, kv_cols]), masked_score)
                pieces = [(near_scores, v_ref[part, kv_cols], 0.0)]
                if p:
                    pieces.append(
                        (scored(k_ref[:part_rows, kv_cols]), v_ref[:part_rows, kv_cols], 0.0)
                    )
                pieces.append((scored(kv_buf[0, :, kv_cols]), kv_buf[1, :, kv_cols], hide))
                top = functools.reduce(
                    jnp.maximum,
                    [jnp.max(s, axis=1, keepdims=True) * factor + away for s, _, away in pieces],
                )
                terms = [jnp.exp2(s * factor - (top - away)) for s, _, away in pieces]
                total = functools.reduce(
                    jnp.add, [jnp.sum(e, axis=1, keepdims=True) for e in terms]
                )
                out = functools.reduce(
                    jnp.add,
                    [
                        jnp.dot(e.astype(bf16), v, preferred_element_type=f32)
                        for e, (_, v, _) in zip(terms, pieces)
                    ],
                )
                out = out * (1.0 / total)
                attended[part, cols] = out
                squares[p] = squares[p] + jnp.sum(out * out, axis=1, keepdims=True)
    inverse = [lax.rsqrt(s / model_width + epsilon) for s in squares]
    for h in range(parts):
        cols = slice(h * part_width, (h + 1) * part_width)
        for p in range(2):
            part = slice(p * part_rows, (p + 1) * part_rows)
            x_full[expert, h, part] = (
                attended[part, cols] * inverse[p] * gain_ref[:, cols]
            ).astype(bf16)
        x_far(expert, h, 0).start()

    @pl.when(inner)
    def _():
        c_copy(far_end, 1).wait_recv()
        for q in early:
            g_far(far_end, q, 1).wait_recv()
        choose(far_end, 2)
        grads_near(far_end, early, 2)
        for h in range(parts):
            tokens_near(expert, h, 0)

    for i in range(2):
        loads[3 + i].wait()

    def weights_from_y(i):
        w_arrived_y(i).wait_recv()
        w_across(i, grp).start()
        w_sibling(i, grp).start()

    def weights_from_x(i):
        w_across(i, across).wait_recv()
        w_diagonal(i, across).start()

    def first_tokens(h):
        @pl.when(inner)
        def _():
            x_far(end, h, 1).wait_recv()
            x_far(end, h, 1).start()
            x_far(far_middle, h, 0).wait_recv()
            tokens_near(far_middle, h, 1)

    def second_tokens(h):
        @pl.when(inner)
        def _():
            x_far(far_end, h, 1).wait_recv()
            tokens_near(far_end, h, 2)

    def tile_of(weight, side, ab, h):
        cols = pl.ds(pl.multiple_of(ab * 2 * slab, 2 * slab), 2 * slab)
        return weight[side, h * part_width : (h + 1) * part_width, cols]

    def keep_factor(z, side, ab, pre_gate, pre_up):
        sigmoid_gate = 1.0 / (1.0 + jnp.exp(-pre_gate))
        value = pre_up * (sigmoid_gate * (1.0 + pre_gate * (1.0 - sigmoid_gate)))
        cols = pl.ds(pl.multiple_of(side * slab, slab), slab)
        for i in range(2):
            h_ref[z, 2 * ab + i, :, cols] = value[:, i * slab : (i + 1) * slab]

    def forward_side(z, side):
        @pl.loop(0, quarters // 2)
        def _(ab):
            def product(weight):
                return sum(
                    jnp.dot(x_full[z, h], tile_of(weight, side, ab, h), preferred_element_type=f32)
                    for h in range(parts)
                )

            keep_factor(z, side, ab, product(w_gate), product(w_up))

    def forward(z):
        @pl.loop(0, 2)
        def _(side):
            forward_side(z, side)

    def forward_part(z, h):
        @pl.loop(0, 4)
        def _(t):
            side, ab = t // 2, lax.rem(t, 2)
            sums = [
                jnp.dot(x_full[z, h], tile_of(weight, side, ab, h), preferred_element_type=f32)
                for weight in weights
            ]
            if h:
                sums = [pre_ref[i, t] + sums[i] for i in range(2)]
            if h < parts - 1:
                for i in range(2):
                    pre_ref[i, t] = sums[i]
            else:
                keep_factor(z, side, ab, *sums)

    diag = lax.broadcasted_iota(jnp.int32, (rows, rows), 0) == lax.broadcasted_iota(
        jnp.int32, (rows, rows), 1
    )

    def products(z, which, fresh):
        share = jnp.sum(jnp.where(diag, share_row(z, expert), 0.0), axis=1, keepdims=True)
        high = 2 * slab * len(which)
        at = slice(2 * slab * which[0], 2 * slab * which[0] + high)
        for i, q in enumerate(which):
            cotangent = (share * g_full[z, q].astype(f32)).astype(bf16).astype(f32)
            delta_ref[2 * slab * i : 2 * slab * (i + 1)] = (cotangent * h_ref[z, q]).T.astype(bf16)

        @pl.loop(0, parts)
        def _(h):
            cols = pl.ds(pl.multiple_of(h * part_width, part_width), part_width)
            term = jnp.dot(delta_ref[:high], x_full[z, h], preferred_element_type=f32)
            if fresh:
                acc[at, cols] = term
            else:
                acc[at, cols] += term

    def grads_here(z, which, slot):
        @pl.when(outer)
        def _():
            for q in which:
                g_near(z, q, slot).wait_recv()

    def tokens_here(z, slot, which):
        @pl.when(outer)
        def _():
            for h in which:
                x_near(z, h, slot).wait_recv()

    forward_side(expert, shard)
    first_tokens(0)
    weights_from_y(0)
    first_tokens(1)
    weights_from_y(1)
    first_tokens(2)
    weights_from_x(0)
    first_tokens(3)

    @pl.when(inner)
    def _():
        g_far(expert, late[1], 0).start()
        for q in late:
            g_far(end, q, 1).wait_recv()
            g_far(end, q, 1).start()

    weights_from_x(1)
    for i in range(2):
        w_sibling(i, sibling).wait_recv()
        w_diagonal(i, diagonal).wait_recv()

    forward_side(expert, peer)
    second_tokens(0)
    products(expert, early, True)
    products(expert, late, True)
    tokens_here(first, 0, range(parts))
    forward(first)
    second_tokens(1)
    grads_here(first, early, 0)
    products(first, early, False)
    tokens_here(far_middle, 1, range(parts))
    second_tokens(2)
    forward(far_middle)
    grads_here(far_middle, early, 1)
    products(far_middle, early, False)
    grads_here(first, late, 0)
    products(first, late, False)
    second_tokens(3)

    @pl.when(inner)
    def _():
        g_far(far_middle, late[0], 0).wait_recv()
        grads_near(far_middle, late[:1], 1)

    for h in range(parts):
        tokens_here(far_end, 2, [h])
        forward_part(far_end, h)
    grads_here(far_end, early, 2)
    products(far_end, early, False)

    def block_of(c):
        return pl.ds(pl.multiple_of(c * block, block), block)

    def to_core(q, t):
        return send(stage.at[q, t], from_core.at[q, t], core_send.at[q, t],
                    core_recv.at[q, t], {"grp": sibling})

    def first_copy(q, t):
        src, dst, target = (
            (x_stage, x_first, {"grp": across}),
            (y_stage, y_first, {"sq": peer}),
        )[t]
        return send(src.at[q, 0], dst.at[q], first_send.at[q, t], first_recv.at[q, t], target)

    def second_copy(q, t, i):
        src, dst, target = (
            (x_stage, x_second, {"grp": across}),
            (y_stage, y_second, {"sq": peer}),
        )[t]
        return send(src.at[q, 1 + i], dst.at[q, i], second_send.at[q, t, i],
                    second_recv.at[q, t, i], target)

    def reduce_start(q):
        at = slice(2 * slab * q, 2 * slab * (q + 1))
        for t, owner in enumerate((diagonal, sibling)):
            stage[q, t] = acc[at, block_of(owner)].astype(bf16)
            to_core(q, t).start()

    def chip_sum(q, t, owner, side):
        here = pl.ds(pl.multiple_of(2 * slab * q + side * slab, slab), slab)
        there = pl.ds(pl.multiple_of(side * slab, slab), slab)
        return acc[here, block_of(owner)] + from_core[q, t, there].astype(f32)

    def reduce_first(q):
        to_core(q, 0).wait_recv()
        both = chip_sum(q, 0, across, peer).astype(bf16)
        x_stage[q, 0] = both[:half]
        y_stage[q, 0] = both[half:]
        for t in range(2):
            first_copy(q, t).start()
        x_side = chip_sum(q, 0, across, shard)
        x_stage[q, 1] = x_side[:half].astype(bf16)
        second_copy(q, 0, 0).start()
        x_rest[q] = x_side[half:]
        to_core(q, 1).wait_recv()
        y_side = chip_sum(q, 1, grp, peer)
        y_stage[q, 1] = y_side[half:].astype(bf16)
        second_copy(q, 1, 0).start()
        y_rest[q] = y_side[:half]
        own_block[q] = chip_sum(q, 1, grp, shard)

    def reduce_second(q):
        first_copy(q, 1).wait_recv()
        x_stage[q, 2] = (x_rest[q] + y_first[q].astype(f32)).astype(bf16)
        second_copy(q, 0, 1).start()
        first_copy(q, 0).wait_recv()
        y_stage[q, 2] = (y_rest[q] + x_first[q].astype(f32)).astype(bf16)
        second_copy(q, 1, 1).start()

    def reduce_end(q):
        for t in range(2):
            for i in range(2):
                second_copy(q, t, i).wait_recv()
        own_block[q, :half] += x_second[q, 0].astype(f32) + y_second[q, 1].astype(f32)
        own_block[q, half:] += x_second[q, 1].astype(f32) + y_second[q, 0].astype(f32)
        out_ref[:, q * slab : (q + 1) * slab] = own_block[q].T

    for q in early:
        reduce_start(q)

    @pl.when(inner)
    def _():
        g_far(far_end, late[0], 1).wait_recv()
        grads_near(far_end, late[:1], 2)
        g_far(far_middle, late[1], 0).wait_recv()
        grads_near(far_middle, late[1:], 1)
        g_far(far_end, late[1], 1).wait_recv()
        grads_near(far_end, late[1:], 2)

    for q in early:
        reduce_first(q)
    for q in early:
        reduce_second(q)
    for q in late:
        grads_here(far_middle, [q], 1)
        products(far_middle, [q], False)
        grads_here(far_end, [q], 2)
        products(far_end, [q], False)
        reduce_start(q)
        if q > late[0]:
            reduce_second(late[0])
        reduce_first(q)
    for q in early:
        reduce_end(q)
    reduce_second(late[1])
    for q in late:
        reduce_end(q)

    @pl.when(shard == 0)
    def _():
        for kv in range(kv_heads):
            for i in range(2):
                kv_copy(i, kv).wait_send()

    for i in range(2):
        w_across_y(i).wait_send()
        w_sibling(i, grp).wait_send()
        w_across(i, grp).wait_send()
        w_diagonal(i, across).wait_send()
    c_copy(expert, 0).wait_send()
    for q in range(quarters):
        g_far(expert, q, 0).wait_send()
    for h in range(parts):
        x_far(expert, h, 0).wait_send()

    @pl.when(inner)
    def _():
        c_copy(end, 1).wait_send()
        for q in range(quarters):
            g_far(end, q, 1).wait_send()
        for h in range(parts):
            x_far(end, h, 1).wait_send()
        for slot, z in enumerate((expert, far_middle, far_end)):
            for q in range(quarters):
                g_near(z, q, slot).wait_send()
            for h in range(parts):
                x_near(z, h, slot).wait_send()

    for q in range(quarters):
        for t in range(2):
            to_core(q, t).wait_send()
            first_copy(q, t).wait_send()
            for i in range(2):
                second_copy(q, t, i).wait_send()


def fused(
    queries, keys, values, norm_gain, expert_ids, gate_values, hidden_grad, gate_weight, up_weight
):
    rows, model_width = queries.shape
    n_ep = lax.axis_size("ep")
    width = gate_weight.shape[2]
    kv_width = keys.shape[1]
    kv_heads = kv_width // HEAD_DIM
    block = model_width // 4
    parts = 4
    part_width = model_width // parts
    quarters = 4
    slab = width // quarters
    half = slab // 2
    cap = rows * expert_ids.shape[1] // n_ep * 3 // 2
    chosen = expert_ids.T[:, None, :] == jnp.arange(8, dtype=jnp.int32)[:, None]
    share = jnp.sum(jnp.where(chosen, gate_values.T[:, None, :], 0.0), axis=0)
    vmem = pl.BlockSpec(memory_space=pltpu.VMEM)
    hbm = pl.BlockSpec(memory_space=pltpu.HBM)
    dma = pltpu.SemaphoreType.DMA
    bf16, f32 = jnp.bfloat16, jnp.float32
    out = pl.pallas_call(
        whole_kernel,
        out_shape=jax.ShapeDtypeStruct((block, width), f32),
        in_specs=[hbm] * 3 + [vmem] * 2 + [hbm] * 3,
        out_specs=vmem,
        scratch_shapes=[
            pltpu.VMEM((rows, model_width), bf16),
            pltpu.VMEM((rows, kv_width), bf16),
            pltpu.VMEM((rows, kv_width), bf16),
            pltpu.VMEM((2, rows, kv_width), bf16),
            pltpu.VMEM((rows, model_width), f32),
            pltpu.VMEM((n_ep, parts, rows, part_width), bf16),
            pltpu.VMEM((3, parts, cap, part_width), bf16),
            pltpu.VMEM((n_ep, quarters, rows, 2 * slab), bf16),
            pltpu.VMEM((3, quarters, cap, 2 * slab), bf16),
            pltpu.VMEM((n_ep, 8, rows), f32),
            pltpu.VMEM((3, cap, rows), bf16),
            pltpu.VMEM((2, model_width, width), bf16),
            pltpu.VMEM((2, model_width, width), bf16),
            pltpu.VMEM((n_ep, quarters, rows, 2 * slab), f32),
            pltpu.VMEM((2, quarters, rows, 2 * slab), f32),
            pltpu.VMEM((width, rows), bf16),
            pltpu.VMEM((2 * width, model_width), f32),
            pltpu.VMEM((quarters, 2, 2 * slab, block), bf16),
            pltpu.VMEM((quarters, 2, 2 * slab, block), bf16),
            pltpu.VMEM((quarters, 3, half, block), bf16),
            pltpu.VMEM((quarters, 3, half, block), bf16),
            pltpu.VMEM((quarters, slab, block), f32),
            pltpu.VMEM((quarters, half, block), f32),
            pltpu.VMEM((quarters, half, block), f32),
            pltpu.VMEM((quarters, half, block), bf16),
            pltpu.VMEM((quarters, half, block), bf16),
            pltpu.VMEM((quarters, 2, half, block), bf16),
            pltpu.VMEM((quarters, 2, half, block), bf16),
            dma((5 + 2 * quarters,)), dma((2, kv_heads)), dma((2, kv_heads)),
            dma((2,)), dma((2,)), dma((2,)), dma((2,)), dma((2,)), dma((2,)), dma((2,)), dma((2,)),
            dma((2,)), dma((n_ep,)), dma((2, quarters)), dma((3, quarters)), dma((n_ep, quarters)),
            dma((2, parts)), dma((3, parts)), dma((n_ep, parts)),
            dma((quarters, 2)), dma((quarters, 2)), dma((quarters, 2)), dma((quarters, 2)),
            dma((quarters, 2, 2)), dma((quarters, 2, 2)),
        ],
        compiler_params=pltpu.CompilerParams(
            collective_id=0, has_side_effects=True, vmem_limit_bytes=56 << 20
        ),
    )(
        queries, keys, values, norm_gain.reshape(1, -1), share, hidden_grad,
        gate_weight[0], up_weight[0],
    )
    return out[None]


def solution(mesh):
    small = mesh.shape["grp"] == 4 and mesh.shape["sq"] == 2 and mesh.shape["ep"] == 4
    return jax.shard_map(
        fused if small else body,
        mesh=mesh,
        in_specs=(
            P(("grp", "ep", "sq"), None),
            P(("grp", "ep", "sq"), None),
            P(("grp", "ep", "sq"), None),
            P(),
            P(("grp", "ep", "sq"), None),
            P(("grp", "ep", "sq"), None),
            P(("grp", "ep", "sq"), None),
            P("ep", None, "sq"),
            P("ep", None, "sq"),
        ),
        out_specs=P("ep", "grp", "sq"),
        check_vma=False,
    )
```

```python
import functools
import math

import jax
import jax.numpy as jnp
from jax import lax
from jax.experimental import pallas as pl
from jax.experimental.pallas import tpu as pltpu
from jax.sharding import PartitionSpec as P

HEAD_DIM = 128

epsilon = 1e-05
masked_score = -1e30
LOG2E = 1.4426950408889634
MESH = pl.DeviceIdType.MESH


def attention_kernel(group_size, shard_ref, q_ref, ko_ref, vo_ref, kp_ref, vp_ref, gain_ref, out_ref, acc_ref):
    rows, model_width = q_ref.shape
    past = kp_ref.shape[0]
    scale = 1.0 / math.sqrt(HEAD_DIM)
    shard = shard_ref[0]
    contract = (((1,), (1,)), ((), ()))
    causal = lax.broadcasted_iota(jnp.int32, (rows, rows), 1) <= lax.broadcasted_iota(
        jnp.int32, (rows, rows), 0
    )
    seen = lax.broadcasted_iota(jnp.int32, (rows, past), 1) < shard * rows
    squares = jnp.zeros((rows, 1), jnp.float32)
    for head in range(model_width // HEAD_DIM):
        cols = slice(head * HEAD_DIM, (head + 1) * HEAD_DIM)
        kv = head // group_size
        kv_cols = slice(kv * HEAD_DIM, (kv + 1) * HEAD_DIM)
        q = q_ref[:, cols]
        own = lax.dot_general(q, ko_ref[:, kv_cols], contract, preferred_element_type=jnp.float32)
        old = lax.dot_general(q, kp_ref[:, kv_cols], contract, preferred_element_type=jnp.float32)
        own = jnp.where(causal, own * scale, masked_score)
        old = jnp.where(seen, old * scale, masked_score)
        top = jnp.maximum(
            jnp.max(own, axis=1, keepdims=True), jnp.max(old, axis=1, keepdims=True)
        )
        own = jnp.exp(own - top)
        old = jnp.exp(old - top)
        total = jnp.sum(own, axis=1, keepdims=True) + jnp.sum(old, axis=1, keepdims=True)
        out = jnp.dot(
            own.astype(jnp.bfloat16), vo_ref[:, kv_cols], preferred_element_type=jnp.float32
        ) + jnp.dot(
            old.astype(jnp.bfloat16), vp_ref[:, kv_cols], preferred_element_type=jnp.float32
        )
        out = out / total
        acc_ref[:, cols] = out
        squares = squares + jnp.sum(out * out, axis=1, keepdims=True)
    inverse = lax.rsqrt(squares / model_width + epsilon)
    out_ref[...] = (acc_ref[...] * inverse * gain_ref[...]).astype(jnp.bfloat16)


def attend(shard, queries, keys, values, past_keys, past_values, norm_gain):
    rows, model_width = queries.shape
    group_size = model_width // keys.shape[1]
    vmem = pl.BlockSpec(memory_space=pltpu.VMEM)
    return pl.pallas_call(
        functools.partial(attention_kernel, group_size),
        out_shape=jax.ShapeDtypeStruct((rows, model_width), jnp.bfloat16),
        in_specs=[pl.BlockSpec(memory_space=pltpu.SMEM)] + [vmem] * 6,
        out_specs=vmem,
        scratch_shapes=[pltpu.VMEM((rows, model_width), jnp.float32)],
        compiler_params=pltpu.CompilerParams(vmem_limit_bytes=32 << 20),
        cost_estimate=pl.CostEstimate(
            flops=4 * rows * model_width * (rows + past_keys.shape[0]),
            bytes_accessed=4 * rows * model_width,
            transcendentals=rows * (model_width // HEAD_DIM) * (rows + past_keys.shape[0]),
        ),
    )(shard.reshape(1), queries, keys, values, past_keys, past_values, norm_gain.reshape(1, -1))


def ring(size, shift):
    return [(i, (i + shift) % size) for i in range(size)]


def body(
    queries, keys, values, norm_gain, expert_ids, gate_values, hidden_grad, gate_weight, up_weight
):
    rows, model_width = queries.shape
    n_ep = lax.axis_size("ep")
    n_sq = lax.axis_size("sq")
    shard = lax.axis_index("sq")
    expert = lax.axis_index("ep")
    weight_gate = gate_weight[0]
    weight_up = up_weight[0]
    width = weight_gate.shape[1]
    kv_width = keys.shape[1]

    both = jnp.concatenate([keys, values], axis=1)
    past = []
    for j in range(1, n_sq):
        past.append(lax.ppermute(both, "sq", [(i, i + j) for i in range(n_sq - j)]))
    past = jnp.concatenate(past, axis=0)

    def columns_of(owner):
        return lax.dynamic_slice_in_dim(hidden_grad, owner * width, width, 1)

    grads = [columns_of(shard)]
    for j in range(1, n_sq):
        grads.append(lax.ppermute(columns_of((shard + j) % n_sq), "sq", ring(n_sq, j)))
    grad = jnp.concatenate(grads, axis=0)

    chosen = expert_ids[:, :, None] == jnp.arange(n_ep, dtype=jnp.int32)
    share = jnp.sum(jnp.where(chosen, gate_values[:, :, None], 0.0), axis=1).T
    shares = lax.all_gather(share, ("ep", "sq"), axis=0, tiled=False)
    shares = lax.dynamic_index_in_dim(shares, expert, 1, keepdims=False).reshape(n_ep, n_sq, rows)
    shares = jnp.concatenate(
        [
            lax.dynamic_index_in_dim(shares, (shard - j) % n_sq, 1, keepdims=False)
            for j in range(n_sq)
        ],
        axis=1,
    )

    normed = attend(
        shard, queries, keys, values, past[:, :kv_width], past[:, kv_width:], norm_gain
    )

    def add_chunk(step, tokens, grad, summed):
        source = (expert - step) % n_ep
        share_here = lax.dynamic_index_in_dim(shares, source, 0, keepdims=False)
        pieces = [tokens]
        for j in range(1, n_sq):
            pieces.append(lax.ppermute(tokens, "sq", ring(n_sq, j)))
        for j, inputs in enumerate(pieces):
            part = slice(j * rows, (j + 1) * rows)
            cotangent = (share_here[part, None] * grad[part].astype(jnp.float32)).astype(
                jnp.bfloat16
            )
            pre_gate = jnp.dot(inputs, weight_gate, preferred_element_type=jnp.float32)
            pre_up = jnp.dot(inputs, weight_up, preferred_element_type=jnp.float32)
            sigmoid_gate = jax.nn.sigmoid(pre_gate)
            slope = sigmoid_gate * (1.0 + pre_gate * (1.0 - sigmoid_gate))
            delta = (cotangent.astype(jnp.float32) * pre_up * slope).astype(jnp.bfloat16)
            term = lax.dot_general(
                inputs, delta, (((0,), (0,)), ((), ())), preferred_element_type=jnp.float32
            )
            summed = term if summed is None else summed + term
        return summed

    def turn(tokens, grad):
        return lax.ppermute(tokens, "ep", ring(n_ep, 1)), lax.ppermute(grad, "ep", ring(n_ep, 1))

    if n_ep <= 8:
        summed = None
        tokens = normed
        for step in range(n_ep):
            if step < n_ep - 1:
                turned = turn(tokens, grad)
            summed = add_chunk(step, tokens, grad, summed)
            if step < n_ep - 1:
                tokens, grad = turned
    else:

        def one_step(step, carried):
            tokens, grad, summed = carried
            turned = turn(tokens, grad)
            return (*turned, add_chunk(step, tokens, grad, summed))

        start = jnp.zeros((model_width, width), jnp.float32)
        summed = lax.fori_loop(0, n_ep, one_step, (normed, grad, start))[2]
    return lax.psum_scatter(
        summed[None].astype(jnp.bfloat16), "grp", scatter_dimension=1, tiled=True
    ).astype(jnp.float32)


def whole_kernel(
    q_hbm, k_hbm, v_hbm, gain_ref, ids_ref, values_ref, hidden_hbm, gate_hbm, up_hbm, out_ref,
    q_ref, k_ref, v_ref, kv_buf, attended, x_full, x_out, g_full, g_out, c_buf, choice_ref,
    w_gate, w_up, h_ref, pre_ref, delta_ref, acc, stage, from_core, x_stage, y_stage, own_block,
    x_rest, y_rest, share_ref,
    x_first, y_first, x_second, y_second,
    load_sem, kv_send, kv_recv, wy_send, wy_recv, ws_send, ws_recv, wa_send, wa_recv,
    wd_send, wd_recv, c_send, c_recv, gf_send, gn_send, g_recv, xf_send, xn_send, x_recv,
    core_send, core_recv, first_send, first_recv, second_send, second_recv,
):
    n_ep = x_full.shape[0]
    rows, model_width = q_ref.shape
    cap = x_out.shape[2]
    parts = x_full.shape[1]
    part_width = model_width // parts
    width = gate_hbm.shape[1]
    quarters = g_full.shape[1]
    slab = width // quarters
    half = slab // 2
    kv_heads = k_ref.shape[1] // HEAD_DIM
    group_size = model_width // k_ref.shape[1]
    block = model_width // 4
    bf16, f32 = jnp.bfloat16, jnp.float32
    grp, expert, shard = lax.axis_index("grp"), lax.axis_index("ep"), lax.axis_index("sq")
    peer = 1 - shard
    core = lax.rem(grp, 2)
    chip = grp // 2
    sibling = chip * 2 + 1 - core
    across = (1 - chip) * 2 + core
    diagonal = (1 - chip) * 2 + 1 - core
    last = n_ep - 1
    right, left = lax.rem(expert + 1, n_ep), lax.rem(expert + last, n_ep)
    upper_side = expert // 2
    inner = jnp.logical_and(expert > 0, expert < last)
    outer = jnp.logical_not(inner)
    end = 3 * upper_side
    middle = 1 + upper_side
    far_middle = 2 - upper_side
    far_end = 3 - 3 * upper_side
    far = {"ep": jnp.where(inner, far_middle, middle)}
    near = {"ep": end}
    first = jnp.where(inner, end, middle)

    def load(i, src, dst):
        return pltpu.make_async_copy(src, dst, load_sem.at[i])

    loads = [
        load(0, q_hbm, q_ref),
        load(1, k_hbm, k_ref),
        load(2, v_hbm, v_ref),
        load(3, gate_hbm, w_gate.at[shard]),
        load(4, up_hbm, w_up.at[shard]),
    ]
    grad_loads = [
        load(
            5 + 2 * q + h,
            hidden_hbm.at[:, h * width + q * slab : h * width + (q + 1) * slab],
            g_full.at[expert, q, :, h * slab : (h + 1) * slab],
        )
        for q in range(quarters)
        for h in range(2)
    ]
    for copy in grad_loads + loads:
        copy.start()

    c_buf[...] = jnp.ones_like(c_buf)
    names = lax.broadcasted_iota(jnp.int32, c_buf.shape[1:], 0)
    c_buf[expert] = sum(
        jnp.where(names == ids_ref[k : k + 1], values_ref[k : k + 1], 0.0)
        for k in range(ids_ref.shape[0])
    )

    @pl.when(outer)
    def _():
        for z in range(n_ep):

            @pl.when(z != expert)
            def _():
                for p in range(parts):
                    x_full[z, p, cap:rows] = jnp.zeros((rows - cap, part_width), bf16)
                for q in range(quarters):
                    g_full[z, q, cap:rows] = jnp.zeros((rows - cap, 2 * slab), bf16)

    @pl.when(shard == 0)
    def _():
        kv_buf[...] = jnp.zeros_like(kv_buf)

    barrier = pltpu.get_barrier_semaphore()
    for target in ({"sq": peer}, {"ep": right}, {"ep": left}, {"grp": sibling}, {"grp": across}):
        pl.semaphore_signal(barrier, inc=1, device_id=target, device_id_type=MESH)
    pl.semaphore_wait(barrier, 5)

    def send(src, dst, send_sem, recv_sem, target):
        return pltpu.make_async_remote_copy(
            src_ref=src, dst_ref=dst, send_sem=send_sem, recv_sem=recv_sem,
            device_id=target, device_id_type=MESH,
        )

    def kv_copy(i, kv):
        cols = slice(kv * HEAD_DIM, (kv + 1) * HEAD_DIM)
        return send((k_hbm, v_hbm)[i].at[:, cols], kv_buf.at[i, :, cols],
                    kv_send.at[i, kv], kv_recv.at[i, kv], {"sq": peer})

    weights = (w_gate, w_up)

    pieces_of = 2 * 2
    piece = block // 2

    def rows_of(w, owner):
        return pl.ds(pl.multiple_of(owner * block + w // 2 * piece, piece), piece)

    def w_over_y(w, half_of):
        mine = rows_of(w, grp)
        return send((gate_hbm, up_hbm)[w % 2].at[mine], weights[w % 2].at[half_of, mine],
                    wy_send.at[w], wy_recv.at[w], {"sq": peer})

    def w_on(w, owner, target, send_sem, recv_sem):
        there = weights[w % 2].at[peer, rows_of(w, owner)]
        return send(there, there, send_sem.at[w], recv_sem.at[w], {"grp": target})

    def w_sibling(w, owner):
        return w_on(w, owner, sibling, ws_send, ws_recv)

    def w_across(w, owner):
        return w_on(w, owner, across, wa_send, wa_recv)

    def w_diagonal(w, owner):
        return w_on(w, owner, sibling, wd_send, wd_recv)

    def c_copy(z, slot):
        return send(c_buf.at[z], c_buf.at[z], c_send.at[slot], c_recv.at[z], far)

    def g_far(z, q, slot):
        return send(g_full.at[z, q], g_full.at[z, q], gf_send.at[slot, q], g_recv.at[z, q], far)

    def g_near(z, q, slot):
        return send(g_out.at[slot, q], g_full.at[z, q, 0:cap], gn_send.at[slot, q],
                    g_recv.at[z, q], near)

    def x_far(z, p, slot):
        return send(x_full.at[z, p], x_full.at[z, p], xf_send.at[slot, p], x_recv.at[z, p], far)

    def x_near(z, p, slot):
        return send(x_out.at[slot, p], x_full.at[z, p, 0:cap], xn_send.at[slot, p],
                    x_recv.at[z, p], near)

    @pl.when(shard == 0)
    def _():
        for kv in range(kv_heads):
            for i in range(2):
                kv_copy(i, kv).start()

    for w in range(pieces_of):
        w_over_y(w, shard).start()

    def share_row(z, who):
        share = c_buf[z]
        here = lax.broadcasted_iota(jnp.int32, share.shape, 0) == who
        return jnp.sum(jnp.where(here, share, 0.0), axis=0, keepdims=True)

    def choose(z, slot):
        upper = (
            lax.broadcasted_iota(jnp.int32, (rows, rows), 0)
            <= lax.broadcasted_iota(jnp.int32, (rows, rows), 1)
        ).astype(f32).astype(bf16)
        places = lax.broadcasted_iota(jnp.int32, (cap, rows), 0).astype(f32)
        share = share_row(z, end)
        routed = jnp.where(share > 0.0, 1.0, 0.0)
        count = jnp.dot(
            jnp.broadcast_to(routed, (16, rows)).astype(bf16), upper, preferred_element_type=f32
        )[:1]
        key = jnp.where(share > 0.0, count - 1.0, -1.0)
        choice_ref[slot] = jnp.where(places == key, 1.0, 0.0).astype(bf16)

    def grads_near(z, which, slot):
        choice = choice_ref[slot]
        share = jnp.sum(choice.astype(f32) * share_row(z, end), axis=1, keepdims=True)
        for q in which:
            grad = jnp.dot(choice, g_full[z, q], preferred_element_type=f32)
            g_out[slot, q] = (share * grad).astype(bf16)
            g_near(z, q, slot).start()

    def tokens_near(z, p, slot):
        x_out[slot, p] = jnp.dot(
            choice_ref[slot], x_full[z, p], preferred_element_type=f32
        ).astype(bf16)
        x_near(z, p, slot).start()

    early, late = range(quarters // 2), range(quarters // 2, quarters)
    c_copy(expert, 0).start()
    for copy in grad_loads:
        copy.wait()
    for q in early:
        g_far(expert, q, 0).start()

    @pl.when(outer)
    def _():
        for q in late:
            g_far(expert, q, 0).start()

    @pl.when(inner)
    def _():
        choose(expert, 0)
        grads_near(expert, range(quarters), 0)

    for copy in loads[:3]:
        copy.wait()

    def early_grads():
        @pl.when(inner)
        def _():
            c_copy(end, 1).wait_recv()
            c_copy(end, 1).start()
            for q in early:
                g_far(end, q, 1).wait_recv()
                g_far(end, q, 1).start()
            g_far(expert, late[0], 0).start()
            c_copy(far_middle, 0).wait_recv()
            for q in early:
                g_far(far_middle, q, 0).wait_recv()
            choose(far_middle, 1)
            grads_near(far_middle, early, 1)

    contract = (((1,), (1,)), ((), ()))
    part_rows = rows // 2
    factor = LOG2E / math.sqrt(HEAD_DIM)
    hide = jnp.where(shard == 0, masked_score, 0.0)
    causal = lax.broadcasted_iota(jnp.int32, (part_rows, part_rows), 1) <= (
        lax.broadcasted_iota(jnp.int32, (part_rows, part_rows), 0)
    )
    squares = [jnp.zeros((part_rows, 1), f32)] * 2
    for kv in range(kv_heads):
        kv_cols = slice(kv * HEAD_DIM, (kv + 1) * HEAD_DIM)

        @pl.when(shard == 1)
        def _():
            for i in range(2):
                kv_copy(i, kv).wait_recv()

        if kv == 2:
            early_grads()
        for head in range(kv * group_size, (kv + 1) * group_size):
            cols = slice(head * HEAD_DIM, (head + 1) * HEAD_DIM)
            for p in range(2):
                part = slice(p * part_rows, (p + 1) * part_rows)
                q = q_ref[part, cols]

                def scored(keys):
                    return lax.dot_general(q, keys, contract, preferred_element_type=f32)

                near_scores = jnp.where(causal, scored(k_ref[part, kv_cols]), masked_score)
                pieces = [(near_scores, v_ref[part, kv_cols], 0.0)]
                if p:
                    pieces.append(
                        (scored(k_ref[:part_rows, kv_cols]), v_ref[:part_rows, kv_cols], 0.0)
                    )
                pieces.append((scored(kv_buf[0, :, kv_cols]), kv_buf[1, :, kv_cols], hide))
                top = functools.reduce(
                    jnp.maximum,
                    [jnp.max(s, axis=1, keepdims=True) * factor + away for s, _, away in pieces],
                )
                terms = [jnp.exp2(s * factor - (top - away)) for s, _, away in pieces]
                total = functools.reduce(
                    jnp.add, [jnp.sum(e, axis=1, keepdims=True) for e in terms]
                )
                out = functools.reduce(
                    jnp.add,
                    [
                        jnp.dot(e.astype(bf16), v, preferred_element_type=f32)
                        for e, (_, v, _) in zip(terms, pieces)
                    ],
                )
                out = out * (1.0 / total)
                attended[part, cols] = out
                squares[p] = squares[p] + jnp.sum(out * out, axis=1, keepdims=True)
    inverse = [lax.rsqrt(s / model_width + epsilon) for s in squares]
    for h in range(parts):
        cols = slice(h * part_width, (h + 1) * part_width)
        for p in range(2):
            part = slice(p * part_rows, (p + 1) * part_rows)
            x_full[expert, h, part] = (
                attended[part, cols] * inverse[p] * gain_ref[:, cols]
            ).astype(bf16)
        x_far(expert, h, 0).start()

    @pl.when(inner)
    def _():
        for h in range(parts):
            tokens_near(expert, h, 0)

    for i in range(2):
        loads[3 + i].wait()

    def weights_from_y(w):
        w_over_y(w, peer).wait_recv()
        w_across(w, grp).start()
        w_sibling(w, grp).start()

    def weights_from_x(w):
        w_across(w, across).wait_recv()
        w_diagonal(w, across).start()

    def first_tokens(h):
        @pl.when(inner)
        def _():
            x_far(end, h, 1).wait_recv()
            x_far(end, h, 1).start()
            x_far(far_middle, h, 0).wait_recv()
            tokens_near(far_middle, h, 1)

    def second_tokens(h):
        @pl.when(inner)
        def _():
            if h == 0:
                c_copy(far_end, 1).wait_recv()
                choose(far_end, 2)
            x_far(far_end, h, 1).wait_recv()
            tokens_near(far_end, h, 2)
            if h == parts - 1:
                for q in early:
                    g_far(far_end, q, 1).wait_recv()
                grads_near(far_end, early, 2)
                g_far(far_middle, late[0], 0).wait_recv()
                grads_near(far_middle, late[:1], 1)

    def tile_of(weight, side, ab, h):
        cols = pl.ds(pl.multiple_of(ab * 2 * slab, 2 * slab), 2 * slab)
        return weight[side, h * part_width : (h + 1) * part_width, cols]

    def keep_factor(z, side, ab, pre_gate, pre_up):
        sigmoid_gate = 0.5 * jnp.tanh(0.5 * pre_gate) + 0.5
        value = pre_up * (sigmoid_gate * (1.0 + pre_gate * (1.0 - sigmoid_gate)))
        cols = pl.ds(pl.multiple_of(side * slab, slab), slab)
        for i in range(2):
            h_ref[z, 2 * ab + i, :, cols] = value[:, i * slab : (i + 1) * slab]

    def forward_side(z, side):
        @pl.loop(0, quarters // 2)
        def _(ab):
            def product(weight):
                return sum(
                    jnp.dot(x_full[z, h], tile_of(weight, side, ab, h), preferred_element_type=f32)
                    for h in range(parts)
                )

            keep_factor(z, side, ab, product(w_gate), product(w_up))

    def forward(z):
        @pl.loop(0, 2)
        def _(side):
            forward_side(z, side)

    def forward_part(z, h):
        @pl.loop(0, 4)
        def _(t):
            side, ab = t // 2, lax.rem(t, 2)
            sums = [
                jnp.dot(x_full[z, h], tile_of(weight, side, ab, h), preferred_element_type=f32)
                for weight in weights
            ]
            if h:
                sums = [pre_ref[i, t] + sums[i] for i in range(2)]
            if h < parts - 1:
                for i in range(2):
                    pre_ref[i, t] = sums[i]
            else:
                keep_factor(z, side, ab, *sums)

    diag = lax.broadcasted_iota(jnp.int32, (rows, rows), 0) == lax.broadcasted_iota(
        jnp.int32, (rows, rows), 1
    )

    def share_column(z):
        share = jnp.sum(jnp.where(diag, share_row(z, expert), 0.0), axis=1, keepdims=True)
        share_ref[z] = jnp.broadcast_to(share, (rows, 2 * slab))

    def products(z, which, fresh):
        high = 2 * slab * len(which)
        at = slice(2 * slab * which[0], 2 * slab * which[0] + high)
        for i, q in enumerate(which):
            cotangent = (share_ref[z] * g_full[z, q].astype(f32)).astype(bf16).astype(f32)
            delta_ref[2 * slab * i : 2 * slab * (i + 1)] = (cotangent * h_ref[z, q]).T.astype(bf16)
        for h in range(parts):
            cols = slice(h * part_width, (h + 1) * part_width)
            term = jnp.dot(delta_ref[:high], x_full[z, h], preferred_element_type=f32)
            if fresh:
                acc[at, cols] = term
            else:
                acc[at, cols] += term

    def grads_here(z, which, slot):
        @pl.when(outer)
        def _():
            for q in which:
                g_near(z, q, slot).wait_recv()

    def tokens_here(z, slot, which):
        @pl.when(outer)
        def _():
            for h in which:
                x_near(z, h, slot).wait_recv()

    share_column(expert)
    forward_side(expert, shard)
    weights_from_y(0)
    first_tokens(0)
    weights_from_y(1)
    weights_from_x(0)
    first_tokens(1)
    weights_from_y(2)
    weights_from_x(1)
    first_tokens(2)
    weights_from_y(3)
    weights_from_x(2)
    first_tokens(3)

    @pl.when(inner)
    def _():
        g_far(end, late[0], 1).wait_recv()
        g_far(end, late[0], 1).start()
        g_far(expert, late[1], 0).start()
        g_far(end, late[1], 1).wait_recv()
        g_far(end, late[1], 1).start()

    weights_from_x(3)
    for w in range(pieces_of):
        w_sibling(w, sibling).wait_recv()
        w_diagonal(w, diagonal).wait_recv()

    forward_side(expert, peer)
    second_tokens(0)
    products(expert, early, True)
    products(expert, late, True)
    tokens_here(first, 0, range(parts))
    share_column(first)
    forward(first)
    second_tokens(1)
    grads_here(first, early, 0)
    products(first, early, False)
    tokens_here(far_middle, 1, range(parts))
    second_tokens(2)
    share_column(far_middle)
    forward(far_middle)
    grads_here(far_middle, early, 1)
    products(far_middle, early, False)
    grads_here(first, late, 0)
    products(first, late, False)
    second_tokens(3)

    share_column(far_end)
    for h in range(parts):
        tokens_here(far_end, 2, [h])
        forward_part(far_end, h)

    def block_of(c):
        return pl.ds(pl.multiple_of(c * block, block), block)

    def to_core(q, t):
        return send(stage.at[q, t], from_core.at[q, t], core_send.at[q, t],
                    core_recv.at[q, t], {"grp": sibling})

    def first_copy(q, t):
        src, dst, target = (
            (x_stage, x_first, {"grp": across}),
            (y_stage, y_first, {"sq": peer}),
        )[t]
        return send(src.at[q, 0], dst.at[q], first_send.at[q, t], first_recv.at[q, t], target)

    def second_copy(q, t, i):
        src, dst, target = (
            (x_stage, x_second, {"grp": across}),
            (y_stage, y_second, {"sq": peer}),
        )[t]
        return send(src.at[q, 1 + i], dst.at[q, i], second_send.at[q, t, i],
                    second_recv.at[q, t, i], target)

    def reduce_start(q):
        at = slice(2 * slab * q, 2 * slab * (q + 1))
        for t, owner in enumerate((diagonal, sibling)):
            stage[q, t] = acc[at, block_of(owner)].astype(bf16)
            to_core(q, t).start()

    def chip_sum(q, t, owner, side):
        here = pl.ds(pl.multiple_of(2 * slab * q + side * slab, slab), slab)
        there = pl.ds(pl.multiple_of(side * slab, slab), slab)
        return acc[here, block_of(owner)] + from_core[q, t, there].astype(f32)

    def reduce_first(q):
        to_core(q, 0).wait_recv()
        both = chip_sum(q, 0, across, peer).astype(bf16)
        x_stage[q, 0] = both[:half]
        y_stage[q, 0] = both[half:]
        for t in range(2):
            first_copy(q, t).start()
        x_side = chip_sum(q, 0, across, shard)
        x_stage[q, 1] = x_side[:half].astype(bf16)
        second_copy(q, 0, 0).start()
        x_rest[q] = x_side[half:]
        to_core(q, 1).wait_recv()
        y_side = chip_sum(q, 1, grp, peer)
        y_stage[q, 1] = y_side[half:].astype(bf16)
        second_copy(q, 1, 0).start()
        y_rest[q] = y_side[:half]
        own_block[q] = chip_sum(q, 1, grp, shard)

    def reduce_second(q):
        first_copy(q, 1).wait_recv()
        x_stage[q, 2] = (x_rest[q] + y_first[q].astype(f32)).astype(bf16)
        second_copy(q, 0, 1).start()
        first_copy(q, 0).wait_recv()
        y_stage[q, 2] = (y_rest[q] + x_first[q].astype(f32)).astype(bf16)
        second_copy(q, 1, 1).start()

    def reduce_end(q):
        for t in range(2):
            for i in range(2):
                second_copy(q, t, i).wait_recv()
        own_block[q, :half] += x_second[q, 0].astype(f32) + y_second[q, 1].astype(f32)
        own_block[q, half:] += x_second[q, 1].astype(f32) + y_second[q, 0].astype(f32)
        out_ref[:, q * slab : (q + 1) * slab] = own_block[q].T

    for q in early:
        grads_here(far_end, [q], 2)
        products(far_end, [q], False)
        reduce_start(q)

    for q in early:
        reduce_first(q)

    @pl.when(inner)
    def _():
        g_far(far_end, late[0], 1).wait_recv()
        grads_near(far_end, late[:1], 2)

    reduce_second(early[0])

    @pl.when(inner)
    def _():
        g_far(far_middle, late[1], 0).wait_recv()
        grads_near(far_middle, late[1:], 1)

    reduce_second(early[1])

    @pl.when(inner)
    def _():
        g_far(far_end, late[1], 1).wait_recv()
        grads_near(far_end, late[1:], 2)

    for q in late:
        grads_here(far_middle, [q], 1)
        products(far_middle, [q], False)
        grads_here(far_end, [q], 2)
        products(far_end, [q], False)
        reduce_start(q)
        if q > late[0]:
            reduce_second(q - 1)
        reduce_first(q)
    for q in early:
        reduce_end(q)
    reduce_second(late[1])
    for q in late:
        reduce_end(q)

    @pl.when(shard == 0)
    def _():
        for kv in range(kv_heads):
            for i in range(2):
                kv_copy(i, kv).wait_send()

    for w in range(pieces_of):
        w_over_y(w, shard).wait_send()
        w_sibling(w, grp).wait_send()
        w_across(w, grp).wait_send()
        w_diagonal(w, across).wait_send()
    c_copy(expert, 0).wait_send()
    for q in range(quarters):
        g_far(expert, q, 0).wait_send()
    for h in range(parts):
        x_far(expert, h, 0).wait_send()

    @pl.when(inner)
    def _():
        c_copy(end, 1).wait_send()
        for q in range(quarters):
            g_far(end, q, 1).wait_send()
        for h in range(parts):
            x_far(end, h, 1).wait_send()
        for slot, z in enumerate((expert, far_middle, far_end)):
            for q in range(quarters):
                g_near(z, q, slot).wait_send()
            for h in range(parts):
                x_near(z, h, slot).wait_send()

    for q in range(quarters):
        for t in range(2):
            to_core(q, t).wait_send()
            first_copy(q, t).wait_send()
            for i in range(2):
                second_copy(q, t, i).wait_send()


def fused(
    queries, keys, values, norm_gain, expert_ids, gate_values, hidden_grad, gate_weight, up_weight
):
    rows, model_width = queries.shape
    n_ep = lax.axis_size("ep")
    width = gate_weight.shape[2]
    kv_width = keys.shape[1]
    kv_heads = kv_width // HEAD_DIM
    block = model_width // 4
    parts = 4
    part_width = model_width // parts
    quarters = 4
    slab = width // quarters
    half = slab // 2
    cap = rows * expert_ids.shape[1] // n_ep * 3 // 2
    vmem = pl.BlockSpec(memory_space=pltpu.VMEM)
    hbm = pl.BlockSpec(memory_space=pltpu.HBM)
    dma = pltpu.SemaphoreType.DMA
    bf16, f32 = jnp.bfloat16, jnp.float32
    out = pl.pallas_call(
        whole_kernel,
        out_shape=jax.ShapeDtypeStruct((block, width), f32),
        in_specs=[hbm] * 3 + [vmem] * 3 + [hbm] * 3,
        out_specs=vmem,
        scratch_shapes=[
            pltpu.VMEM((rows, model_width), bf16),
            pltpu.VMEM((rows, kv_width), bf16),
            pltpu.VMEM((rows, kv_width), bf16),
            pltpu.VMEM((2, rows, kv_width), bf16),
            pltpu.VMEM((rows, model_width), f32),
            pltpu.VMEM((n_ep, parts, rows, part_width), bf16),
            pltpu.VMEM((3, parts, cap, part_width), bf16),
            pltpu.VMEM((n_ep, quarters, rows, 2 * slab), bf16),
            pltpu.VMEM((3, quarters, cap, 2 * slab), bf16),
            pltpu.VMEM((n_ep, 8, rows), f32),
            pltpu.VMEM((3, cap, rows), bf16),
            pltpu.VMEM((2, model_width, width), bf16),
            pltpu.VMEM((2, model_width, width), bf16),
            pltpu.VMEM((n_ep, quarters, rows, 2 * slab), f32),
            pltpu.VMEM((2, quarters, rows, 2 * slab), f32),
            pltpu.VMEM((width, rows), bf16),
            pltpu.VMEM((2 * width, model_width), f32),
            pltpu.VMEM((quarters, 2, 2 * slab, block), bf16),
            pltpu.VMEM((quarters, 2, 2 * slab, block), bf16),
            pltpu.VMEM((quarters, 3, half, block), bf16),
            pltpu.VMEM((quarters, 3, half, block), bf16),
            pltpu.VMEM((quarters, slab, block), f32),
            pltpu.VMEM((quarters, half, block), f32),
            pltpu.VMEM((quarters, half, block), f32),
            pltpu.VMEM((n_ep, rows, 2 * slab), f32),
            pltpu.VMEM((quarters, half, block), bf16),
            pltpu.VMEM((quarters, half, block), bf16),
            pltpu.VMEM((quarters, 2, half, block), bf16),
            pltpu.VMEM((quarters, 2, half, block), bf16),
            dma((5 + 2 * quarters,)), dma((2, kv_heads)), dma((2, kv_heads)),
            dma((4,)), dma((4,)), dma((4,)), dma((4,)), dma((4,)), dma((4,)), dma((4,)), dma((4,)),
            dma((2,)), dma((n_ep,)), dma((2, quarters)), dma((3, quarters)), dma((n_ep, quarters)),
            dma((2, parts)), dma((3, parts)), dma((n_ep, parts)),
            dma((quarters, 2)), dma((quarters, 2)), dma((quarters, 2)), dma((quarters, 2)),
            dma((quarters, 2, 2)), dma((quarters, 2, 2)),
        ],
        compiler_params=pltpu.CompilerParams(
            collective_id=0, has_side_effects=True, vmem_limit_bytes=56 << 20
        ),
    )(
        queries, keys, values, norm_gain.reshape(1, -1), expert_ids.T, gate_values.T, hidden_grad,
        gate_weight[0], up_weight[0],
    )
    return out[None]


def solution(mesh):
    small = mesh.shape["grp"] == 4 and mesh.shape["sq"] == 2 and mesh.shape["ep"] == 4
    return jax.shard_map(
        fused if small else body,
        mesh=mesh,
        in_specs=(
            P(("grp", "ep", "sq"), None),
            P(("grp", "ep", "sq"), None),
            P(("grp", "ep", "sq"), None),
            P(),
            P(("grp", "ep", "sq"), None),
            P(("grp", "ep", "sq"), None),
            P(("grp", "ep", "sq"), None),
            P("ep", None, "sq"),
            P("ep", None, "sq"),
        ),
        out_specs=P("ep", "grp", "sq"),
        check_vma=False,
    )
```

```python
import functools
import math

import jax
import jax.numpy as jnp
from jax import lax
from jax.experimental import pallas as pl
from jax.experimental.pallas import tpu as pltpu
from jax.sharding import PartitionSpec as P

HEAD_DIM = 128

epsilon = 1e-05
masked_score = -1e30
LOG2E = 1.4426950408889634
MESH = pl.DeviceIdType.MESH


def attention_kernel(group_size, shard_ref, q_ref, ko_ref, vo_ref, kp_ref, vp_ref, gain_ref, out_ref, acc_ref):
    rows, model_width = q_ref.shape
    past = kp_ref.shape[0]
    scale = 1.0 / math.sqrt(HEAD_DIM)
    shard = shard_ref[0]
    contract = (((1,), (1,)), ((), ()))
    causal = lax.broadcasted_iota(jnp.int32, (rows, rows), 1) <= lax.broadcasted_iota(
        jnp.int32, (rows, rows), 0
    )
    seen = lax.broadcasted_iota(jnp.int32, (rows, past), 1) < shard * rows
    squares = jnp.zeros((rows, 1), jnp.float32)
    for head in range(model_width // HEAD_DIM):
        cols = slice(head * HEAD_DIM, (head + 1) * HEAD_DIM)
        kv = head // group_size
        kv_cols = slice(kv * HEAD_DIM, (kv + 1) * HEAD_DIM)
        q = q_ref[:, cols]
        own = lax.dot_general(q, ko_ref[:, kv_cols], contract, preferred_element_type=jnp.float32)
        old = lax.dot_general(q, kp_ref[:, kv_cols], contract, preferred_element_type=jnp.float32)
        own = jnp.where(causal, own * scale, masked_score)
        old = jnp.where(seen, old * scale, masked_score)
        top = jnp.maximum(
            jnp.max(own, axis=1, keepdims=True), jnp.max(old, axis=1, keepdims=True)
        )
        own = jnp.exp(own - top)
        old = jnp.exp(old - top)
        total = jnp.sum(own, axis=1, keepdims=True) + jnp.sum(old, axis=1, keepdims=True)
        out = jnp.dot(
            own.astype(jnp.bfloat16), vo_ref[:, kv_cols], preferred_element_type=jnp.float32
        ) + jnp.dot(
            old.astype(jnp.bfloat16), vp_ref[:, kv_cols], preferred_element_type=jnp.float32
        )
        out = out / total
        acc_ref[:, cols] = out
        squares = squares + jnp.sum(out * out, axis=1, keepdims=True)
    inverse = lax.rsqrt(squares / model_width + epsilon)
    out_ref[...] = (acc_ref[...] * inverse * gain_ref[...]).astype(jnp.bfloat16)


def attend(shard, queries, keys, values, past_keys, past_values, norm_gain):
    rows, model_width = queries.shape
    group_size = model_width // keys.shape[1]
    vmem = pl.BlockSpec(memory_space=pltpu.VMEM)
    return pl.pallas_call(
        functools.partial(attention_kernel, group_size),
        out_shape=jax.ShapeDtypeStruct((rows, model_width), jnp.bfloat16),
        in_specs=[pl.BlockSpec(memory_space=pltpu.SMEM)] + [vmem] * 6,
        out_specs=vmem,
        scratch_shapes=[pltpu.VMEM((rows, model_width), jnp.float32)],
        compiler_params=pltpu.CompilerParams(vmem_limit_bytes=32 << 20),
        cost_estimate=pl.CostEstimate(
            flops=4 * rows * model_width * (rows + past_keys.shape[0]),
            bytes_accessed=4 * rows * model_width,
            transcendentals=rows * (model_width // HEAD_DIM) * (rows + past_keys.shape[0]),
        ),
    )(shard.reshape(1), queries, keys, values, past_keys, past_values, norm_gain.reshape(1, -1))


def ring(size, shift):
    return [(i, (i + shift) % size) for i in range(size)]


def body(
    queries, keys, values, norm_gain, expert_ids, gate_values, hidden_grad, gate_weight, up_weight
):
    rows, model_width = queries.shape
    n_ep = lax.axis_size("ep")
    n_sq = lax.axis_size("sq")
    shard = lax.axis_index("sq")
    expert = lax.axis_index("ep")
    weight_gate = gate_weight[0]
    weight_up = up_weight[0]
    width = weight_gate.shape[1]
    kv_width = keys.shape[1]

    both = jnp.concatenate([keys, values], axis=1)
    past = []
    for j in range(1, n_sq):
        past.append(lax.ppermute(both, "sq", [(i, i + j) for i in range(n_sq - j)]))
    past = jnp.concatenate(past, axis=0)

    def columns_of(owner):
        return lax.dynamic_slice_in_dim(hidden_grad, owner * width, width, 1)

    grads = [columns_of(shard)]
    for j in range(1, n_sq):
        grads.append(lax.ppermute(columns_of((shard + j) % n_sq), "sq", ring(n_sq, j)))
    grad = jnp.concatenate(grads, axis=0)

    chosen = expert_ids[:, :, None] == jnp.arange(n_ep, dtype=jnp.int32)
    share = jnp.sum(jnp.where(chosen, gate_values[:, :, None], 0.0), axis=1).T
    shares = lax.all_gather(share, ("ep", "sq"), axis=0, tiled=False)
    shares = lax.dynamic_index_in_dim(shares, expert, 1, keepdims=False).reshape(n_ep, n_sq, rows)
    shares = jnp.concatenate(
        [
            lax.dynamic_index_in_dim(shares, (shard - j) % n_sq, 1, keepdims=False)
            for j in range(n_sq)
        ],
        axis=1,
    )

    normed = attend(
        shard, queries, keys, values, past[:, :kv_width], past[:, kv_width:], norm_gain
    )

    def add_chunk(step, tokens, grad, summed):
        source = (expert - step) % n_ep
        share_here = lax.dynamic_index_in_dim(shares, source, 0, keepdims=False)
        pieces = [tokens]
        for j in range(1, n_sq):
            pieces.append(lax.ppermute(tokens, "sq", ring(n_sq, j)))
        for j, inputs in enumerate(pieces):
            part = slice(j * rows, (j + 1) * rows)
            cotangent = (share_here[part, None] * grad[part].astype(jnp.float32)).astype(
                jnp.bfloat16
            )
            pre_gate = jnp.dot(inputs, weight_gate, preferred_element_type=jnp.float32)
            pre_up = jnp.dot(inputs, weight_up, preferred_element_type=jnp.float32)
            sigmoid_gate = jax.nn.sigmoid(pre_gate)
            slope = sigmoid_gate * (1.0 + pre_gate * (1.0 - sigmoid_gate))
            delta = (cotangent.astype(jnp.float32) * pre_up * slope).astype(jnp.bfloat16)
            term = lax.dot_general(
                inputs, delta, (((0,), (0,)), ((), ())), preferred_element_type=jnp.float32
            )
            summed = term if summed is None else summed + term
        return summed

    def turn(tokens, grad):
        return lax.ppermute(tokens, "ep", ring(n_ep, 1)), lax.ppermute(grad, "ep", ring(n_ep, 1))

    if n_ep <= 8:
        summed = None
        tokens = normed
        for step in range(n_ep):
            if step < n_ep - 1:
                turned = turn(tokens, grad)
            summed = add_chunk(step, tokens, grad, summed)
            if step < n_ep - 1:
                tokens, grad = turned
    else:

        def one_step(step, carried):
            tokens, grad, summed = carried
            turned = turn(tokens, grad)
            return (*turned, add_chunk(step, tokens, grad, summed))

        start = jnp.zeros((model_width, width), jnp.float32)
        summed = lax.fori_loop(0, n_ep, one_step, (normed, grad, start))[2]
    return lax.psum_scatter(
        summed[None].astype(jnp.bfloat16), "grp", scatter_dimension=1, tiled=True
    ).astype(jnp.float32)


def whole_kernel(
    q_hbm, k_hbm, v_hbm, gain_ref, ids_ref, values_ref, hidden_hbm, gate_hbm, up_hbm, out_ref,
    q_ref, k_ref, v_ref, kv_buf, n_buf, n_out, inverse_ref, x_full, x_out, g_full, g_out, c_buf, choice_ref,
    w_gate, w_up, h_ref, pre_ref, delta_ref, acc, stage, from_core, x_stage, y_stage, own_block,
    x_rest, y_rest, share_ref,
    x_first, y_first, x_second, y_second,
    load_sem, kv_send, kv_recv, wy_send, wy_recv, ws_send, ws_recv, wa_send, wa_recv,
    wd_send, wd_recv, c_send, c_recv, nf_send, nn_send, n_recv, gf_send, gn_send, g_recv, xf_send, xn_send, x_recv,
    core_send, core_recv, first_send, first_recv, second_send, second_recv,
):
    n_ep = x_full.shape[0]
    rows, model_width = q_ref.shape
    cap = x_out.shape[2]
    parts = x_full.shape[1]
    part_width = model_width // parts
    width = gate_hbm.shape[1]
    quarters = g_full.shape[1]
    slab = width // quarters
    half = slab // 2
    kv_heads = k_ref.shape[1] // HEAD_DIM
    group_size = model_width // k_ref.shape[1]
    block = model_width // 4
    bf16, f32 = jnp.bfloat16, jnp.float32
    grp, expert, shard = lax.axis_index("grp"), lax.axis_index("ep"), lax.axis_index("sq")
    peer = 1 - shard
    core = lax.rem(grp, 2)
    chip = grp // 2
    sibling = chip * 2 + 1 - core
    across = (1 - chip) * 2 + core
    diagonal = (1 - chip) * 2 + 1 - core
    last = n_ep - 1
    right, left = lax.rem(expert + 1, n_ep), lax.rem(expert + last, n_ep)
    upper_side = expert // 2
    inner = jnp.logical_and(expert > 0, expert < last)
    outer = jnp.logical_not(inner)
    end = 3 * upper_side
    middle = 1 + upper_side
    far_middle = 2 - upper_side
    far_end = 3 - 3 * upper_side
    far = {"ep": jnp.where(inner, far_middle, middle)}
    near = {"ep": end}
    first = jnp.where(inner, end, middle)

    def load(i, src, dst):
        return pltpu.make_async_copy(src, dst, load_sem.at[i])

    loads = [
        load(0, q_hbm, q_ref),
        load(1, k_hbm, k_ref),
        load(2, v_hbm, v_ref),
        load(3, gate_hbm, w_gate.at[shard]),
        load(4, up_hbm, w_up.at[shard]),
    ]
    grad_loads = [
        load(
            5 + 2 * q + h,
            hidden_hbm.at[:, h * width + q * slab : h * width + (q + 1) * slab],
            g_full.at[expert, q, :, h * slab : (h + 1) * slab],
        )
        for q in range(quarters)
        for h in range(2)
    ]
    for copy in grad_loads + loads:
        copy.start()

    c_buf[...] = jnp.ones_like(c_buf)
    n_out[...] = jnp.zeros_like(n_out)
    names = lax.broadcasted_iota(jnp.int32, c_buf.shape[1:], 0)
    c_buf[expert] = sum(
        jnp.where(names == ids_ref[k : k + 1], values_ref[k : k + 1], 0.0)
        for k in range(ids_ref.shape[0])
    )

    @pl.when(outer)
    def _():
        for z in range(n_ep):

            @pl.when(z != expert)
            def _():
                for p in range(parts):
                    x_full[z, p, cap:rows] = jnp.zeros((rows - cap, part_width), bf16)
                for q in range(quarters):
                    g_full[z, q, cap:rows] = jnp.zeros((rows - cap, 2 * slab), bf16)

    @pl.when(shard == 0)
    def _():
        kv_buf[...] = jnp.zeros_like(kv_buf)

    barrier = pltpu.get_barrier_semaphore()
    for target in ({"sq": peer}, {"ep": right}, {"ep": left}, {"grp": sibling}, {"grp": across}):
        pl.semaphore_signal(barrier, inc=1, device_id=target, device_id_type=MESH)
    pl.semaphore_wait(barrier, 5)

    def send(src, dst, send_sem, recv_sem, target):
        return pltpu.make_async_remote_copy(
            src_ref=src, dst_ref=dst, send_sem=send_sem, recv_sem=recv_sem,
            device_id=target, device_id_type=MESH,
        )

    def kv_copy(i, kv):
        cols = slice(kv * HEAD_DIM, (kv + 1) * HEAD_DIM)
        return send((k_hbm, v_hbm)[i].at[:, cols], kv_buf.at[i, :, cols],
                    kv_send.at[i, kv], kv_recv.at[i, kv], {"sq": peer})

    weights = (w_gate, w_up)

    pieces_of = 2 * 2
    piece = block // 2

    def rows_of(w, owner):
        return pl.ds(pl.multiple_of(owner * block + w // 2 * piece, piece), piece)

    def w_over_y(w, half_of):
        mine = rows_of(w, grp)
        return send((gate_hbm, up_hbm)[w % 2].at[mine], weights[w % 2].at[half_of, mine],
                    wy_send.at[w], wy_recv.at[w], {"sq": peer})

    def w_on(w, owner, target, send_sem, recv_sem):
        there = weights[w % 2].at[peer, rows_of(w, owner)]
        return send(there, there, send_sem.at[w], recv_sem.at[w], {"grp": target})

    def w_sibling(w, owner):
        return w_on(w, owner, sibling, ws_send, ws_recv)

    def w_across(w, owner):
        return w_on(w, owner, across, wa_send, wa_recv)

    def w_diagonal(w, owner):
        return w_on(w, owner, sibling, wd_send, wd_recv)

    def c_copy(z, slot):
        return send(c_buf.at[z], c_buf.at[z], c_send.at[slot], c_recv.at[z], far)

    def n_far(z, slot):
        return send(n_buf.at[z], n_buf.at[z], nf_send.at[slot], n_recv.at[z], far)

    def n_near(z, slot):
        return send(n_out.at[slot], n_buf.at[z], nn_send.at[slot], n_recv.at[z], near)

    def g_far(z, q, slot):
        return send(g_full.at[z, q], g_full.at[z, q], gf_send.at[slot, q], g_recv.at[z, q], far)

    def g_near(z, q, slot):
        return send(g_out.at[slot, q], g_full.at[z, q, 0:cap], gn_send.at[slot, q],
                    g_recv.at[z, q], near)

    def x_far(z, p, slot):
        return send(x_full.at[z, p], x_full.at[z, p], xf_send.at[slot, p], x_recv.at[z, p], far)

    def x_near(z, p, slot):
        return send(x_out.at[slot, p], x_full.at[z, p, 0:cap], xn_send.at[slot, p],
                    x_recv.at[z, p], near)

    @pl.when(shard == 0)
    def _():
        for kv in range(kv_heads):
            for i in range(2):
                kv_copy(i, kv).start()

    for w in range(pieces_of):
        w_over_y(w, shard).start()

    diag = lax.broadcasted_iota(jnp.int32, (rows, rows), 0) == lax.broadcasted_iota(
        jnp.int32, (rows, rows), 1
    )

    def share_row(z, who):
        share = c_buf[z]
        here = lax.broadcasted_iota(jnp.int32, share.shape, 0) == who
        return jnp.sum(jnp.where(here, share, 0.0), axis=0, keepdims=True)

    def choose(z, slot):
        upper = (
            lax.broadcasted_iota(jnp.int32, (rows, rows), 0)
            <= lax.broadcasted_iota(jnp.int32, (rows, rows), 1)
        ).astype(f32).astype(bf16)
        places = lax.broadcasted_iota(jnp.int32, (cap, rows), 0).astype(f32)
        share = share_row(z, end)
        routed = jnp.where(share > 0.0, 1.0, 0.0)
        count = jnp.dot(
            jnp.broadcast_to(routed, (16, rows)).astype(bf16), upper, preferred_element_type=f32
        )[:1]
        key = jnp.where(share > 0.0, count - 1.0, -1.0)
        choice_ref[slot] = jnp.where(places == key, 1.0, 0.0).astype(bf16)

    def grads_near(z, which, slot):
        choice = choice_ref[slot]
        share = jnp.sum(choice.astype(f32) * share_row(z, end), axis=1, keepdims=True)
        for q in which:
            grad = jnp.dot(choice, g_full[z, q], preferred_element_type=f32)
            g_out[slot, q] = (share * grad).astype(bf16)
            g_near(z, q, slot).start()

    def tokens_near(z, p, slot):
        x_out[slot, p] = jnp.dot(
            choice_ref[slot], x_full[z, p], preferred_element_type=f32
        ).astype(bf16)
        x_near(z, p, slot).start()

    def inverse_near(z, slot):
        column = jnp.sum(jnp.where(diag, n_buf[z, 0:1], 0.0), axis=1, keepdims=True)
        chosen = choice_ref[slot].astype(f32).T
        row = jnp.sum(chosen * column, axis=0, keepdims=True)
        n_out[slot, :, 0:cap] = jnp.broadcast_to(row, (8, cap))
        n_near(z, slot).start()

    early, late = range(quarters // 2), range(quarters // 2, quarters)
    c_copy(expert, 0).start()
    for copy in grad_loads:
        copy.wait()
    for q in early:
        g_far(expert, q, 0).start()

    @pl.when(inner)
    def _():
        choose(expert, 0)
        grads_near(expert, early, 0)

    for copy in loads[:3]:
        copy.wait()

    def early_grads():
        @pl.when(inner)
        def _():
            c_copy(end, 1).wait_recv()
            c_copy(end, 1).start()
            for q in early:
                g_far(end, q, 1).wait_recv()
                g_far(end, q, 1).start()
            c_copy(far_middle, 0).wait_recv()
            for q in early:
                g_far(far_middle, q, 0).wait_recv()
            choose(far_middle, 1)
            grads_near(far_middle, early, 1)

    contract = (((1,), (1,)), ((), ()))
    part_rows = rows // 2
    factor = LOG2E / math.sqrt(HEAD_DIM)
    hide = jnp.where(shard == 0, masked_score, 0.0)
    causal = lax.broadcasted_iota(jnp.int32, (part_rows, part_rows), 1) <= (
        lax.broadcasted_iota(jnp.int32, (part_rows, part_rows), 0)
    )
    squares = [jnp.zeros((part_rows, 1), f32)] * 2
    for kv in range(kv_heads):
        kv_cols = slice(kv * HEAD_DIM, (kv + 1) * HEAD_DIM)

        @pl.when(shard == 1)
        def _():
            for i in range(2):
                kv_copy(i, kv).wait_recv()

        if kv == 2:
            early_grads()
        for head in range(kv * group_size, (kv + 1) * group_size):
            cols = slice(head * HEAD_DIM, (head + 1) * HEAD_DIM)
            for p in range(2):
                part = slice(p * part_rows, (p + 1) * part_rows)
                q = q_ref[part, cols]

                def scored(keys):
                    return lax.dot_general(q, keys, contract, preferred_element_type=f32)

                near_scores = jnp.where(causal, scored(k_ref[part, kv_cols]), masked_score)
                pieces = [(near_scores, v_ref[part, kv_cols], 0.0)]
                if p:
                    pieces.append(
                        (scored(k_ref[:part_rows, kv_cols]), v_ref[:part_rows, kv_cols], 0.0)
                    )
                pieces.append((scored(kv_buf[0, :, kv_cols]), kv_buf[1, :, kv_cols], hide))
                top = functools.reduce(
                    jnp.maximum,
                    [jnp.max(s, axis=1, keepdims=True) * factor + away for s, _, away in pieces],
                )
                terms = [jnp.exp2(s * factor - (top - away)) for s, _, away in pieces]
                total = functools.reduce(
                    jnp.add, [jnp.sum(e, axis=1, keepdims=True) for e in terms]
                )
                out = functools.reduce(
                    jnp.add,
                    [
                        jnp.dot(e.astype(bf16), v, preferred_element_type=f32)
                        for e, (_, v, _) in zip(terms, pieces)
                    ],
                )
                out = out * (1.0 / total)
                inside = slice(cols.start - kv * part_width, cols.stop - kv * part_width)
                x_full[expert, kv, part, inside] = (out * gain_ref[:, cols]).astype(bf16)
                squares[p] = squares[p] + jnp.sum(out * out, axis=1, keepdims=True)
        x_far(expert, kv, 0).start()

        @pl.when(inner)
        def _():
            tokens_near(expert, kv, 0)

    inverse = jnp.concatenate(
        [lax.rsqrt(s / model_width + epsilon) for s in squares], axis=0
    )
    inverse = jnp.sum(jnp.where(diag, inverse, 0.0), axis=0, keepdims=True)
    n_buf[expert] = jnp.broadcast_to(inverse, (8, rows))
    n_far(expert, 0).start()

    @pl.when(inner)
    def _():
        inverse_near(expert, 0)

    @pl.when(outer)
    def _():
        for q in late:
            g_far(expert, q, 0).start()

    for i in range(2):
        loads[3 + i].wait()

    def weights_from_y(w):
        w_over_y(w, peer).wait_recv()
        w_across(w, grp).start()
        w_sibling(w, grp).start()

    def weights_from_x(w):
        w_across(w, across).wait_recv()
        w_diagonal(w, across).start()

    def first_tokens(h):
        @pl.when(inner)
        def _():
            x_far(end, h, 1).wait_recv()
            x_far(end, h, 1).start()
            x_far(far_middle, h, 0).wait_recv()
            tokens_near(far_middle, h, 1)
            if h == parts - 1:
                n_far(end, 1).wait_recv()
                n_far(end, 1).start()
                n_far(far_middle, 0).wait_recv()
                inverse_near(far_middle, 1)

    def second_tokens(h):
        @pl.when(inner)
        def _():
            if h == 0:
                c_copy(far_end, 1).wait_recv()
                choose(far_end, 2)
            if h == parts - 1:
                for q in early:
                    g_far(far_end, q, 1).wait_recv()
                grads_near(far_end, early, 2)
            x_far(far_end, h, 1).wait_recv()
            tokens_near(far_end, h, 2)
            if h == parts - 1:
                n_far(far_end, 1).wait_recv()
                inverse_near(far_end, 2)
                grads_near(expert, late[:1], 0)

    def tile_of(weight, side, ab, h):
        cols = pl.ds(pl.multiple_of(ab * 2 * slab, 2 * slab), 2 * slab)
        return weight[side, h * part_width : (h + 1) * part_width, cols]

    def keep_factor(z, side, ab, pre_gate, pre_up):
        scale = inverse_ref[z]
        pre_gate = pre_gate * scale
        sigmoid_gate = 0.5 * jnp.tanh(0.5 * pre_gate) + 0.5
        value = pre_up * scale * scale * (sigmoid_gate * (1.0 + pre_gate * (1.0 - sigmoid_gate)))
        cols = pl.ds(pl.multiple_of(side * slab, slab), slab)
        for i in range(2):
            h_ref[z, 2 * ab + i, :, cols] = value[:, i * slab : (i + 1) * slab]

    def forward_side(z, side):
        @pl.loop(0, quarters // 2)
        def _(ab):
            def product(weight):
                return sum(
                    jnp.dot(x_full[z, h], tile_of(weight, side, ab, h), preferred_element_type=f32)
                    for h in range(parts)
                )

            keep_factor(z, side, ab, product(w_gate), product(w_up))

    def forward(z):
        @pl.loop(0, 2)
        def _(side):
            forward_side(z, side)

    def forward_part(z, h):
        @pl.loop(0, 4)
        def _(t):
            side, ab = t // 2, lax.rem(t, 2)
            sums = [
                jnp.dot(x_full[z, h], tile_of(weight, side, ab, h), preferred_element_type=f32)
                for weight in weights
            ]
            if h:
                sums = [pre_ref[i, t] + sums[i] for i in range(2)]
            if h < parts - 1:
                for i in range(2):
                    pre_ref[i, t] = sums[i]
            else:
                keep_factor(z, side, ab, *sums)

    def share_column(z):
        share = jnp.sum(jnp.where(diag, share_row(z, expert), 0.0), axis=1, keepdims=True)
        share_ref[z] = jnp.broadcast_to(share, (rows, 2 * slab))

    def inverse_column(z):
        column = jnp.sum(jnp.where(diag, n_buf[z, 0:1], 0.0), axis=1, keepdims=True)
        inverse_ref[z] = jnp.broadcast_to(column, (rows, 2 * slab))

    def products(z, which, fresh):
        high = 2 * slab * len(which)
        at = slice(2 * slab * which[0], 2 * slab * which[0] + high)
        for i, q in enumerate(which):
            cotangent = (share_ref[z] * g_full[z, q].astype(f32)).astype(bf16).astype(f32)
            delta_ref[2 * slab * i : 2 * slab * (i + 1)] = (cotangent * h_ref[z, q]).T.astype(bf16)
        for h in range(parts):
            cols = slice(h * part_width, (h + 1) * part_width)
            term = jnp.dot(delta_ref[:high], x_full[z, h], preferred_element_type=f32)
            if fresh:
                acc[at, cols] = term
            else:
                acc[at, cols] += term

    def grads_here(z, which, slot):
        @pl.when(outer)
        def _():
            for q in which:
                g_near(z, q, slot).wait_recv()

    def tokens_here(z, slot, which):
        @pl.when(outer)
        def _():
            for h in which:
                x_near(z, h, slot).wait_recv()
                if h == parts - 1:
                    n_near(z, slot).wait_recv()

    share_column(expert)
    inverse_column(expert)
    forward_side(expert, shard)
    weights_from_y(0)
    first_tokens(0)
    weights_from_y(1)
    weights_from_x(0)
    first_tokens(1)
    weights_from_y(2)
    weights_from_x(1)
    first_tokens(2)
    weights_from_y(3)
    weights_from_x(2)
    first_tokens(3)

    @pl.when(inner)
    def _():
        for q in late:
            g_far(expert, q, 0).start()
            g_far(end, q, 1).wait_recv()
            g_far(end, q, 1).start()

    weights_from_x(3)
    for w in range(pieces_of):
        w_sibling(w, sibling).wait_recv()
        w_diagonal(w, diagonal).wait_recv()

    forward_side(expert, peer)
    second_tokens(0)
    products(expert, early, True)
    products(expert, late, True)
    tokens_here(first, 0, range(parts))
    share_column(first)
    inverse_column(first)
    forward(first)
    second_tokens(1)
    grads_here(first, early, 0)
    products(first, early, False)
    tokens_here(far_middle, 1, range(parts))
    second_tokens(2)
    share_column(far_middle)
    inverse_column(far_middle)
    forward(far_middle)
    grads_here(far_middle, early, 1)
    products(far_middle, early, False)
    second_tokens(3)

    share_column(far_end)
    for h in range(parts):
        tokens_here(far_end, 2, [h])
        if h == parts - 1:
            inverse_column(far_end)
        forward_part(far_end, h)

    def block_of(c):
        return pl.ds(pl.multiple_of(c * block, block), block)

    def to_core(q, t):
        return send(stage.at[q, t], from_core.at[q, t], core_send.at[q, t],
                    core_recv.at[q, t], {"grp": sibling})

    def first_copy(q, t):
        src, dst, target = (
            (x_stage, x_first, {"grp": across}),
            (y_stage, y_first, {"sq": peer}),
        )[t]
        return send(src.at[q, 0], dst.at[q], first_send.at[q, t], first_recv.at[q, t], target)

    def second_copy(q, t, i):
        src, dst, target = (
            (x_stage, x_second, {"grp": across}),
            (y_stage, y_second, {"sq": peer}),
        )[t]
        return send(src.at[q, 1 + i], dst.at[q, i], second_send.at[q, t, i],
                    second_recv.at[q, t, i], target)

    def reduce_start(q):
        at = slice(2 * slab * q, 2 * slab * (q + 1))
        for t, owner in enumerate((diagonal, sibling)):
            stage[q, t] = acc[at, block_of(owner)].astype(bf16)
            to_core(q, t).start()

    def chip_sum(q, t, owner, side):
        here = pl.ds(pl.multiple_of(2 * slab * q + side * slab, slab), slab)
        there = pl.ds(pl.multiple_of(side * slab, slab), slab)
        return acc[here, block_of(owner)] + from_core[q, t, there].astype(f32)

    def reduce_first(q):
        to_core(q, 0).wait_recv()
        both = chip_sum(q, 0, across, peer).astype(bf16)
        x_stage[q, 0] = both[:half]
        y_stage[q, 0] = both[half:]
        for t in range(2):
            first_copy(q, t).start()
        x_side = chip_sum(q, 0, across, shard)
        x_stage[q, 1] = x_side[:half].astype(bf16)
        second_copy(q, 0, 0).start()
        x_rest[q] = x_side[half:]
        to_core(q, 1).wait_recv()
        y_side = chip_sum(q, 1, grp, peer)
        y_stage[q, 1] = y_side[half:].astype(bf16)
        second_copy(q, 1, 0).start()
        y_rest[q] = y_side[:half]
        own_block[q] = chip_sum(q, 1, grp, shard)

    def reduce_second(q):
        first_copy(q, 1).wait_recv()
        x_stage[q, 2] = (x_rest[q] + y_first[q].astype(f32)).astype(bf16)
        second_copy(q, 0, 1).start()
        first_copy(q, 0).wait_recv()
        y_stage[q, 2] = (y_rest[q] + x_first[q].astype(f32)).astype(bf16)
        second_copy(q, 1, 1).start()

    def reduce_end(q):
        for t in range(2):
            for i in range(2):
                second_copy(q, t, i).wait_recv()
        own_block[q, :half] += x_second[q, 0].astype(f32) + y_second[q, 1].astype(f32)
        own_block[q, half:] += x_second[q, 1].astype(f32) + y_second[q, 0].astype(f32)
        out_ref[:, q * slab : (q + 1) * slab] = own_block[q].T

    for q in early:
        grads_here(far_end, [q], 2)
        products(far_end, [q], False)
        reduce_start(q)

    for q in early:
        reduce_first(q)

    @pl.when(inner)
    def _():
        g_far(far_middle, late[0], 0).wait_recv()
        grads_near(far_middle, late[:1], 1)
        g_far(far_end, late[0], 1).wait_recv()
        grads_near(far_end, late[:1], 2)
        grads_near(expert, late[1:], 0)

    reduce_second(early[0])

    @pl.when(inner)
    def _():
        g_far(far_middle, late[1], 0).wait_recv()
        grads_near(far_middle, late[1:], 1)

    reduce_second(early[1])

    @pl.when(inner)
    def _():
        g_far(far_end, late[1], 1).wait_recv()
        grads_near(far_end, late[1:], 2)

    for q in late:
        grads_here(first, [q], 0)
        products(first, [q], False)
        grads_here(far_middle, [q], 1)
        products(far_middle, [q], False)
        grads_here(far_end, [q], 2)
        products(far_end, [q], False)
        reduce_start(q)
        if q > late[0]:
            reduce_second(q - 1)
        reduce_first(q)
    for q in early:
        reduce_end(q)
    reduce_second(late[1])
    for q in late:
        reduce_end(q)

    @pl.when(shard == 0)
    def _():
        for kv in range(kv_heads):
            for i in range(2):
                kv_copy(i, kv).wait_send()

    for w in range(pieces_of):
        w_over_y(w, shard).wait_send()
        w_sibling(w, grp).wait_send()
        w_across(w, grp).wait_send()
        w_diagonal(w, across).wait_send()
    c_copy(expert, 0).wait_send()
    n_far(expert, 0).wait_send()
    for q in range(quarters):
        g_far(expert, q, 0).wait_send()
    for h in range(parts):
        x_far(expert, h, 0).wait_send()

    @pl.when(inner)
    def _():
        c_copy(end, 1).wait_send()
        n_far(end, 1).wait_send()
        for q in range(quarters):
            g_far(end, q, 1).wait_send()
        for h in range(parts):
            x_far(end, h, 1).wait_send()
        for slot, z in enumerate((expert, far_middle, far_end)):
            n_near(z, slot).wait_send()
            for q in range(quarters):
                g_near(z, q, slot).wait_send()
            for h in range(parts):
                x_near(z, h, slot).wait_send()

    for q in range(quarters):
        for t in range(2):
            to_core(q, t).wait_send()
            first_copy(q, t).wait_send()
            for i in range(2):
                second_copy(q, t, i).wait_send()


def fused(
    queries, keys, values, norm_gain, expert_ids, gate_values, hidden_grad, gate_weight, up_weight
):
    rows, model_width = queries.shape
    n_ep = lax.axis_size("ep")
    width = gate_weight.shape[2]
    kv_width = keys.shape[1]
    kv_heads = kv_width // HEAD_DIM
    block = model_width // 4
    parts = 4
    part_width = model_width // parts
    quarters = 4
    slab = width // quarters
    half = slab // 2
    cap = rows * expert_ids.shape[1] // n_ep * 3 // 2
    vmem = pl.BlockSpec(memory_space=pltpu.VMEM)
    hbm = pl.BlockSpec(memory_space=pltpu.HBM)
    dma = pltpu.SemaphoreType.DMA
    bf16, f32 = jnp.bfloat16, jnp.float32
    out = pl.pallas_call(
        whole_kernel,
        out_shape=jax.ShapeDtypeStruct((block, width), f32),
        in_specs=[hbm] * 3 + [vmem] * 3 + [hbm] * 3,
        out_specs=vmem,
        scratch_shapes=[
            pltpu.VMEM((rows, model_width), bf16),
            pltpu.VMEM((rows, kv_width), bf16),
            pltpu.VMEM((rows, kv_width), bf16),
            pltpu.VMEM((2, rows, kv_width), bf16),
            pltpu.VMEM((n_ep, 8, rows), f32),
            pltpu.VMEM((3, 8, rows), f32),
            pltpu.VMEM((n_ep, rows, 2 * slab), f32),
            pltpu.VMEM((n_ep, parts, rows, part_width), bf16),
            pltpu.VMEM((3, parts, cap, part_width), bf16),
            pltpu.VMEM((n_ep, quarters, rows, 2 * slab), bf16),
            pltpu.VMEM((3, quarters, cap, 2 * slab), bf16),
            pltpu.VMEM((n_ep, 8, rows), f32),
            pltpu.VMEM((3, cap, rows), bf16),
            pltpu.VMEM((2, model_width, width), bf16),
            pltpu.VMEM((2, model_width, width), bf16),
            pltpu.VMEM((n_ep, quarters, rows, 2 * slab), f32),
            pltpu.VMEM((2, quarters, rows, 2 * slab), f32),
            pltpu.VMEM((width, rows), bf16),
            pltpu.VMEM((2 * width, model_width), f32),
            pltpu.VMEM((quarters, 2, 2 * slab, block), bf16),
            pltpu.VMEM((quarters, 2, 2 * slab, block), bf16),
            pltpu.VMEM((quarters, 3, half, block), bf16),
            pltpu.VMEM((quarters, 3, half, block), bf16),
            pltpu.VMEM((quarters, slab, block), f32),
            pltpu.VMEM((quarters, half, block), f32),
            pltpu.VMEM((quarters, half, block), f32),
            pltpu.VMEM((n_ep, rows, 2 * slab), f32),
            pltpu.VMEM((quarters, half, block), bf16),
            pltpu.VMEM((quarters, half, block), bf16),
            pltpu.VMEM((quarters, 2, half, block), bf16),
            pltpu.VMEM((quarters, 2, half, block), bf16),
            dma((5 + 2 * quarters,)), dma((2, kv_heads)), dma((2, kv_heads)),
            dma((4,)), dma((4,)), dma((4,)), dma((4,)), dma((4,)), dma((4,)), dma((4,)), dma((4,)),
            dma((2,)), dma((n_ep,)), dma((2,)), dma((3,)), dma((n_ep,)), dma((2, quarters)), dma((3, quarters)), dma((n_ep, quarters)),
            dma((2, parts)), dma((3, parts)), dma((n_ep, parts)),
            dma((quarters, 2)), dma((quarters, 2)), dma((quarters, 2)), dma((quarters, 2)),
            dma((quarters, 2, 2)), dma((quarters, 2, 2)),
        ],
        compiler_params=pltpu.CompilerParams(
            collective_id=0, has_side_effects=True, vmem_limit_bytes=56 << 20
        ),
    )(
        queries, keys, values, norm_gain.reshape(1, -1), expert_ids.T, gate_values.T, hidden_grad,
        gate_weight[0], up_weight[0],
    )
    return out[None]


def solution(mesh):
    small = mesh.shape["grp"] == 4 and mesh.shape["sq"] == 2 and mesh.shape["ep"] == 4
    return jax.shard_map(
        fused if small else body,
        mesh=mesh,
        in_specs=(
            P(("grp", "ep", "sq"), None),
            P(("grp", "ep", "sq"), None),
            P(("grp", "ep", "sq"), None),
            P(),
            P(("grp", "ep", "sq"), None),
            P(("grp", "ep", "sq"), None),
            P(("grp", "ep", "sq"), None),
            P("ep", None, "sq"),
            P("ep", None, "sq"),
        ),
        out_specs=P("ep", "grp", "sq"),
        check_vma=False,
    )
```

```python
import functools
import math

import jax
import jax.numpy as jnp
from jax import lax
from jax.experimental import pallas as pl
from jax.experimental.pallas import tpu as pltpu
from jax.sharding import PartitionSpec as P

HEAD_DIM = 128

epsilon = 1e-05
masked_score = -1e30
LOG2E = 1.4426950408889634
MESH = pl.DeviceIdType.MESH


def attention_kernel(group_size, shard_ref, q_ref, ko_ref, vo_ref, kp_ref, vp_ref, gain_ref, out_ref, acc_ref):
    rows, model_width = q_ref.shape
    past = kp_ref.shape[0]
    scale = 1.0 / math.sqrt(HEAD_DIM)
    shard = shard_ref[0]
    contract = (((1,), (1,)), ((), ()))
    causal = lax.broadcasted_iota(jnp.int32, (rows, rows), 1) <= lax.broadcasted_iota(
        jnp.int32, (rows, rows), 0
    )
    seen = lax.broadcasted_iota(jnp.int32, (rows, past), 1) < shard * rows
    squares = jnp.zeros((rows, 1), jnp.float32)
    for head in range(model_width // HEAD_DIM):
        cols = slice(head * HEAD_DIM, (head + 1) * HEAD_DIM)
        kv = head // group_size
        kv_cols = slice(kv * HEAD_DIM, (kv + 1) * HEAD_DIM)
        q = q_ref[:, cols]
        own = lax.dot_general(q, ko_ref[:, kv_cols], contract, preferred_element_type=jnp.float32)
        old = lax.dot_general(q, kp_ref[:, kv_cols], contract, preferred_element_type=jnp.float32)
        own = jnp.where(causal, own * scale, masked_score)
        old = jnp.where(seen, old * scale, masked_score)
        top = jnp.maximum(
            jnp.max(own, axis=1, keepdims=True), jnp.max(old, axis=1, keepdims=True)
        )
        own = jnp.exp(own - top)
        old = jnp.exp(old - top)
        total = jnp.sum(own, axis=1, keepdims=True) + jnp.sum(old, axis=1, keepdims=True)
        out = jnp.dot(
            own.astype(jnp.bfloat16), vo_ref[:, kv_cols], preferred_element_type=jnp.float32
        ) + jnp.dot(
            old.astype(jnp.bfloat16), vp_ref[:, kv_cols], preferred_element_type=jnp.float32
        )
        out = out / total
        acc_ref[:, cols] = out
        squares = squares + jnp.sum(out * out, axis=1, keepdims=True)
    inverse = lax.rsqrt(squares / model_width + epsilon)
    out_ref[...] = (acc_ref[...] * inverse * gain_ref[...]).astype(jnp.bfloat16)


def attend(shard, queries, keys, values, past_keys, past_values, norm_gain):
    rows, model_width = queries.shape
    group_size = model_width // keys.shape[1]
    vmem = pl.BlockSpec(memory_space=pltpu.VMEM)
    return pl.pallas_call(
        functools.partial(attention_kernel, group_size),
        out_shape=jax.ShapeDtypeStruct((rows, model_width), jnp.bfloat16),
        in_specs=[pl.BlockSpec(memory_space=pltpu.SMEM)] + [vmem] * 6,
        out_specs=vmem,
        scratch_shapes=[pltpu.VMEM((rows, model_width), jnp.float32)],
        compiler_params=pltpu.CompilerParams(vmem_limit_bytes=32 << 20),
        cost_estimate=pl.CostEstimate(
            flops=4 * rows * model_width * (rows + past_keys.shape[0]),
            bytes_accessed=4 * rows * model_width,
            transcendentals=rows * (model_width // HEAD_DIM) * (rows + past_keys.shape[0]),
        ),
    )(shard.reshape(1), queries, keys, values, past_keys, past_values, norm_gain.reshape(1, -1))


def ring(size, shift):
    return [(i, (i + shift) % size) for i in range(size)]


def body(
    queries, keys, values, norm_gain, expert_ids, gate_values, hidden_grad, gate_weight, up_weight
):
    rows, model_width = queries.shape
    n_ep = lax.axis_size("ep")
    n_sq = lax.axis_size("sq")
    shard = lax.axis_index("sq")
    expert = lax.axis_index("ep")
    weight_gate = gate_weight[0]
    weight_up = up_weight[0]
    width = weight_gate.shape[1]
    kv_width = keys.shape[1]

    both = jnp.concatenate([keys, values], axis=1)
    past = []
    for j in range(1, n_sq):
        past.append(lax.ppermute(both, "sq", [(i, i + j) for i in range(n_sq - j)]))
    past = jnp.concatenate(past, axis=0)

    def columns_of(owner):
        return lax.dynamic_slice_in_dim(hidden_grad, owner * width, width, 1)

    grads = [columns_of(shard)]
    for j in range(1, n_sq):
        grads.append(lax.ppermute(columns_of((shard + j) % n_sq), "sq", ring(n_sq, j)))
    grad = jnp.concatenate(grads, axis=0)

    chosen = expert_ids[:, :, None] == jnp.arange(n_ep, dtype=jnp.int32)
    share = jnp.sum(jnp.where(chosen, gate_values[:, :, None], 0.0), axis=1).T
    shares = lax.all_gather(share, ("ep", "sq"), axis=0, tiled=False)
    shares = lax.dynamic_index_in_dim(shares, expert, 1, keepdims=False).reshape(n_ep, n_sq, rows)
    shares = jnp.concatenate(
        [
            lax.dynamic_index_in_dim(shares, (shard - j) % n_sq, 1, keepdims=False)
            for j in range(n_sq)
        ],
        axis=1,
    )

    normed = attend(
        shard, queries, keys, values, past[:, :kv_width], past[:, kv_width:], norm_gain
    )

    def add_chunk(step, tokens, grad, summed):
        source = (expert - step) % n_ep
        share_here = lax.dynamic_index_in_dim(shares, source, 0, keepdims=False)
        pieces = [tokens]
        for j in range(1, n_sq):
            pieces.append(lax.ppermute(tokens, "sq", ring(n_sq, j)))
        for j, inputs in enumerate(pieces):
            part = slice(j * rows, (j + 1) * rows)
            cotangent = (share_here[part, None] * grad[part].astype(jnp.float32)).astype(
                jnp.bfloat16
            )
            pre_gate = jnp.dot(inputs, weight_gate, preferred_element_type=jnp.float32)
            pre_up = jnp.dot(inputs, weight_up, preferred_element_type=jnp.float32)
            sigmoid_gate = jax.nn.sigmoid(pre_gate)
            slope = sigmoid_gate * (1.0 + pre_gate * (1.0 - sigmoid_gate))
            delta = (cotangent.astype(jnp.float32) * pre_up * slope).astype(jnp.bfloat16)
            term = lax.dot_general(
                inputs, delta, (((0,), (0,)), ((), ())), preferred_element_type=jnp.float32
            )
            summed = term if summed is None else summed + term
        return summed

    def turn(tokens, grad):
        return lax.ppermute(tokens, "ep", ring(n_ep, 1)), lax.ppermute(grad, "ep", ring(n_ep, 1))

    if n_ep <= 8:
        summed = None
        tokens = normed
        for step in range(n_ep):
            if step < n_ep - 1:
                turned = turn(tokens, grad)
            summed = add_chunk(step, tokens, grad, summed)
            if step < n_ep - 1:
                tokens, grad = turned
    else:

        def one_step(step, carried):
            tokens, grad, summed = carried
            turned = turn(tokens, grad)
            return (*turned, add_chunk(step, tokens, grad, summed))

        start = jnp.zeros((model_width, width), jnp.float32)
        summed = lax.fori_loop(0, n_ep, one_step, (normed, grad, start))[2]
    return lax.psum_scatter(
        summed[None].astype(jnp.bfloat16), "grp", scatter_dimension=1, tiled=True
    ).astype(jnp.float32)


def whole_kernel(
    q_hbm, k_hbm, v_hbm, gain_ref, ids_ref, values_ref, hidden_hbm, gate_hbm, up_hbm, out_ref,
    q_ref, k_ref, v_ref, kv_buf, n_buf, n_out, inverse_ref, x_full, x_out, g_full, g_out, c_buf, choice_ref,
    w_gate, w_up, h_ref, pre_ref, delta_ref, acc, stage, from_core, x_stage, y_stage, own_block,
    x_rest, y_rest, share_ref,
    x_first, y_first, x_second, y_second,
    load_sem, kv_send, kv_recv, wy_send, wy_recv, ws_send, ws_recv, wa_send, wa_recv,
    wd_send, wd_recv, c_send, c_recv, nf_send, nn_send, n_recv, gf_send, gn_send, g_recv, xf_send, xn_send, x_recv,
    core_send, core_recv, first_send, first_recv, second_send, second_recv,
):
    n_ep = x_full.shape[0]
    rows, model_width = q_ref.shape
    cap = x_out.shape[2]
    parts = x_full.shape[1]
    part_width = model_width // parts
    width = gate_hbm.shape[1]
    quarters = g_full.shape[1]
    slab = width // quarters
    half = slab // 2
    kv_heads = k_ref.shape[1] // HEAD_DIM
    group_size = model_width // k_ref.shape[1]
    block = model_width // 4
    bf16, f32 = jnp.bfloat16, jnp.float32
    grp, expert, shard = lax.axis_index("grp"), lax.axis_index("ep"), lax.axis_index("sq")
    peer = 1 - shard
    core = lax.rem(grp, 2)
    chip = grp // 2
    sibling = chip * 2 + 1 - core
    across = (1 - chip) * 2 + core
    diagonal = (1 - chip) * 2 + 1 - core
    last = n_ep - 1
    right, left = lax.rem(expert + 1, n_ep), lax.rem(expert + last, n_ep)
    upper_side = expert // 2
    inner = jnp.logical_and(expert > 0, expert < last)
    outer = jnp.logical_not(inner)
    end = 3 * upper_side
    middle = 1 + upper_side
    far_middle = 2 - upper_side
    far_end = 3 - 3 * upper_side
    far = {"ep": jnp.where(inner, far_middle, middle)}
    near = {"ep": end}
    first = jnp.where(inner, end, middle)

    def load(i, src, dst):
        return pltpu.make_async_copy(src, dst, load_sem.at[i])

    loads = [
        load(0, q_hbm, q_ref),
        load(1, k_hbm, k_ref),
        load(2, v_hbm, v_ref),
        load(3, gate_hbm, w_gate.at[shard]),
        load(4, up_hbm, w_up.at[shard]),
    ]
    grad_loads = [
        load(
            5 + 2 * q + h,
            hidden_hbm.at[:, h * width + q * slab : h * width + (q + 1) * slab],
            g_full.at[expert, q, :, h * slab : (h + 1) * slab],
        )
        for q in range(quarters)
        for h in range(2)
    ]
    for copy in grad_loads + loads:
        copy.start()

    c_buf[...] = jnp.ones_like(c_buf)
    n_out[...] = jnp.zeros_like(n_out)
    names = lax.broadcasted_iota(jnp.int32, c_buf.shape[1:], 0)
    c_buf[expert] = sum(
        jnp.where(names == ids_ref[k : k + 1], values_ref[k : k + 1], 0.0)
        for k in range(ids_ref.shape[0])
    )

    @pl.when(outer)
    def _():
        for z in range(n_ep):

            @pl.when(z != expert)
            def _():
                for p in range(parts):
                    x_full[z, p, cap:rows] = jnp.zeros((rows - cap, part_width), bf16)
                for q in range(quarters):
                    g_full[z, q, cap:rows] = jnp.zeros((rows - cap, 2 * slab), bf16)

    @pl.when(shard == 0)
    def _():
        kv_buf[...] = jnp.zeros_like(kv_buf)

    barrier = pltpu.get_barrier_semaphore()
    for target in ({"sq": peer}, {"ep": right}, {"ep": left}, {"grp": sibling}, {"grp": across}):
        pl.semaphore_signal(barrier, inc=1, device_id=target, device_id_type=MESH)
    pl.semaphore_wait(barrier, 5)

    def send(src, dst, send_sem, recv_sem, target):
        return pltpu.make_async_remote_copy(
            src_ref=src, dst_ref=dst, send_sem=send_sem, recv_sem=recv_sem,
            device_id=target, device_id_type=MESH,
        )

    def kv_copy(i, kv):
        cols = slice(kv * HEAD_DIM, (kv + 1) * HEAD_DIM)
        return send((k_hbm, v_hbm)[i].at[:, cols], kv_buf.at[i, :, cols],
                    kv_send.at[i, kv], kv_recv.at[i, kv], {"sq": peer})

    weights = (w_gate, w_up)

    pieces_of = 2 * 2
    piece = block // 2

    def rows_of(w, owner):
        return pl.ds(pl.multiple_of(owner * block + w // 2 * piece, piece), piece)

    def w_over_y(w, half_of):
        mine = rows_of(w, grp)
        return send((gate_hbm, up_hbm)[w % 2].at[mine], weights[w % 2].at[half_of, mine],
                    wy_send.at[w], wy_recv.at[w], {"sq": peer})

    def w_on(w, owner, target, send_sem, recv_sem):
        there = weights[w % 2].at[peer, rows_of(w, owner)]
        return send(there, there, send_sem.at[w], recv_sem.at[w], {"grp": target})

    def w_sibling(w, owner):
        return w_on(w, owner, sibling, ws_send, ws_recv)

    def w_across(w, owner):
        return w_on(w, owner, across, wa_send, wa_recv)

    def w_diagonal(w, owner):
        return w_on(w, owner, sibling, wd_send, wd_recv)

    def c_copy(z, slot):
        return send(c_buf.at[z], c_buf.at[z], c_send.at[slot], c_recv.at[z], far)

    def n_far(z, slot):
        return send(n_buf.at[z], n_buf.at[z], nf_send.at[slot], n_recv.at[z], far)

    def n_near(z, slot):
        return send(n_out.at[slot], n_buf.at[z], nn_send.at[slot], n_recv.at[z], near)

    def g_far(z, q, slot):
        return send(g_full.at[z, q], g_full.at[z, q], gf_send.at[slot, q], g_recv.at[z, q], far)

    def g_near(z, q, slot):
        return send(g_out.at[slot, q], g_full.at[z, q, 0:cap], gn_send.at[slot, q],
                    g_recv.at[z, q], near)

    def x_far(z, p, slot):
        return send(x_full.at[z, p], x_full.at[z, p], xf_send.at[slot, p], x_recv.at[z, p], far)

    def x_near(z, p, slot):
        return send(x_out.at[slot, p], x_full.at[z, p, 0:cap], xn_send.at[slot, p],
                    x_recv.at[z, p], near)

    @pl.when(shard == 0)
    def _():
        for kv in range(kv_heads):
            for i in range(2):
                kv_copy(i, kv).start()

    for w in range(pieces_of):
        w_over_y(w, shard).start()

    diag = lax.broadcasted_iota(jnp.int32, (rows, rows), 0) == lax.broadcasted_iota(
        jnp.int32, (rows, rows), 1
    )

    def share_row(z, who):
        share = c_buf[z]
        here = lax.broadcasted_iota(jnp.int32, share.shape, 0) == who
        return jnp.sum(jnp.where(here, share, 0.0), axis=0, keepdims=True)

    def choose(z, slot):
        upper = (
            lax.broadcasted_iota(jnp.int32, (rows, rows), 0)
            <= lax.broadcasted_iota(jnp.int32, (rows, rows), 1)
        ).astype(f32).astype(bf16)
        places = lax.broadcasted_iota(jnp.int32, (cap, rows), 0).astype(f32)
        share = share_row(z, end)
        routed = jnp.where(share > 0.0, 1.0, 0.0)
        count = jnp.dot(
            jnp.broadcast_to(routed, (16, rows)).astype(bf16), upper, preferred_element_type=f32
        )[:1]
        key = jnp.where(share > 0.0, count - 1.0, -1.0)
        choice_ref[slot] = jnp.where(places == key, 1.0, 0.0).astype(bf16)

    def grads_near(z, which, slot):
        choice = choice_ref[slot]
        share = jnp.sum(choice.astype(f32) * share_row(z, end), axis=1, keepdims=True)
        for q in which:
            grad = jnp.dot(choice, g_full[z, q], preferred_element_type=f32)
            g_out[slot, q] = (share * grad).astype(bf16)
            g_near(z, q, slot).start()

    def tokens_near(z, p, slot):
        x_out[slot, p] = jnp.dot(
            choice_ref[slot], x_full[z, p], preferred_element_type=f32
        ).astype(bf16)
        x_near(z, p, slot).start()

    def inverse_near(z, slot):
        column = jnp.sum(jnp.where(diag, n_buf[z, 0:1], 0.0), axis=1, keepdims=True)
        chosen = choice_ref[slot].astype(f32).T
        row = jnp.sum(chosen * column, axis=0, keepdims=True)
        n_out[slot, :, 0:cap] = jnp.broadcast_to(row, (8, cap))
        n_near(z, slot).start()

    early, late = range(quarters // 2), range(quarters // 2, quarters)
    c_copy(expert, 0).start()
    for copy in grad_loads:
        copy.wait()
    for q in early:
        g_far(expert, q, 0).start()

    @pl.when(inner)
    def _():
        choose(expert, 0)
        grads_near(expert, early, 0)

    for copy in loads[:3]:
        copy.wait()

    def early_grads():
        @pl.when(inner)
        def _():
            c_copy(end, 1).wait_recv()
            c_copy(end, 1).start()
            for q in early:
                g_far(end, q, 1).wait_recv()
                g_far(end, q, 1).start()
            c_copy(far_middle, 0).wait_recv()
            for q in early:
                g_far(far_middle, q, 0).wait_recv()
            choose(far_middle, 1)
            grads_near(far_middle, early, 1)

    contract = (((1,), (1,)), ((), ()))
    part_rows = rows // 2
    factor = LOG2E / math.sqrt(HEAD_DIM)
    hide = jnp.where(shard == 0, masked_score, 0.0)
    causal = lax.broadcasted_iota(jnp.int32, (part_rows, part_rows), 1) <= (
        lax.broadcasted_iota(jnp.int32, (part_rows, part_rows), 0)
    )
    squares = [jnp.zeros((part_rows, 1), f32)] * 2
    for kv in range(kv_heads):
        kv_cols = slice(kv * HEAD_DIM, (kv + 1) * HEAD_DIM)

        @pl.when(shard == 1)
        def _():
            for i in range(2):
                kv_copy(i, kv).wait_recv()

        if kv == 2:
            early_grads()
        for head in range(kv * group_size, (kv + 1) * group_size):
            cols = slice(head * HEAD_DIM, (head + 1) * HEAD_DIM)
            for p in range(2):
                part = slice(p * part_rows, (p + 1) * part_rows)
                q = q_ref[part, cols]

                def scored(keys):
                    return lax.dot_general(q, keys, contract, preferred_element_type=f32)

                near_scores = jnp.where(causal, scored(k_ref[part, kv_cols]), masked_score)
                pieces = [(near_scores, v_ref[part, kv_cols], 0.0)]
                if p:
                    pieces.append(
                        (scored(k_ref[:part_rows, kv_cols]), v_ref[:part_rows, kv_cols], 0.0)
                    )
                pieces.append((scored(kv_buf[0, :, kv_cols]), kv_buf[1, :, kv_cols], hide))
                top = functools.reduce(
                    jnp.maximum,
                    [jnp.max(s, axis=1, keepdims=True) * factor + away for s, _, away in pieces],
                )
                terms = [jnp.exp2(s * factor - (top - away)) for s, _, away in pieces]
                total = functools.reduce(
                    jnp.add, [jnp.sum(e, axis=1, keepdims=True) for e in terms]
                )
                out = functools.reduce(
                    jnp.add,
                    [
                        jnp.dot(e.astype(bf16), v, preferred_element_type=f32)
                        for e, (_, v, _) in zip(terms, pieces)
                    ],
                )
                out = out * (1.0 / total)
                inside = slice(cols.start - kv * part_width, cols.stop - kv * part_width)
                x_full[expert, kv, part, inside] = (out * gain_ref[:, cols]).astype(bf16)
                squares[p] = squares[p] + jnp.sum(out * out, axis=1, keepdims=True)
        x_far(expert, kv, 0).start()

        @pl.when(inner)
        def _():
            tokens_near(expert, kv, 0)

    inverse = jnp.concatenate(
        [lax.rsqrt(s / model_width + epsilon) for s in squares], axis=0
    )
    inverse = jnp.sum(jnp.where(diag, inverse, 0.0), axis=0, keepdims=True)
    n_buf[expert] = jnp.broadcast_to(inverse, (8, rows))
    n_far(expert, 0).start()

    @pl.when(inner)
    def _():
        inverse_near(expert, 0)

    @pl.when(outer)
    def _():
        for q in late:
            g_far(expert, q, 0).start()

    for i in range(2):
        loads[3 + i].wait()

    def weights_from_y(w):
        w_over_y(w, peer).wait_recv()
        w_across(w, grp).start()
        w_sibling(w, grp).start()

    def weights_from_x(w):
        w_across(w, across).wait_recv()
        w_diagonal(w, across).start()

    def first_tokens(h):
        @pl.when(inner)
        def _():
            x_far(end, h, 1).wait_recv()
            x_far(end, h, 1).start()
            x_far(far_middle, h, 0).wait_recv()
            tokens_near(far_middle, h, 1)
            if h == parts - 1:
                n_far(end, 1).wait_recv()
                n_far(end, 1).start()
                n_far(far_middle, 0).wait_recv()
                inverse_near(far_middle, 1)

    def second_tokens(h):
        @pl.when(inner)
        def _():
            if h == 0:
                c_copy(far_end, 1).wait_recv()
                choose(far_end, 2)
            if h == parts - 1:
                for q in early:
                    g_far(far_end, q, 1).wait_recv()
                grads_near(far_end, early, 2)
            x_far(far_end, h, 1).wait_recv()
            tokens_near(far_end, h, 2)
            if h == parts - 1:
                n_far(far_end, 1).wait_recv()
                inverse_near(far_end, 2)
                grads_near(expert, late[:1], 0)

    def tile_of(weight, side, ab, h):
        cols = pl.ds(pl.multiple_of(ab * 2 * slab, 2 * slab), 2 * slab)
        return weight[side, h * part_width : (h + 1) * part_width, cols]

    def keep_factor(z, side, ab, pre_gate, pre_up):
        scale = inverse_ref[z]
        pre_gate = pre_gate * scale
        sigmoid_gate = 0.5 * jnp.tanh(0.5 * pre_gate) + 0.5
        value = pre_up * scale * scale * (sigmoid_gate * (1.0 + pre_gate * (1.0 - sigmoid_gate)))
        cols = pl.ds(pl.multiple_of(side * slab, slab), slab)
        for i in range(2):
            h_ref[z, 2 * ab + i, :, cols] = value[:, i * slab : (i + 1) * slab]

    def forward_side(z, side):
        @pl.loop(0, quarters // 2)
        def _(ab):
            def product(weight):
                return sum(
                    jnp.dot(x_full[z, h], tile_of(weight, side, ab, h), preferred_element_type=f32)
                    for h in range(parts)
                )

            keep_factor(z, side, ab, product(w_gate), product(w_up))

    def forward(z):
        @pl.loop(0, 2)
        def _(side):
            forward_side(z, side)

    def forward_part(z, h):
        @pl.loop(0, 4)
        def _(t):
            side, ab = t // 2, lax.rem(t, 2)
            sums = [
                jnp.dot(x_full[z, h], tile_of(weight, side, ab, h), preferred_element_type=f32)
                for weight in weights
            ]
            if h:
                sums = [pre_ref[i, t] + sums[i] for i in range(2)]
            if h < parts - 1:
                for i in range(2):
                    pre_ref[i, t] = sums[i]
            else:
                keep_factor(z, side, ab, *sums)

    def share_column(z):
        share = jnp.sum(jnp.where(diag, share_row(z, expert), 0.0), axis=1, keepdims=True)
        share_ref[z] = jnp.broadcast_to(share, (rows, 2 * slab))

    def inverse_column(z):
        column = jnp.sum(jnp.where(diag, n_buf[z, 0:1], 0.0), axis=1, keepdims=True)
        inverse_ref[z] = jnp.broadcast_to(column, (rows, 2 * slab))

    def products(z, which, fresh):
        high = 2 * slab * len(which)
        at = slice(2 * slab * which[0], 2 * slab * which[0] + high)
        for i, q in enumerate(which):
            cotangent = (share_ref[z] * g_full[z, q].astype(f32)).astype(bf16).astype(f32)
            delta_ref[2 * slab * i : 2 * slab * (i + 1)] = (cotangent * h_ref[z, q]).T.astype(bf16)
        for h in range(parts):
            cols = slice(h * part_width, (h + 1) * part_width)
            term = jnp.dot(delta_ref[:high], x_full[z, h], preferred_element_type=f32)
            if fresh:
                acc[at, cols] = term
            else:
                acc[at, cols] += term

    def grads_here(z, which, slot):
        @pl.when(outer)
        def _():
            for q in which:
                g_near(z, q, slot).wait_recv()

    def tokens_here(z, slot, which):
        @pl.when(outer)
        def _():
            for h in which:
                x_near(z, h, slot).wait_recv()
                if h == parts - 1:
                    n_near(z, slot).wait_recv()

    share_column(expert)
    inverse_column(expert)
    forward_side(expert, shard)
    weights_from_y(0)
    first_tokens(0)
    weights_from_y(1)
    weights_from_x(0)
    first_tokens(1)
    weights_from_y(2)
    weights_from_x(1)
    first_tokens(2)
    weights_from_y(3)
    weights_from_x(2)
    first_tokens(3)

    @pl.when(inner)
    def _():
        for q in late:
            g_far(expert, q, 0).start()
            g_far(end, q, 1).wait_recv()
            g_far(end, q, 1).start()

    weights_from_x(3)
    for w in range(pieces_of):
        w_sibling(w, sibling).wait_recv()
        w_diagonal(w, diagonal).wait_recv()

    second_tokens(0)
    forward_side(expert, peer)
    products(expert, early, True)
    second_tokens(1)
    products(expert, late, True)
    tokens_here(first, 0, range(parts))
    share_column(first)
    inverse_column(first)
    forward(first)
    second_tokens(2)
    grads_here(first, early, 0)
    products(first, early, False)
    tokens_here(far_middle, 1, range(parts))
    share_column(far_middle)
    inverse_column(far_middle)
    forward(far_middle)
    second_tokens(3)
    grads_here(far_middle, early, 1)
    products(far_middle, early, False)

    share_column(far_end)
    for h in range(parts):
        tokens_here(far_end, 2, [h])
        if h == parts - 1:
            inverse_column(far_end)
        forward_part(far_end, h)

    def block_of(c):
        return pl.ds(pl.multiple_of(c * block, block), block)

    def to_core(q, t):
        return send(stage.at[q, t], from_core.at[q, t], core_send.at[q, t],
                    core_recv.at[q, t], {"grp": sibling})

    def first_copy(q, t):
        src, dst, target = (
            (x_stage, x_first, {"grp": across}),
            (y_stage, y_first, {"sq": peer}),
        )[t]
        return send(src.at[q, 0], dst.at[q], first_send.at[q, t], first_recv.at[q, t], target)

    def second_copy(q, t, i):
        src, dst, target = (
            (x_stage, x_second, {"grp": across}),
            (y_stage, y_second, {"sq": peer}),
        )[t]
        return send(src.at[q, 1 + i], dst.at[q, i], second_send.at[q, t, i],
                    second_recv.at[q, t, i], target)

    def reduce_start(q):
        at = slice(2 * slab * q, 2 * slab * (q + 1))
        for t, owner in enumerate((diagonal, sibling)):
            stage[q, t] = acc[at, block_of(owner)].astype(bf16)
            to_core(q, t).start()

    def chip_sum(q, t, owner, side):
        here = pl.ds(pl.multiple_of(2 * slab * q + side * slab, slab), slab)
        there = pl.ds(pl.multiple_of(side * slab, slab), slab)
        return acc[here, block_of(owner)] + from_core[q, t, there].astype(f32)

    def reduce_first(q):
        to_core(q, 0).wait_recv()
        both = chip_sum(q, 0, across, peer).astype(bf16)
        x_stage[q, 0] = both[:half]
        y_stage[q, 0] = both[half:]
        for t in range(2):
            first_copy(q, t).start()
        x_side = chip_sum(q, 0, across, shard)
        x_stage[q, 1] = x_side[:half].astype(bf16)
        second_copy(q, 0, 0).start()
        x_rest[q] = x_side[half:]
        to_core(q, 1).wait_recv()
        y_side = chip_sum(q, 1, grp, peer)
        y_stage[q, 1] = y_side[half:].astype(bf16)
        second_copy(q, 1, 0).start()
        y_rest[q] = y_side[:half]
        own_block[q] = chip_sum(q, 1, grp, shard)

    def reduce_second(q):
        first_copy(q, 1).wait_recv()
        x_stage[q, 2] = (x_rest[q] + y_first[q].astype(f32)).astype(bf16)
        second_copy(q, 0, 1).start()
        first_copy(q, 0).wait_recv()
        y_stage[q, 2] = (y_rest[q] + x_first[q].astype(f32)).astype(bf16)
        second_copy(q, 1, 1).start()

    def reduce_end(q):
        for t in range(2):
            for i in range(2):
                second_copy(q, t, i).wait_recv()
        own_block[q, :half] += x_second[q, 0].astype(f32) + y_second[q, 1].astype(f32)
        own_block[q, half:] += x_second[q, 1].astype(f32) + y_second[q, 0].astype(f32)
        out_ref[:, q * slab : (q + 1) * slab] = own_block[q].T

    for q in early:
        grads_here(far_end, [q], 2)
        products(far_end, [q], False)
        reduce_start(q)

    for q in early:
        reduce_first(q)

    @pl.when(inner)
    def _():
        g_far(far_middle, late[0], 0).wait_recv()
        grads_near(far_middle, late[:1], 1)
        g_far(far_end, late[0], 1).wait_recv()
        grads_near(far_end, late[:1], 2)
        grads_near(expert, late[1:], 0)

    reduce_second(early[0])

    @pl.when(inner)
    def _():
        g_far(far_middle, late[1], 0).wait_recv()
        grads_near(far_middle, late[1:], 1)

    reduce_second(early[1])

    @pl.when(inner)
    def _():
        g_far(far_end, late[1], 1).wait_recv()
        grads_near(far_end, late[1:], 2)

    for q in late:
        grads_here(first, [q], 0)
        products(first, [q], False)
        grads_here(far_middle, [q], 1)
        products(far_middle, [q], False)
        grads_here(far_end, [q], 2)
        products(far_end, [q], False)
        reduce_start(q)
        if q > late[0]:
            reduce_second(q - 1)
        reduce_first(q)
    for q in early:
        reduce_end(q)
    reduce_second(late[1])
    for q in late:
        reduce_end(q)

    @pl.when(shard == 0)
    def _():
        for kv in range(kv_heads):
            for i in range(2):
                kv_copy(i, kv).wait_send()

    for w in range(pieces_of):
        w_over_y(w, shard).wait_send()
        w_sibling(w, grp).wait_send()
        w_across(w, grp).wait_send()
        w_diagonal(w, across).wait_send()
    c_copy(expert, 0).wait_send()
    n_far(expert, 0).wait_send()
    for q in range(quarters):
        g_far(expert, q, 0).wait_send()
    for h in range(parts):
        x_far(expert, h, 0).wait_send()

    @pl.when(inner)
    def _():
        c_copy(end, 1).wait_send()
        n_far(end, 1).wait_send()
        for q in range(quarters):
            g_far(end, q, 1).wait_send()
        for h in range(parts):
            x_far(end, h, 1).wait_send()
        for slot, z in enumerate((expert, far_middle, far_end)):
            n_near(z, slot).wait_send()
            for q in range(quarters):
                g_near(z, q, slot).wait_send()
            for h in range(parts):
                x_near(z, h, slot).wait_send()

    for q in range(quarters):
        for t in range(2):
            to_core(q, t).wait_send()
            first_copy(q, t).wait_send()
            for i in range(2):
                second_copy(q, t, i).wait_send()


def fused(
    queries, keys, values, norm_gain, expert_ids, gate_values, hidden_grad, gate_weight, up_weight
):
    rows, model_width = queries.shape
    n_ep = lax.axis_size("ep")
    width = gate_weight.shape[2]
    kv_width = keys.shape[1]
    kv_heads = kv_width // HEAD_DIM
    block = model_width // 4
    parts = 4
    part_width = model_width // parts
    quarters = 4
    slab = width // quarters
    half = slab // 2
    cap = rows * expert_ids.shape[1] // n_ep * 3 // 2
    vmem = pl.BlockSpec(memory_space=pltpu.VMEM)
    hbm = pl.BlockSpec(memory_space=pltpu.HBM)
    dma = pltpu.SemaphoreType.DMA
    bf16, f32 = jnp.bfloat16, jnp.float32
    out = pl.pallas_call(
        whole_kernel,
        out_shape=jax.ShapeDtypeStruct((block, width), f32),
        in_specs=[hbm] * 3 + [vmem] * 3 + [hbm] * 3,
        out_specs=vmem,
        scratch_shapes=[
            pltpu.VMEM((rows, model_width), bf16),
            pltpu.VMEM((rows, kv_width), bf16),
            pltpu.VMEM((rows, kv_width), bf16),
            pltpu.VMEM((2, rows, kv_width), bf16),
            pltpu.VMEM((n_ep, 8, rows), f32),
            pltpu.VMEM((3, 8, rows), f32),
            pltpu.VMEM((n_ep, rows, 2 * slab), f32),
            pltpu.VMEM((n_ep, parts, rows, part_width), bf16),
            pltpu.VMEM((3, parts, cap, part_width), bf16),
            pltpu.VMEM((n_ep, quarters, rows, 2 * slab), bf16),
            pltpu.VMEM((3, quarters, cap, 2 * slab), bf16),
            pltpu.VMEM((n_ep, 8, rows), f32),
            pltpu.VMEM((3, cap, rows), bf16),
            pltpu.VMEM((2, model_width, width), bf16),
            pltpu.VMEM((2, model_width, width), bf16),
            pltpu.VMEM((n_ep, quarters, rows, 2 * slab), f32),
            pltpu.VMEM((2, quarters, rows, 2 * slab), f32),
            pltpu.VMEM((width, rows), bf16),
            pltpu.VMEM((2 * width, model_width), f32),
            pltpu.VMEM((quarters, 2, 2 * slab, block), bf16),
            pltpu.VMEM((quarters, 2, 2 * slab, block), bf16),
            pltpu.VMEM((quarters, 3, half, block), bf16),
            pltpu.VMEM((quarters, 3, half, block), bf16),
            pltpu.VMEM((quarters, slab, block), f32),
            pltpu.VMEM((quarters, half, block), f32),
            pltpu.VMEM((quarters, half, block), f32),
            pltpu.VMEM((n_ep, rows, 2 * slab), f32),
            pltpu.VMEM((quarters, half, block), bf16),
            pltpu.VMEM((quarters, half, block), bf16),
            pltpu.VMEM((quarters, 2, half, block), bf16),
            pltpu.VMEM((quarters, 2, half, block), bf16),
            dma((5 + 2 * quarters,)), dma((2, kv_heads)), dma((2, kv_heads)),
            dma((4,)), dma((4,)), dma((4,)), dma((4,)), dma((4,)), dma((4,)), dma((4,)), dma((4,)),
            dma((2,)), dma((n_ep,)), dma((2,)), dma((3,)), dma((n_ep,)), dma((2, quarters)), dma((3, quarters)), dma((n_ep, quarters)),
            dma((2, parts)), dma((3, parts)), dma((n_ep, parts)),
            dma((quarters, 2)), dma((quarters, 2)), dma((quarters, 2)), dma((quarters, 2)),
            dma((quarters, 2, 2)), dma((quarters, 2, 2)),
        ],
        compiler_params=pltpu.CompilerParams(
            collective_id=0, has_side_effects=True, vmem_limit_bytes=56 << 20
        ),
    )(
        queries, keys, values, norm_gain.reshape(1, -1), expert_ids.T, gate_values.T, hidden_grad,
        gate_weight[0], up_weight[0],
    )
    return out[None]


def solution(mesh):
    small = mesh.shape["grp"] == 4 and mesh.shape["sq"] == 2 and mesh.shape["ep"] == 4
    return jax.shard_map(
        fused if small else body,
        mesh=mesh,
        in_specs=(
            P(("grp", "ep", "sq"), None),
            P(("grp", "ep", "sq"), None),
            P(("grp", "ep", "sq"), None),
            P(),
            P(("grp", "ep", "sq"), None),
            P(("grp", "ep", "sq"), None),
            P(("grp", "ep", "sq"), None),
            P("ep", None, "sq"),
            P("ep", None, "sq"),
        ),
        out_specs=P("ep", "grp", "sq"),
        check_vma=False,
    )
```

```python
import functools
import math

import jax
import jax.numpy as jnp
from jax import lax
from jax.experimental import pallas as pl
from jax.experimental.pallas import tpu as pltpu
from jax.sharding import PartitionSpec as P

HEAD_DIM = 128

epsilon = 1e-05
masked_score = -1e30
LOG2E = 1.4426950408889634
MESH = pl.DeviceIdType.MESH


def attention_kernel(group_size, shard_ref, q_ref, ko_ref, vo_ref, kp_ref, vp_ref, gain_ref, out_ref, acc_ref):
    rows, model_width = q_ref.shape
    past = kp_ref.shape[0]
    scale = 1.0 / math.sqrt(HEAD_DIM)
    shard = shard_ref[0]
    contract = (((1,), (1,)), ((), ()))
    causal = lax.broadcasted_iota(jnp.int32, (rows, rows), 1) <= lax.broadcasted_iota(
        jnp.int32, (rows, rows), 0
    )
    seen = lax.broadcasted_iota(jnp.int32, (rows, past), 1) < shard * rows
    squares = jnp.zeros((rows, 1), jnp.float32)
    for head in range(model_width // HEAD_DIM):
        cols = slice(head * HEAD_DIM, (head + 1) * HEAD_DIM)
        kv = head // group_size
        kv_cols = slice(kv * HEAD_DIM, (kv + 1) * HEAD_DIM)
        q = q_ref[:, cols]
        own = lax.dot_general(q, ko_ref[:, kv_cols], contract, preferred_element_type=jnp.float32)
        old = lax.dot_general(q, kp_ref[:, kv_cols], contract, preferred_element_type=jnp.float32)
        own = jnp.where(causal, own * scale, masked_score)
        old = jnp.where(seen, old * scale, masked_score)
        top = jnp.maximum(
            jnp.max(own, axis=1, keepdims=True), jnp.max(old, axis=1, keepdims=True)
        )
        own = jnp.exp(own - top)
        old = jnp.exp(old - top)
        total = jnp.sum(own, axis=1, keepdims=True) + jnp.sum(old, axis=1, keepdims=True)
        out = jnp.dot(
            own.astype(jnp.bfloat16), vo_ref[:, kv_cols], preferred_element_type=jnp.float32
        ) + jnp.dot(
            old.astype(jnp.bfloat16), vp_ref[:, kv_cols], preferred_element_type=jnp.float32
        )
        out = out / total
        acc_ref[:, cols] = out
        squares = squares + jnp.sum(out * out, axis=1, keepdims=True)
    inverse = lax.rsqrt(squares / model_width + epsilon)
    out_ref[...] = (acc_ref[...] * inverse * gain_ref[...]).astype(jnp.bfloat16)


def attend(shard, queries, keys, values, past_keys, past_values, norm_gain):
    rows, model_width = queries.shape
    group_size = model_width // keys.shape[1]
    vmem = pl.BlockSpec(memory_space=pltpu.VMEM)
    return pl.pallas_call(
        functools.partial(attention_kernel, group_size),
        out_shape=jax.ShapeDtypeStruct((rows, model_width), jnp.bfloat16),
        in_specs=[pl.BlockSpec(memory_space=pltpu.SMEM)] + [vmem] * 6,
        out_specs=vmem,
        scratch_shapes=[pltpu.VMEM((rows, model_width), jnp.float32)],
        compiler_params=pltpu.CompilerParams(vmem_limit_bytes=32 << 20),
        cost_estimate=pl.CostEstimate(
            flops=4 * rows * model_width * (rows + past_keys.shape[0]),
            bytes_accessed=4 * rows * model_width,
            transcendentals=rows * (model_width // HEAD_DIM) * (rows + past_keys.shape[0]),
        ),
    )(shard.reshape(1), queries, keys, values, past_keys, past_values, norm_gain.reshape(1, -1))


def ring(size, shift):
    return [(i, (i + shift) % size) for i in range(size)]


def body(
    queries, keys, values, norm_gain, expert_ids, gate_values, hidden_grad, gate_weight, up_weight
):
    rows, model_width = queries.shape
    n_ep = lax.axis_size("ep")
    n_sq = lax.axis_size("sq")
    shard = lax.axis_index("sq")
    expert = lax.axis_index("ep")
    weight_gate = gate_weight[0]
    weight_up = up_weight[0]
    width = weight_gate.shape[1]
    kv_width = keys.shape[1]

    both = jnp.concatenate([keys, values], axis=1)
    past = []
    for j in range(1, n_sq):
        past.append(lax.ppermute(both, "sq", [(i, i + j) for i in range(n_sq - j)]))
    past = jnp.concatenate(past, axis=0)

    def columns_of(owner):
        return lax.dynamic_slice_in_dim(hidden_grad, owner * width, width, 1)

    grads = [columns_of(shard)]
    for j in range(1, n_sq):
        grads.append(lax.ppermute(columns_of((shard + j) % n_sq), "sq", ring(n_sq, j)))
    grad = jnp.concatenate(grads, axis=0)

    chosen = expert_ids[:, :, None] == jnp.arange(n_ep, dtype=jnp.int32)
    share = jnp.sum(jnp.where(chosen, gate_values[:, :, None], 0.0), axis=1).T
    shares = lax.all_gather(share, ("ep", "sq"), axis=0, tiled=False)
    shares = lax.dynamic_index_in_dim(shares, expert, 1, keepdims=False).reshape(n_ep, n_sq, rows)
    shares = jnp.concatenate(
        [
            lax.dynamic_index_in_dim(shares, (shard - j) % n_sq, 1, keepdims=False)
            for j in range(n_sq)
        ],
        axis=1,
    )

    normed = attend(
        shard, queries, keys, values, past[:, :kv_width], past[:, kv_width:], norm_gain
    )

    def add_chunk(step, tokens, grad, summed):
        source = (expert - step) % n_ep
        share_here = lax.dynamic_index_in_dim(shares, source, 0, keepdims=False)
        pieces = [tokens]
        for j in range(1, n_sq):
            pieces.append(lax.ppermute(tokens, "sq", ring(n_sq, j)))
        for j, inputs in enumerate(pieces):
            part = slice(j * rows, (j + 1) * rows)
            cotangent = (share_here[part, None] * grad[part].astype(jnp.float32)).astype(
                jnp.bfloat16
            )
            pre_gate = jnp.dot(inputs, weight_gate, preferred_element_type=jnp.float32)
            pre_up = jnp.dot(inputs, weight_up, preferred_element_type=jnp.float32)
            sigmoid_gate = jax.nn.sigmoid(pre_gate)
            slope = sigmoid_gate * (1.0 + pre_gate * (1.0 - sigmoid_gate))
            delta = (cotangent.astype(jnp.float32) * pre_up * slope).astype(jnp.bfloat16)
            term = lax.dot_general(
                inputs, delta, (((0,), (0,)), ((), ())), preferred_element_type=jnp.float32
            )
            summed = term if summed is None else summed + term
        return summed

    def turn(tokens, grad):
        return lax.ppermute(tokens, "ep", ring(n_ep, 1)), lax.ppermute(grad, "ep", ring(n_ep, 1))

    if n_ep <= 8:
        summed = None
        tokens = normed
        for step in range(n_ep):
            if step < n_ep - 1:
                turned = turn(tokens, grad)
            summed = add_chunk(step, tokens, grad, summed)
            if step < n_ep - 1:
                tokens, grad = turned
    else:

        def one_step(step, carried):
            tokens, grad, summed = carried
            turned = turn(tokens, grad)
            return (*turned, add_chunk(step, tokens, grad, summed))

        start = jnp.zeros((model_width, width), jnp.float32)
        summed = lax.fori_loop(0, n_ep, one_step, (normed, grad, start))[2]
    return lax.psum_scatter(
        summed[None].astype(jnp.bfloat16), "grp", scatter_dimension=1, tiled=True
    ).astype(jnp.float32)


def whole_kernel(
    q_hbm, k_hbm, v_hbm, gain_ref, ids_ref, values_ref, hidden_hbm, gate_hbm, up_hbm, out_ref,
    q_ref, k_ref, v_ref, kv_buf, n_buf, n_out, inverse_ref, x_full, x_out, g_full, g_out, c_buf, choice_ref,
    w_gate, w_up, h_ref, pre_ref, delta_ref, acc, stage, from_core, x_stage, y_stage, own_block,
    x_rest, y_rest, share_ref,
    x_first, y_first, x_second, y_second,
    load_sem, kv_send, kv_recv, wy_send, wy_recv, ws_send, ws_recv, wa_send, wa_recv,
    wd_send, wd_recv, c_send, c_recv, nf_send, nn_send, n_recv, gf_send, gn_send, g_recv, xf_send, xn_send, x_recv,
    core_send, core_recv, first_send, first_recv, second_send, second_recv,
):
    n_ep = x_full.shape[0]
    rows, model_width = q_ref.shape
    cap = x_out.shape[2]
    parts = x_full.shape[1]
    part_width = model_width // parts
    width = gate_hbm.shape[1]
    quarters = g_full.shape[1]
    slab = width // quarters
    half = slab // 2
    kv_heads = k_ref.shape[1] // HEAD_DIM
    group_size = model_width // k_ref.shape[1]
    block = model_width // 4
    bf16, f32 = jnp.bfloat16, jnp.float32
    grp, expert, shard = lax.axis_index("grp"), lax.axis_index("ep"), lax.axis_index("sq")
    peer = 1 - shard
    core = lax.rem(grp, 2)
    chip = grp // 2
    sibling = chip * 2 + 1 - core
    across = (1 - chip) * 2 + core
    diagonal = (1 - chip) * 2 + 1 - core
    last = n_ep - 1
    right, left = lax.rem(expert + 1, n_ep), lax.rem(expert + last, n_ep)
    upper_side = expert // 2
    inner = jnp.logical_and(expert > 0, expert < last)
    outer = jnp.logical_not(inner)
    end = 3 * upper_side
    middle = 1 + upper_side
    far_middle = 2 - upper_side
    far_end = 3 - 3 * upper_side
    far = {"ep": jnp.where(inner, far_middle, middle)}
    near = {"ep": end}
    first = jnp.where(inner, end, middle)

    def load(i, src, dst):
        return pltpu.make_async_copy(src, dst, load_sem.at[i])

    loads = [
        load(0, q_hbm, q_ref),
        load(1, k_hbm, k_ref),
        load(2, v_hbm, v_ref),
        load(3, gate_hbm, w_gate.at[shard]),
        load(4, up_hbm, w_up.at[shard]),
    ]
    grad_loads = [
        load(
            5 + 2 * q + h,
            hidden_hbm.at[:, h * width + q * slab : h * width + (q + 1) * slab],
            g_full.at[expert, q, :, h * slab : (h + 1) * slab],
        )
        for q in range(quarters)
        for h in range(2)
    ]
    for copy in grad_loads + loads:
        copy.start()

    c_buf[...] = jnp.ones_like(c_buf)
    n_out[...] = jnp.zeros_like(n_out)
    names = lax.broadcasted_iota(jnp.int32, c_buf.shape[1:], 0)
    c_buf[expert] = sum(
        jnp.where(names == ids_ref[k : k + 1], values_ref[k : k + 1], 0.0)
        for k in range(ids_ref.shape[0])
    )

    @pl.when(outer)
    def _():
        for z in range(n_ep):

            @pl.when(z != expert)
            def _():
                for p in range(parts):
                    x_full[z, p, cap:rows] = jnp.zeros((rows - cap, part_width), bf16)
                for q in range(quarters):
                    g_full[z, q, cap:rows] = jnp.zeros((rows - cap, 2 * slab), bf16)

    @pl.when(shard == 0)
    def _():
        kv_buf[...] = jnp.zeros_like(kv_buf)

    barrier = pltpu.get_barrier_semaphore()
    for target in ({"sq": peer}, {"ep": right}, {"ep": left}, {"grp": sibling}, {"grp": across}):
        pl.semaphore_signal(barrier, inc=1, device_id=target, device_id_type=MESH)
    pl.semaphore_wait(barrier, 5)

    def send(src, dst, send_sem, recv_sem, target):
        return pltpu.make_async_remote_copy(
            src_ref=src, dst_ref=dst, send_sem=send_sem, recv_sem=recv_sem,
            device_id=target, device_id_type=MESH,
        )

    def kv_copy(i, kv):
        cols = slice(kv * HEAD_DIM, (kv + 1) * HEAD_DIM)
        return send((k_hbm, v_hbm)[i].at[:, cols], kv_buf.at[i, :, cols],
                    kv_send.at[i, kv], kv_recv.at[i, kv], {"sq": peer})

    weights = (w_gate, w_up)

    pieces_of = 2 * 2
    piece = block // 2

    def rows_of(w, owner):
        return pl.ds(pl.multiple_of(owner * block + w // 2 * piece, piece), piece)

    def w_over_y(w, half_of):
        mine = rows_of(w, grp)
        return send((gate_hbm, up_hbm)[w % 2].at[mine], weights[w % 2].at[half_of, mine],
                    wy_send.at[w], wy_recv.at[w], {"sq": peer})

    def w_on(w, owner, target, send_sem, recv_sem):
        there = weights[w % 2].at[peer, rows_of(w, owner)]
        return send(there, there, send_sem.at[w], recv_sem.at[w], {"grp": target})

    def w_sibling(w, owner):
        return w_on(w, owner, sibling, ws_send, ws_recv)

    def w_across(w, owner):
        return w_on(w, owner, across, wa_send, wa_recv)

    def w_diagonal(w, owner):
        return w_on(w, owner, sibling, wd_send, wd_recv)

    def c_copy(z, slot):
        return send(c_buf.at[z], c_buf.at[z], c_send.at[slot], c_recv.at[z], far)

    def n_far(z, slot):
        return send(n_buf.at[z], n_buf.at[z], nf_send.at[slot], n_recv.at[z], far)

    def n_near(z, slot):
        return send(n_out.at[slot], n_buf.at[z], nn_send.at[slot], n_recv.at[z], near)

    def g_far(z, q, slot):
        return send(g_full.at[z, q], g_full.at[z, q], gf_send.at[slot, q], g_recv.at[z, q], far)

    def g_near(z, q, slot):
        return send(g_out.at[slot, q], g_full.at[z, q, 0:cap], gn_send.at[slot, q],
                    g_recv.at[z, q], near)

    def x_far(z, p, slot):
        return send(x_full.at[z, p], x_full.at[z, p], xf_send.at[slot, p], x_recv.at[z, p], far)

    def x_near(z, p, slot):
        return send(x_out.at[slot, p], x_full.at[z, p, 0:cap], xn_send.at[slot, p],
                    x_recv.at[z, p], near)

    @pl.when(shard == 0)
    def _():
        for kv in range(kv_heads):
            for i in range(2):
                kv_copy(i, kv).start()

    for w in range(pieces_of):
        w_over_y(w, shard).start()

    diag = lax.broadcasted_iota(jnp.int32, (rows, rows), 0) == lax.broadcasted_iota(
        jnp.int32, (rows, rows), 1
    )

    def share_row(z, who):
        share = c_buf[z]
        here = lax.broadcasted_iota(jnp.int32, share.shape, 0) == who
        return jnp.sum(jnp.where(here, share, 0.0), axis=0, keepdims=True)

    def choose(z, slot):
        upper = (
            lax.broadcasted_iota(jnp.int32, (rows, rows), 0)
            <= lax.broadcasted_iota(jnp.int32, (rows, rows), 1)
        ).astype(f32).astype(bf16)
        places = lax.broadcasted_iota(jnp.int32, (cap, rows), 0).astype(f32)
        share = share_row(z, end)
        routed = jnp.where(share > 0.0, 1.0, 0.0)
        count = jnp.dot(
            jnp.broadcast_to(routed, (16, rows)).astype(bf16), upper, preferred_element_type=f32
        )[:1]
        key = jnp.where(share > 0.0, count - 1.0, -1.0)
        choice_ref[slot] = jnp.where(places == key, 1.0, 0.0).astype(bf16)

    def grads_near(z, which, slot):
        choice = choice_ref[slot]
        share = jnp.sum(choice.astype(f32) * share_row(z, end), axis=1, keepdims=True)
        for q in which:
            grad = jnp.dot(choice, g_full[z, q], preferred_element_type=f32)
            g_out[slot, q] = (share * grad).astype(bf16)
            g_near(z, q, slot).start()

    def tokens_near(z, p, slot):
        x_out[slot, p] = jnp.dot(
            choice_ref[slot], x_full[z, p], preferred_element_type=f32
        ).astype(bf16)
        x_near(z, p, slot).start()

    def inverse_near(z, slot):
        column = jnp.sum(jnp.where(diag, n_buf[z, 0:1], 0.0), axis=1, keepdims=True)
        chosen = choice_ref[slot].astype(f32).T
        row = jnp.sum(chosen * column, axis=0, keepdims=True)
        n_out[slot, :, 0:cap] = jnp.broadcast_to(row, (8, cap))
        n_near(z, slot).start()

    early, late = range(quarters // 2), range(quarters // 2, quarters)
    c_copy(expert, 0).start()
    for copy in grad_loads:
        copy.wait()
    for q in early:
        g_far(expert, q, 0).start()

    @pl.when(inner)
    def _():
        choose(expert, 0)
        grads_near(expert, early, 0)

    for copy in loads[:3]:
        copy.wait()

    def early_grads():
        @pl.when(inner)
        def _():
            c_copy(end, 1).wait_recv()
            c_copy(end, 1).start()
            for q in early:
                g_far(end, q, 1).wait_recv()
                g_far(end, q, 1).start()
            c_copy(far_middle, 0).wait_recv()
            for q in early:
                g_far(far_middle, q, 0).wait_recv()
            choose(far_middle, 1)
            grads_near(far_middle, early, 1)

    contract = (((1,), (1,)), ((), ()))
    part_rows = rows // 2
    factor = LOG2E / math.sqrt(HEAD_DIM)
    hide = jnp.where(shard == 0, masked_score, 0.0)
    causal = lax.broadcasted_iota(jnp.int32, (part_rows, part_rows), 1) <= (
        lax.broadcasted_iota(jnp.int32, (part_rows, part_rows), 0)
    )
    squares = [jnp.zeros((part_rows, 1), f32)] * 2
    for kv in range(kv_heads):
        kv_cols = slice(kv * HEAD_DIM, (kv + 1) * HEAD_DIM)

        @pl.when(shard == 1)
        def _():
            for i in range(2):
                kv_copy(i, kv).wait_recv()

        if kv == 2:
            early_grads()
        for head in range(kv * group_size, (kv + 1) * group_size):
            cols = slice(head * HEAD_DIM, (head + 1) * HEAD_DIM)
            for p in range(2):
                part = slice(p * part_rows, (p + 1) * part_rows)
                q = q_ref[part, cols]

                def scored(keys):
                    return lax.dot_general(q, keys, contract, preferred_element_type=f32)

                near_scores = jnp.where(causal, scored(k_ref[part, kv_cols]), masked_score)
                pieces = [(near_scores, v_ref[part, kv_cols], 0.0)]
                if p:
                    pieces.append(
                        (scored(k_ref[:part_rows, kv_cols]), v_ref[:part_rows, kv_cols], 0.0)
                    )
                pieces.append((scored(kv_buf[0, :, kv_cols]), kv_buf[1, :, kv_cols], hide))
                top = functools.reduce(
                    jnp.maximum,
                    [jnp.max(s, axis=1, keepdims=True) * factor + away for s, _, away in pieces],
                )
                terms = [jnp.exp2(s * factor - (top - away)) for s, _, away in pieces]
                total = functools.reduce(
                    jnp.add, [jnp.sum(e, axis=1, keepdims=True) for e in terms]
                )
                out = functools.reduce(
                    jnp.add,
                    [
                        jnp.dot(e.astype(bf16), v, preferred_element_type=f32)
                        for e, (_, v, _) in zip(terms, pieces)
                    ],
                )
                out = out * (1.0 / total)
                inside = slice(cols.start - kv * part_width, cols.stop - kv * part_width)
                x_full[expert, kv, part, inside] = (out * gain_ref[:, cols]).astype(bf16)
                squares[p] = squares[p] + jnp.sum(out * out, axis=1, keepdims=True)
        x_far(expert, kv, 0).start()

        @pl.when(inner)
        def _():
            tokens_near(expert, kv, 0)

    inverse = jnp.concatenate(
        [lax.rsqrt(s / model_width + epsilon) for s in squares], axis=0
    )
    inverse = jnp.sum(jnp.where(diag, inverse, 0.0), axis=0, keepdims=True)
    n_buf[expert] = jnp.broadcast_to(inverse, (8, rows))
    n_far(expert, 0).start()

    @pl.when(inner)
    def _():
        inverse_near(expert, 0)

    @pl.when(outer)
    def _():
        for q in late:
            g_far(expert, q, 0).start()

    for i in range(2):
        loads[3 + i].wait()

    def weights_from_y(w):
        w_over_y(w, peer).wait_recv()
        w_across(w, grp).start()
        w_sibling(w, grp).start()

    def weights_from_x(w):
        w_across(w, across).wait_recv()
        w_diagonal(w, across).start()

    def first_tokens(h):
        @pl.when(inner)
        def _():
            x_far(end, h, 1).wait_recv()
            x_far(end, h, 1).start()
            x_far(far_middle, h, 0).wait_recv()
            tokens_near(far_middle, h, 1)
            if h == parts - 1:
                n_far(end, 1).wait_recv()
                n_far(end, 1).start()
                n_far(far_middle, 0).wait_recv()
                inverse_near(far_middle, 1)

    def second_tokens(h):
        @pl.when(inner)
        def _():
            if h == 0:
                c_copy(far_end, 1).wait_recv()
                choose(far_end, 2)
            if h == parts - 1:
                for q in early:
                    g_far(far_end, q, 1).wait_recv()
                grads_near(far_end, early, 2)
            x_far(far_end, h, 1).wait_recv()
            tokens_near(far_end, h, 2)
            if h == parts - 1:
                n_far(far_end, 1).wait_recv()
                inverse_near(far_end, 2)
                grads_near(expert, late, 0)

    def tile_of(weight, side, ab, h):
        cols = pl.ds(pl.multiple_of(ab * 2 * slab, 2 * slab), 2 * slab)
        return weight[side, h * part_width : (h + 1) * part_width, cols]

    def keep_factor(z, side, ab, pre_gate, pre_up):
        scale = inverse_ref[z]
        pre_gate = pre_gate * scale
        sigmoid_gate = 0.5 * jnp.tanh(0.5 * pre_gate) + 0.5
        value = pre_up * scale * scale * (sigmoid_gate * (1.0 + pre_gate * (1.0 - sigmoid_gate)))
        cols = pl.ds(pl.multiple_of(side * slab, slab), slab)
        for i in range(2):
            h_ref[z, 2 * ab + i, :, cols] = value[:, i * slab : (i + 1) * slab]

    def forward_side(z, side):
        @pl.loop(0, quarters // 2)
        def _(ab):
            def product(weight):
                return sum(
                    jnp.dot(x_full[z, h], tile_of(weight, side, ab, h), preferred_element_type=f32)
                    for h in range(parts)
                )

            keep_factor(z, side, ab, product(w_gate), product(w_up))

    def forward(z):
        @pl.loop(0, 2)
        def _(side):
            forward_side(z, side)

    def forward_part(z, h):
        @pl.loop(0, 4)
        def _(t):
            side, ab = t // 2, lax.rem(t, 2)
            sums = [
                jnp.dot(x_full[z, h], tile_of(weight, side, ab, h), preferred_element_type=f32)
                for weight in weights
            ]
            if h:
                sums = [pre_ref[i, t] + sums[i] for i in range(2)]
            if h < parts - 1:
                for i in range(2):
                    pre_ref[i, t] = sums[i]
            else:
                keep_factor(z, side, ab, *sums)

    def share_column(z):
        share = jnp.sum(jnp.where(diag, share_row(z, expert), 0.0), axis=1, keepdims=True)
        share_ref[z] = jnp.broadcast_to(share, (rows, 2 * slab))

    def inverse_column(z):
        column = jnp.sum(jnp.where(diag, n_buf[z, 0:1], 0.0), axis=1, keepdims=True)
        inverse_ref[z] = jnp.broadcast_to(column, (rows, 2 * slab))

    def products(z, which, fresh):
        high = 2 * slab * len(which)
        at = slice(2 * slab * which[0], 2 * slab * which[0] + high)
        for i, q in enumerate(which):
            cotangent = (share_ref[z] * g_full[z, q].astype(f32)).astype(bf16).astype(f32)
            delta_ref[2 * slab * i : 2 * slab * (i + 1)] = (cotangent * h_ref[z, q]).T.astype(bf16)
        for h in range(parts):
            cols = slice(h * part_width, (h + 1) * part_width)
            term = jnp.dot(delta_ref[:high], x_full[z, h], preferred_element_type=f32)
            if fresh:
                acc[at, cols] = term
            else:
                acc[at, cols] += term

    def grads_here(z, which, slot):
        @pl.when(outer)
        def _():
            for q in which:
                g_near(z, q, slot).wait_recv()

    def tokens_here(z, slot, which):
        @pl.when(outer)
        def _():
            for h in which:
                x_near(z, h, slot).wait_recv()
                if h == parts - 1:
                    n_near(z, slot).wait_recv()

    share_column(expert)
    inverse_column(expert)
    forward_side(expert, shard)
    weights_from_y(0)
    first_tokens(0)
    weights_from_y(1)
    weights_from_x(0)
    first_tokens(1)
    weights_from_y(2)
    weights_from_x(1)
    first_tokens(2)
    weights_from_y(3)
    weights_from_x(2)
    first_tokens(3)

    @pl.when(inner)
    def _():
        for q in late:
            g_far(expert, q, 0).start()
            g_far(end, q, 1).wait_recv()
            g_far(end, q, 1).start()

    weights_from_x(3)
    for w in range(pieces_of):
        w_sibling(w, sibling).wait_recv()
        w_diagonal(w, diagonal).wait_recv()

    second_tokens(0)
    forward_side(expert, peer)
    products(expert, early, True)
    second_tokens(1)
    products(expert, late, True)
    tokens_here(first, 0, range(parts))
    share_column(first)
    inverse_column(first)
    forward(first)
    second_tokens(2)
    grads_here(first, early, 0)
    products(first, early, False)
    tokens_here(far_middle, 1, range(parts))
    share_column(far_middle)
    inverse_column(far_middle)
    forward(far_middle)
    second_tokens(3)
    grads_here(far_middle, early, 1)
    products(far_middle, early, False)

    share_column(far_end)
    for h in range(parts):
        tokens_here(far_end, 2, [h])
        if h == parts - 1:
            inverse_column(far_end)
        forward_part(far_end, h)

    def block_of(c):
        return pl.ds(pl.multiple_of(c * block, block), block)

    def to_core(q, t):
        return send(stage.at[q, t], from_core.at[q, t], core_send.at[q, t],
                    core_recv.at[q, t], {"grp": sibling})

    def first_copy(q, t):
        src, dst, target = (
            (x_stage, x_first, {"grp": across}),
            (y_stage, y_first, {"sq": peer}),
        )[t]
        return send(src.at[q, 0], dst.at[q], first_send.at[q, t], first_recv.at[q, t], target)

    def second_copy(q, t, i):
        src, dst, target = (
            (x_stage, x_second, {"grp": across}),
            (y_stage, y_second, {"sq": peer}),
        )[t]
        return send(src.at[q, 1 + i], dst.at[q, i], second_send.at[q, t, i],
                    second_recv.at[q, t, i], target)

    def reduce_start(q):
        at = slice(2 * slab * q, 2 * slab * (q + 1))
        for t, owner in enumerate((diagonal, sibling)):
            stage[q, t] = acc[at, block_of(owner)].astype(bf16)
            to_core(q, t).start()

    def chip_sum(q, t, owner, side):
        here = pl.ds(pl.multiple_of(2 * slab * q + side * slab, slab), slab)
        there = pl.ds(pl.multiple_of(side * slab, slab), slab)
        return acc[here, block_of(owner)] + from_core[q, t, there].astype(f32)

    def reduce_first(q):
        to_core(q, 0).wait_recv()
        both = chip_sum(q, 0, across, peer).astype(bf16)
        x_stage[q, 0] = both[:half]
        y_stage[q, 0] = both[half:]
        for t in range(2):
            first_copy(q, t).start()
        x_side = chip_sum(q, 0, across, shard)
        x_stage[q, 1] = x_side[:half].astype(bf16)
        second_copy(q, 0, 0).start()
        x_rest[q] = x_side[half:]
        to_core(q, 1).wait_recv()
        y_side = chip_sum(q, 1, grp, peer)
        y_stage[q, 1] = y_side[half:].astype(bf16)
        second_copy(q, 1, 0).start()
        y_rest[q] = y_side[:half]
        own_block[q] = chip_sum(q, 1, grp, shard)

    def reduce_second(q):
        first_copy(q, 1).wait_recv()
        x_stage[q, 2] = (x_rest[q] + y_first[q].astype(f32)).astype(bf16)
        second_copy(q, 0, 1).start()
        first_copy(q, 0).wait_recv()
        y_stage[q, 2] = (y_rest[q] + x_first[q].astype(f32)).astype(bf16)
        second_copy(q, 1, 1).start()

    def reduce_end(q):
        for t in range(2):
            for i in range(2):
                second_copy(q, t, i).wait_recv()
        own_block[q, :half] += x_second[q, 0].astype(f32) + y_second[q, 1].astype(f32)
        own_block[q, half:] += x_second[q, 1].astype(f32) + y_second[q, 0].astype(f32)
        out_ref[:, q * slab : (q + 1) * slab] = own_block[q].T

    for q in early:
        grads_here(far_end, [q], 2)
        products(far_end, [q], False)
        reduce_start(q)

    for q in early:
        reduce_first(q)

    @pl.when(inner)
    def _():
        g_far(far_middle, late[0], 0).wait_recv()
        grads_near(far_middle, late[:1], 1)
        g_far(far_end, late[0], 1).wait_recv()
        grads_near(far_end, late[:1], 2)

    reduce_second(early[0])

    @pl.when(inner)
    def _():
        g_far(far_middle, late[1], 0).wait_recv()
        grads_near(far_middle, late[1:], 1)

    reduce_second(early[1])

    @pl.when(inner)
    def _():
        g_far(far_end, late[1], 1).wait_recv()
        grads_near(far_end, late[1:], 2)

    for q in late:
        grads_here(first, [q], 0)
        products(first, [q], False)
        grads_here(far_middle, [q], 1)
        products(far_middle, [q], False)
        grads_here(far_end, [q], 2)
        products(far_end, [q], False)
        reduce_start(q)
        if q > late[0]:
            reduce_second(q - 1)
        reduce_first(q)
    for q in early:
        reduce_end(q)
    reduce_second(late[1])
    for q in late:
        reduce_end(q)

    @pl.when(shard == 0)
    def _():
        for kv in range(kv_heads):
            for i in range(2):
                kv_copy(i, kv).wait_send()

    for w in range(pieces_of):
        w_over_y(w, shard).wait_send()
        w_sibling(w, grp).wait_send()
        w_across(w, grp).wait_send()
        w_diagonal(w, across).wait_send()
    c_copy(expert, 0).wait_send()
    n_far(expert, 0).wait_send()
    for q in range(quarters):
        g_far(expert, q, 0).wait_send()
    for h in range(parts):
        x_far(expert, h, 0).wait_send()

    @pl.when(inner)
    def _():
        c_copy(end, 1).wait_send()
        n_far(end, 1).wait_send()
        for q in range(quarters):
            g_far(end, q, 1).wait_send()
        for h in range(parts):
            x_far(end, h, 1).wait_send()
        for slot, z in enumerate((expert, far_middle, far_end)):
            n_near(z, slot).wait_send()
            for q in range(quarters):
                g_near(z, q, slot).wait_send()
            for h in range(parts):
                x_near(z, h, slot).wait_send()

    for q in range(quarters):
        for t in range(2):
            to_core(q, t).wait_send()
            first_copy(q, t).wait_send()
            for i in range(2):
                second_copy(q, t, i).wait_send()


def fused(
    queries, keys, values, norm_gain, expert_ids, gate_values, hidden_grad, gate_weight, up_weight
):
    rows, model_width = queries.shape
    n_ep = lax.axis_size("ep")
    width = gate_weight.shape[2]
    kv_width = keys.shape[1]
    kv_heads = kv_width // HEAD_DIM
    block = model_width // 4
    parts = 4
    part_width = model_width // parts
    quarters = 4
    slab = width // quarters
    half = slab // 2
    cap = rows * expert_ids.shape[1] // n_ep * 3 // 2
    vmem = pl.BlockSpec(memory_space=pltpu.VMEM)
    hbm = pl.BlockSpec(memory_space=pltpu.HBM)
    dma = pltpu.SemaphoreType.DMA
    bf16, f32 = jnp.bfloat16, jnp.float32
    out = pl.pallas_call(
        whole_kernel,
        out_shape=jax.ShapeDtypeStruct((block, width), f32),
        in_specs=[hbm] * 3 + [vmem] * 3 + [hbm] * 3,
        out_specs=vmem,
        scratch_shapes=[
            pltpu.VMEM((rows, model_width), bf16),
            pltpu.VMEM((rows, kv_width), bf16),
            pltpu.VMEM((rows, kv_width), bf16),
            pltpu.VMEM((2, rows, kv_width), bf16),
            pltpu.VMEM((n_ep, 8, rows), f32),
            pltpu.VMEM((3, 8, rows), f32),
            pltpu.VMEM((n_ep, rows, 2 * slab), f32),
            pltpu.VMEM((n_ep, parts, rows, part_width), bf16),
            pltpu.VMEM((3, parts, cap, part_width), bf16),
            pltpu.VMEM((n_ep, quarters, rows, 2 * slab), bf16),
            pltpu.VMEM((3, quarters, cap, 2 * slab), bf16),
            pltpu.VMEM((n_ep, 8, rows), f32),
            pltpu.VMEM((3, cap, rows), bf16),
            pltpu.VMEM((2, model_width, width), bf16),
            pltpu.VMEM((2, model_width, width), bf16),
            pltpu.VMEM((n_ep, quarters, rows, 2 * slab), f32),
            pltpu.VMEM((2, quarters, rows, 2 * slab), f32),
            pltpu.VMEM((width, rows), bf16),
            pltpu.VMEM((2 * width, model_width), f32),
            pltpu.VMEM((quarters, 2, 2 * slab, block), bf16),
            pltpu.VMEM((quarters, 2, 2 * slab, block), bf16),
            pltpu.VMEM((quarters, 3, half, block), bf16),
            pltpu.VMEM((quarters, 3, half, block), bf16),
            pltpu.VMEM((quarters, slab, block), f32),
            pltpu.VMEM((quarters, half, block), f32),
            pltpu.VMEM((quarters, half, block), f32),
            pltpu.VMEM((n_ep, rows, 2 * slab), f32),
            pltpu.VMEM((quarters, half, block), bf16),
            pltpu.VMEM((quarters, half, block), bf16),
            pltpu.VMEM((quarters, 2, half, block), bf16),
            pltpu.VMEM((quarters, 2, half, block), bf16),
            dma((5 + 2 * quarters,)), dma((2, kv_heads)), dma((2, kv_heads)),
            dma((4,)), dma((4,)), dma((4,)), dma((4,)), dma((4,)), dma((4,)), dma((4,)), dma((4,)),
            dma((2,)), dma((n_ep,)), dma((2,)), dma((3,)), dma((n_ep,)), dma((2, quarters)), dma((3, quarters)), dma((n_ep, quarters)),
            dma((2, parts)), dma((3, parts)), dma((n_ep, parts)),
            dma((quarters, 2)), dma((quarters, 2)), dma((quarters, 2)), dma((quarters, 2)),
            dma((quarters, 2, 2)), dma((quarters, 2, 2)),
        ],
        compiler_params=pltpu.CompilerParams(
            collective_id=0, has_side_effects=True, vmem_limit_bytes=56 << 20
        ),
    )(
        queries, keys, values, norm_gain.reshape(1, -1), expert_ids.T, gate_values.T, hidden_grad,
        gate_weight[0], up_weight[0],
    )
    return out[None]


def solution(mesh):
    small = mesh.shape["grp"] == 4 and mesh.shape["sq"] == 2 and mesh.shape["ep"] == 4
    return jax.shard_map(
        fused if small else body,
        mesh=mesh,
        in_specs=(
            P(("grp", "ep", "sq"), None),
            P(("grp", "ep", "sq"), None),
            P(("grp", "ep", "sq"), None),
            P(),
            P(("grp", "ep", "sq"), None),
            P(("grp", "ep", "sq"), None),
            P(("grp", "ep", "sq"), None),
            P("ep", None, "sq"),
            P("ep", None, "sq"),
        ),
        out_specs=P("ep", "grp", "sq"),
        check_vma=False,
    )
```
